128 devices in a mesh: gx: 4 (over x), gy: 4 (over y), gz: 8 (over z, core).
Axes of the slice: x: 4, y: 4, z: 4, core: 2. Of those that a mesh axis runs over, the one named last changes fastest.
Arguments:
- scalar_field: float32 [64, 384, 2048], P('gx', 'gy', 'gz'), may hold values from -6 to 6
- velocity: bfloat16 [3, 64, 384, 2048], P(None, 'gx', 'gy', 'gz'), may hold values from -12 to 12
Outputs:
- updated: float32 [64, 384, 2048], P('gx', 'gy', 'gz')
The draws below stay inside these ranges and needn't reach their ends.
All inputs are finite; a program needn't handle non-finite values.
Results may differ from the reference program's by a relative error of at most 0.0003.
Values sent between devices are 32-bit elements; how exact they have to be, the bound alone decides.
No kernel may reach another device: no remote copies, remote signals or barrier semaphores. Data moves between devices by JAX's collectives and lax.ppermute only.
A program may use at most 128 MiB of HBM per device.

```python
import jax
import jax.numpy as jnp
from jax import lax

NX = 64
NY = 384
NZ = 2048


def block_levels(key, extent, pieces, least, high):
    loudness = 1.0
    for dim, parts in pieces:
        steps = jax.random.uniform(jax.random.fold_in(jax.random.fold_in(key, 6), dim), (parts,), jnp.float32, least / len(pieces), high / len(pieces))
        loudness = loudness * jnp.repeat(jnp.exp(steps), extent[dim] // parts).reshape((-1,) + (1,) * (len(extent) - 1 - dim))
    return loudness


def normal_values(key, extent, deviation, most, pieces=(), kind=jnp.bfloat16):
    entries = deviation * jax.random.normal(key, extent, jnp.float32)
    if pieces:
        entries = entries * block_levels(key, extent, pieces, -0.22, 0.18)
    return jnp.clip(entries, -most, most).astype(kind)


def setup_inputs(seed: int = 0) -> dict:
    arg_keys = jax.random.split(jax.random.key(seed), 3)
    return {
        "scalar_field": normal_values(arg_keys[0], (NX, NY, NZ), 1.0, 6.0, ((0, 4), (1, 4), (2, 8)), jnp.float32),
        "velocity": normal_values(arg_keys[1], (3, NX, NY, NZ), 3.0, 12.0, ((1, 4), (2, 4), (3, 8))),
    }


DT = 0.002
NU_BASE = 0.3
SGS_COEF = 0.01
FILTER_STRENGTH = 0.3
GLL_POINTS = [-1.0, -0.8717401485096066, -0.5917001814331423, -0.2092992179024789, 0.2092992179024789, 0.5917001814331423, 0.8717401485096066, 1.0]

def legendre_all(point):
    values_list = [1.0, point]
    for order in range(1, 7):
        values_list.append(((2 * order + 1) * point * values_list[order] - order * values_list[order - 1]) / (order + 1))
    return values_list

def gll_tables():
    degree = 7
    table = [legendre_all(p) for p in GLL_POINTS]
    top = [table[i][degree] for i in range(8)]
    weights = [2.0 / (degree * (degree + 1) * top[i] * top[i]) for i in range(8)]
    derivative = [[0.0] * 8 for i in range(8)]
    for i in range(8):
        for j in range(8):
            if i != j:
                derivative[i][j] = top[i] / (top[j] * (GLL_POINTS[i] - GLL_POINTS[j]))
    derivative[0][0] = -degree * (degree + 1) / 4.0
    derivative[7][7] = degree * (degree + 1) / 4.0
    damping = [1.0] * 8
    for k in (6, 7):
        damping[k] = 1.0 - FILTER_STRENGTH * ((k - 5) / 2.0) ** 2
    gammas = [2.0 / (2 * k + 1) for k in range(7)] + [2.0 / degree]
    filter_mat = [[0.0] * 8 for i in range(8)]
    for i in range(8):
        for j in range(8):
            total = 0.0
            for k in range(8):
                total += table[i][k] * damping[k] * weights[j] * table[j][k] / gammas[k]
            filter_mat[i][j] = total
    return (derivative, weights, filter_mat)

def apply_matrix(matrix, blocked_field, which, transpose):
    if transpose:
        pattern = ['ia,xiybzc->xaybzc', 'ib,xayizc->xaybzc', 'ic,xaybzi->xaybzc'][which]
    else:
        pattern = ['ia,xaybzc->xiybzc', 'ib,xaybzc->xayizc', 'ic,xaybzc->xaybzi'][which]
    return jnp.einsum(pattern, matrix, blocked_field, precision=lax.Precision.HIGHEST)

def position_mask(length, which, ndim):
    target = [1] * ndim
    target[which] = length
    return (jnp.arange(length) % 8).reshape(target)

def pair_sum(values_arr, which):
    length = values_arr.shape[which]
    position = position_mask(length, which, values_arr.ndim)
    before = jnp.roll(values_arr, 1, axis=which)
    after = jnp.roll(values_arr, -1, axis=which)
    return values_arr + jnp.where(position == 0, before, 0.0) + jnp.where(position == 7, after, 0.0)

def summation(values_arr):
    return pair_sum(pair_sum(pair_sum(values_arr, 0), 1), 2)

def edge_factor(length):
    position = jnp.arange(length) % 8
    return 1.0 + ((position == 0) | (position == 7)).astype(jnp.float32)

def count_sharers(size_x, size_y, size_z):
    return edge_factor(size_x)[:, None, None] * edge_factor(size_y)[None, :, None] * edge_factor(size_z)[None, None, :]

def node_mass(weights, size_x, size_y, size_z):
    along_x = jnp.tile(weights, size_x // 8)
    along_y = jnp.tile(weights, size_y // 8)
    along_z = jnp.tile(weights, size_z // 8)
    return along_x[:, None, None] * along_y[None, :, None] * along_z[None, None, :]

def reference(scalar_field, velocity):
    derivative_list, weights_list, filter_list = gll_tables()
    derivative = jnp.asarray(derivative_list, jnp.float32)
    weights = jnp.asarray(weights_list, jnp.float32)
    filter_mat = jnp.asarray(filter_list, jnp.float32)
    size_x, size_y, size_z = scalar_field.shape
    blocked = (size_x // 8, 8, size_y // 8, 8, size_z // 8, 8)
    element_view = scalar_field.reshape(blocked)
    sharers = count_sharers(size_x, size_y, size_z)
    mass_diag = node_mass(weights, size_x, size_y, size_z)
    smooth = []
    for d in range(3):
        gradient = apply_matrix(derivative, element_view, d, False).reshape(scalar_field.shape)
        smooth.append(summation(gradient) / sharers)
    magnitude = smooth[0] * smooth[0] + smooth[1] * smooth[1] + smooth[2] * smooth[2]
    viscosity = NU_BASE + SGS_COEF * jnp.sqrt(1.0 + magnitude)
    residue = jnp.zeros(blocked, jnp.float32)
    for d in range(3):
        flux_term = mass_diag * (viscosity * smooth[d] - velocity[d].astype(jnp.float32) * scalar_field)
        residue = residue - apply_matrix(derivative, flux_term.reshape(blocked), d, True)
    summed = summation(residue.reshape(scalar_field.shape))
    advanced = scalar_field + DT * summed / (sharers * mass_diag)
    filtered = advanced.reshape(blocked)
    for d in range(3):
        filtered = apply_matrix(filter_mat, filtered, d, False)
    return summation(filtered.reshape(scalar_field.shape)) / sharers
```

```python
import functools

import jax
import jax.numpy as jnp
import numpy as np
from jax import lax
from jax.experimental import pallas as pl
from jax.experimental.pallas import tpu as pltpu
from jax.sharding import PartitionSpec as P

DT = 0.002
NU_BASE = 0.3
SGS_COEF = 0.01
FILTER_STRENGTH = 0.3
GLL_POINTS = [
    -1.0,
    -0.8717401485096066,
    -0.5917001814331423,
    -0.2092992179024789,
    0.2092992179024789,
    0.5917001814331423,
    0.8717401485096066,
    1.0,
]
BF = jnp.bfloat16
F32 = jnp.float32
VM = pl.BlockSpec(memory_space=pltpu.VMEM)


def legendre_all(point):
    values_list = [1.0, point]
    for order in range(1, 7):
        values_list.append(
            ((2 * order + 1) * point * values_list[order] - order * values_list[order - 1])
            / (order + 1)
        )
    return values_list


def gll_tables():
    degree = 7
    table = [legendre_all(p) for p in GLL_POINTS]
    top = [table[i][degree] for i in range(8)]
    weights = [2.0 / (degree * (degree + 1) * top[i] * top[i]) for i in range(8)]
    derivative = [[0.0] * 8 for i in range(8)]
    for i in range(8):
        for j in range(8):
            if i != j:
                derivative[i][j] = top[i] / (top[j] * (GLL_POINTS[i] - GLL_POINTS[j]))
    derivative[0][0] = -degree * (degree + 1) / 4.0
    derivative[7][7] = degree * (degree + 1) / 4.0
    damping = [1.0] * 8
    for k in (6, 7):
        damping[k] = 1.0 - FILTER_STRENGTH * ((k - 5) / 2.0) ** 2
    gammas = [2.0 / (2 * k + 1) for k in range(7)] + [2.0 / degree]
    filter_mat = [[0.0] * 8 for i in range(8)]
    for i in range(8):
        for j in range(8):
            total = 0.0
            for k in range(8):
                total += table[i][k] * damping[k] * weights[j] * table[j][k] / gammas[k]
            filter_mat[i][j] = total
    return np.array(derivative), np.array(weights), np.array(filter_mat)


D, WT, FM = gll_tables()
DR = -DT * (D.T * WT[None, :]) / WT[:, None]


def block(mat, length):
    return np.kron(np.eye(length // 8), mat)


def average(length):
    mat = np.eye(length)
    for k in range(8, length, 8):
        mat[k - 1 : k + 1, k - 1 : k + 1] = 0.5
    mat[0, 0] = mat[-1, -1] = 0.5
    return mat


class Line:
    def __init__(self, length):
        avg = average(length)
        filt = block(FM, length)
        self.avg = avg
        self.grad = avg @ block(D, length)
        self.res = block(DR, length)
        self.filt = avg @ filt
        self.both = avg @ filt @ avg
        self.both[0, 0] += 0.25 * FM[7, 7]
        self.both[-1, -1] += 0.25 * FM[0, 0]
        self.face = filt @ avg
        first, last = np.eye(length)[0], np.eye(length)[-1]
        self.halo = np.stack([self.filt[:, 0] * 0.5, 0.5 * first, self.filt[:, -1] * 0.5, 0.5 * last])


def parts(mat):
    mat = np.asarray(mat, np.float64)
    high = mat.astype(jnp.bfloat16)
    low = (mat - high.astype(np.float64)).astype(jnp.bfloat16)
    return high, low


def split(val):
    high = val.astype(BF)
    return high, (val - high.astype(F32)).astype(BF)


def mm(a, b):
    return jnp.dot(a, b, preferred_element_type=F32)


def right(pair, mat):
    return mm(pair[0], mat[0]) + (mm(pair[1], mat[0]) + mm(pair[0], mat[1]))


def right_exact(pair, mat):
    return mm(pair[0], mat) + mm(pair[1], mat)


def left(mat, pair):
    return mm(mat[0], pair[0]) + (mm(mat[0], pair[1]) + mm(mat[1], pair[0]))


def left_exact(mat, pair):
    return mm(mat, pair[0]) + mm(mat, pair[1])


def call(kernel, outs, *args, scratch=(), flops=0, nbytes=0, name=None):
    single = not isinstance(outs, list)
    shapes = [jax.ShapeDtypeStruct(o, F32) for o in ([outs] if single else outs)]
    res = pl.pallas_call(
        kernel,
        out_shape=shapes,
        in_specs=[VM] * len(args),
        out_specs=[VM] * len(shapes),
        scratch_shapes=list(scratch),
        compiler_params=pltpu.CompilerParams(vmem_limit_bytes=20 << 20),
        cost_estimate=pl.CostEstimate(flops=flops, bytes_accessed=nbytes, transcendentals=0),
        name=name,
    )(*args)
    return res[0] if single else res


NXL, NYL, NZL = 16, 96, 256
ROWS = NXL * NYL
TILES = NYL // 8


def face_x_kernel(u_ref, lo_ref, hi_ref):
    def body(t, carry):
        rows = pl.ds(pl.multiple_of(t * 8, 8), 8)
        nodes = [u_ref[k, rows, :] for k in range(NXL)]
        lo_ref[0, rows, :] = 0.5 * nodes[0]
        lo_ref[1, rows, :] = sum(float(0.5 * D[0, j]) * nodes[j] for j in range(8))
        hi_ref[0, rows, :] = 0.5 * nodes[15]
        hi_ref[1, rows, :] = sum(float(0.5 * D[7, j]) * nodes[8 + j] for j in range(8))
        return carry

    lax.fori_loop(0, TILES, body, 0)


def even_odd(mat, nodes, sign):
    even = [nodes[j] + nodes[7 - j] for j in range(4)]
    odd = [nodes[j] - nodes[7 - j] for j in range(4)]
    out = [None] * 8
    for i in range(4):
        a = sum(float(0.5 * (mat[i, j] + mat[i, 7 - j])) * even[j] for j in range(4))
        b = sum(float(0.5 * (mat[i, j] - mat[i, 7 - j])) * odd[j] for j in range(4))
        out[i] = a + b
        out[7 - i] = (a - b) if sign > 0 else (b - a)
    return out


def average_x(vals):
    vals = list(vals)
    mid = 0.5 * (vals[7] + vals[8])
    vals[7] = vals[8] = mid
    vals[0] = 0.5 * vals[0]
    vals[15] = 0.5 * vals[15]
    return vals


def lane_iota(rows):
    return lax.broadcasted_iota(jnp.int32, (rows, 128), 1)


def pack_columns(fields, x, lane, offset=0):
    total = None
    for q, field in enumerate(fields):
        both = jnp.where(lane == 127, field[:, 0:128], field[:, 128:256])
        swap = jnp.where(lane == 127, field[:, 128:256], field[:, 0:128])
        del both
        pos = 2 * (16 * (q + offset) + x)
        rolled = pltpu.roll(swap, (pos - 127) % 128, 1)
        keep = (lane == pos) | (lane == (pos + 1) % 128)
        piece = jnp.where(keep, rolled, 0.0)
        total = piece if total is None else total + piece
    return total


def local_z_kernel(u_ref, sz_ref, dh_ref, dl_ref, fh_ref, fl_ref, z1, z2, z3, z4, cols, ph, plo, qh, qlo):
    def xstage(t, carry):
        rows = pl.ds(pl.multiple_of(t * 16, 16), 16)
        for h in range(2):
            ls = pl.ds(h * 128, 128)
            nodes = [u_ref[k, rows, ls] for k in range(NXL)]
            grads = even_odd(D, nodes[:8], -1) + even_odd(D, nodes[8:], -1)
            for k, (p, g) in enumerate(zip(average_x(nodes), average_x(grads))):
                a, b = split(p)
                ph[k, rows, ls] = a
                plo[k, rows, ls] = b
                a, b = split(g)
                qh[k, rows, ls] = a
                qlo[k, rows, ls] = b
        return carry

    lax.fori_loop(0, NYL // 16, xstage, 0)
    chunk = 4

    def zstage(c, carry):
        xs = pl.ds(c * chunk, chunk)
        flat = lambda ref: ref[xs].reshape(chunk * NYL, NZL)
        back = lambda val: val.reshape(chunk, NYL, NZL)
        p = (flat(ph), flat(plo))
        sz = sz_ref[...]
        z1[xs] = back(right_exact(p, sz))
        z2[xs] = back(right(p, (dh_ref[...], dl_ref[...])))
        z3[xs] = back(right_exact((flat(qh), flat(qlo)), sz))
        z4[xs] = back(right(split(flat(u_ref)), (fh_ref[...], fl_ref[...])))
        return carry

    lax.fori_loop(0, NXL // chunk, zstage, 0)
    lane = lane_iota(NYL)
    acc = jnp.zeros((NYL, 128), F32)
    for x in range(NXL):
        acc = acc + pack_columns([r[x] for r in (z1, z2, z3, z4)], x, lane)
    cols[...] = acc


def face_z_kernel(lo_ref, hi_ref, cols_ref, sz_ref, dh_ref, dl_ref, dz, cols):
    hu = jnp.concatenate([lo_ref[0], hi_ref[0]], axis=0)
    hq = jnp.concatenate([lo_ref[1], hi_ref[1]], axis=0)
    sz = sz_ref[...]
    p = split(hu)
    a = right_exact(p, sz)
    b = right(p, (dh_ref[...], dl_ref[...]))
    c = right_exact(split(hq), sz)
    lane = lane_iota(NYL)
    acc = cols_ref[...]
    for s, x in ((0, 0), (1, NXL - 1)):
        vals = [v[s * NYL : (s + 1) * NYL] for v in (a, b, c)]
        for q in range(3):
            dz[s, q] = vals[q]
        acc = acc + pack_columns(vals, x, lane)
    cols[...] = acc


def local_y_kernel(z1, z2, z3, dz, sy_ref, dh_ref, dl_ref, sx_, sy_, sz_, rows_lo, rows_hi):
    for s, x in ((0, 0), (1, NXL - 1)):
        for q, ref in enumerate((z1, z2, z3)):
            pass
    avg = sy_ref[...]
    grad = (dh_ref[...], dl_ref[...])

    def one(x, v1, v2, v3):
        sy_[x] = left(grad, split(v1))
        sz_[x] = left_exact(avg, split(v2))
        sx_[x] = left_exact(avg, split(v3))

    one(0, z1[0] + dz[0, 0], z2[0] + dz[0, 1], z3[0] + dz[0, 2])
    one(NXL - 1, z1[NXL - 1] + dz[1, 0], z2[NXL - 1] + dz[1, 1], z3[NXL - 1] + dz[1, 2])

    def body(x, carry):
        one(x, z1[x], z2[x], z3[x])
        return carry

    lax.fori_loop(1, NXL - 1, body, 0)
    for q, ref in enumerate((sy_, sz_, sx_)):
        for x in range(NXL):
            rows_lo[q, x : x + 1, :] = ref[x, 0:1, :]
            rows_hi[q, x : x + 1, :] = ref[x, NYL - 1 : NYL, :]


def halo_columns(from_lo, from_hi):
    lane = lane_iota(NYL)
    even = (lane % 2) == 0
    shifted = pltpu.roll(from_hi, 126, 1)
    return jnp.where(even, from_lo, shifted)


def face_y_kernel(lo_ref, hi_ref, rlo_ref, rhi_ref, sy_ref, dh_ref, dl_ref, inj_ref, cols, out_lo, out_hi):
    halo = halo_columns(lo_ref[...], hi_ref[...])
    pair = split(halo)
    grad = left((dh_ref[...], dl_ref[...]), pair)
    avg = left_exact(sy_ref[...], pair)
    lane = lane_iota(NYL)
    which = ((lane + 1) % 128) // 32
    mixed = jnp.where(which == 0, grad, jnp.where(which == 3, halo, avg))
    cols[...] = mixed
    lane48 = lax.broadcasted_iota(jnp.int32, (48, 128), 1)
    row48 = lax.broadcasted_iota(jnp.int32, (48, 128), 0)
    diag = (((lane48 + 1) % 128) // 2) == row48
    inj = inj_ref[...]
    for row, src, dst in ((0, rlo_ref, out_lo), (NYL - 1, rhi_ref, out_hi)):
        vec = jnp.broadcast_to(mixed[row : row + 1, :], (48, 128))
        add = right_exact(split(jnp.where(diag, vec, 0.0)), inj)
        dst[...] = src[...] + add.reshape(3, NXL, NZL)


def inject(field, cols, q, x, lane):
    pos = 2 * (16 * q + x)
    rolled = pltpu.roll(cols, (-pos) % 128, 1)
    return (
        field[:, 0:128] + jnp.where(lane == 0, rolled, 0.0),
        field[:, 128:256] + jnp.where(lane == 127, rolled, 0.0),
    )


def columns_kernel(sx_, sy_, sz_, z4, cols_ref, fh_ref, fl_ref, ox, oy, oz, ou):
    lane = lane_iota(NYL)
    filt = (fh_ref[...], fl_ref[...])
    for x in range(NXL):
        cols = cols_ref[...]
        for q, (src, dst) in enumerate(((sy_, oy), (sz_, oz), (sx_, ox))):
            a, b = inject(src[x], cols, q, x, lane)
            dst[x, :, 0:128] = a
            dst[x, :, 128:256] = b
        a, b = inject(z4[x], cols, 3, x, lane)
        ou[x, :, 0:128] = left(filt, split(a))
        ou[x, :, 128:256] = left(filt, split(b))


def product_kernel(u_ref, v_ref, h_ref):
    def body(x, carry):
        for d in range(3):
            h_ref[d, x] = v_ref[d, x].astype(F32) * u_ref[x]
        return carry

    lax.fori_loop(0, NXL, body, 0)


def row_sum(vals, coefs):
    row = lax.broadcasted_iota(jnp.int32, vals.shape, 0)
    weight = jnp.zeros(vals.shape, F32)
    for k, c in enumerate(coefs):
        weight = jnp.where(row == k, float(c), weight)
    return jnp.sum(vals * weight, axis=0, keepdims=True)


def residue_kernel(
    sx_, sy_, sz_, h_ref, lo_ref, hi_ref, vu_ref, yh_ref, yl_ref, zh_ref, zl_ref,
    r_ref, out_lo, out_hi, fx, fyh, fyl, fzh, fzl, lo_s, hi_s,
):
    lo_s[...] = lo_ref[...]
    hi_s[...] = hi_ref[...]
    row16 = lax.broadcasted_iota(jnp.int32, (16, NZL), 0)

    def flux(x, carry):
        for t in range(NYL // 16):
            rows = slice(t * 16, t * 16 + 16)
            s = [sy_[x, rows, :], sz_[x, rows, :], sx_[x, rows, :]]
            if t == 0:
                s = [jnp.where(row16 == 0, v + lo_s[q, pl.ds(x, 1), :], v) for q, v in enumerate(s)]
            if t == NYL // 16 - 1:
                s = [jnp.where(row16 == 15, v + hi_s[q, pl.ds(x, 1), :], v) for q, v in enumerate(s)]
            mag = 1.0 + s[0] * s[0] + s[1] * s[1] + s[2] * s[2]
            nu = NU_BASE + SGS_COEF * jnp.sqrt(mag)
            fx[x, rows, :] = nu * s[2] - h_ref[0, x, rows, :]
            a, b = split(nu * s[0] - h_ref[1, x, rows, :])
            fyh[x, rows, :] = a
            fyl[x, rows, :] = b
            a, b = split(nu * s[1] - h_ref[2, x, rows, :])
            fzh[x, rows, :] = a
            fzl[x, rows, :] = b
        return carry

    lax.fori_loop(0, NXL, flux, 0)

    def along_y(x, carry):
        r_ref[x] = left((yh_ref[...], yl_ref[...]), (fyh[x], fyl[x]))
        return carry

    lax.fori_loop(0, NXL, along_y, 0)
    chunk = 4

    def along_z(c, carry):
        xs = pl.ds(c * chunk, chunk)
        flat = lambda ref: ref[xs].reshape(chunk * NYL, NZL)
        val = right((flat(fzh), flat(fzl)), (zh_ref[...], zl_ref[...]))
        r_ref[xs] = r_ref[xs] + val.reshape(chunk, NYL, NZL)
        return carry

    lax.fori_loop(0, NXL // chunk, along_z, 0)

    def along_x(t, carry):
        rows = pl.ds(pl.multiple_of(t * 8, 8), 8)
        for e in range(2):
            nodes = [fx[8 * e + k, rows, :] for k in range(8)]
            for k, val in enumerate(even_odd(DR, nodes, -1)):
                r_ref[8 * e + k, rows, :] = r_ref[8 * e + k, rows, :] + val
        return carry

    lax.fori_loop(0, TILES, along_x, 0)
    face = LY.face
    for x in range(NXL):
        one = slice(x, x + 1)
        out_lo[0, one, :] = r_ref[x, 0:1, :]
        out_hi[0, one, :] = r_ref[x, NYL - 1 : NYL, :]
        out_lo[1, one, :] = row_sum(r_ref[x, 0:16, :], face[0, 0:16])
        out_hi[1, one, :] = row_sum(r_ref[x, NYL - 16 : NYL, :], face[-1, NYL - 16 :])
        out_lo[2, one, :] = vu_ref[x, 0:1, :]
        out_hi[2, one, :] = vu_ref[x, NYL - 1 : NYL, :]


def filter_y_kernel(r_ref, th_ref, tl_ref, ph_ref, pl_ref, out, cols):
    op = (th_ref[...], tl_ref[...])
    lane = lane_iota(NYL)
    acc = jnp.zeros((NYL, 128), F32)
    for x in range(NXL):
        val = left(op, split(r_ref[x]))
        out[x] = val
        pay = right(split(val), (ph_ref[...], pl_ref[...]))
        acc = acc + place(pay, x, lane)
    cols[...] = acc


def place(pay, x, lane):
    keep = ((lane % 32) // 2) == x
    return jnp.where(keep, pltpu.roll(pay, 2 * x, 1) if x else pay, 0.0)


def face_z2_kernel(cols_ref, lo_ref, hi_ref, ph_ref, pl_ref, ay_ref, cols):
    lane16 = lax.broadcasted_iota(jnp.int32, (NXL, 128), 1)
    row16 = lax.broadcasted_iota(jnp.int32, (NXL, 128), 0)
    keep = ((lane16 % 32) // 2) == row16
    acc = cols_ref[...]
    mat = (ph_ref[...], pl_ref[...])
    for k, (ref, q) in enumerate(((lo_ref, 0), (lo_ref, 1), (hi_ref, 0), (hi_ref, 1))):
        pay = right(split(ref[q]), mat)
        spread = pay
        rolled = jnp.zeros((NXL, 128), F32)
        for x in range(NXL):
            moved = pltpu.roll(spread, 2 * x, 1) if x else spread
            rolled = jnp.where(row16 == x, moved, rolled)
        vec = jnp.sum(jnp.where(keep, rolled, 0.0), axis=0, keepdims=True)
        acc = acc + ay_ref[:, k : k + 1] * vec
    cols[...] = acc


def filter_z_kernel(r1, vu, lo_ref, hi_ref, ay_ref, th_ref, tl_ref, out, vout, vals):
    row = lax.broadcasted_iota(jnp.int32, (8, NZL), 0)

    def add(x, carry):
        one = pl.ds(x, 1)
        vals[x] = r1[x]
        vout[x] = vu[x]
        low = [lo_ref[q, one, :] for q in range(3)]
        high = [hi_ref[q, one, :] for q in range(3)]
        vals[x, 0:16, :] = vals[x, 0:16, :] + (ay_ref[0:16, 0:1] * low[0] + ay_ref[0:16, 1:2] * low[1])
        tail = slice(NYL - 16, NYL)
        vals[x, tail, :] = vals[x, tail, :] + (ay_ref[tail, 2:3] * high[0] + ay_ref[tail, 3:4] * high[1])
        vout[x, 0:8, :] = vout[x, 0:8, :] + jnp.where(row == 0, low[2], 0.0)
        vout[x, NYL - 8 : NYL, :] = vout[x, NYL - 8 : NYL, :] + jnp.where(row == 7, high[2], 0.0)
        return carry

    lax.fori_loop(0, NXL, add, 0)
    chunk = 4

    def zstage(c, carry):
        xs = pl.ds(c * chunk, chunk)
        val = vals[xs].reshape(chunk * NYL, NZL)
        out[xs] = right(split(val), (th_ref[...], tl_ref[...])).reshape(chunk, NYL, NZL)
        return carry

    lax.fori_loop(0, NXL // chunk, zstage, 0)


def add_z_kernel(r2, vu, lo_ref, hi_ref, ah_ref, al_ref, out, pay_lo, pay_hi, hs):
    even = (lane_iota(NYL) % 2) == 0
    halo = jnp.where(even, lo_ref[...], hi_ref[...])
    hs[...] = halo
    for x in range(NXL):
        rolled = pltpu.roll(hs[...], (-2 * x) % 128, 1) if x else hs[...]
        out[x] = r2[x] + right(split(rolled), (ah_ref[...], al_ref[...]))

    def faces(t, carry):
        rows = pl.ds(pl.multiple_of(t * 8, 8), 8)
        r = [out[k, rows, :] for k in range(NXL)]
        vu_ = [vu[k, rows, :] for k in range(NXL)]
        a = [s + v for s, v in zip(average_x(r), vu_)]
        pay_lo[0, rows, :] = r[0]
        pay_hi[0, rows, :] = r[15]
        pay_lo[1, rows, :] = sum(float(FM[0, j]) * a[j] for j in range(8))
        pay_hi[1, rows, :] = sum(float(FM[7, j]) * a[8 + j] for j in range(8))
        return carry

    lax.fori_loop(0, TILES, faces, 0)


def final_kernel(r2, vu, lo_ref, hi_ref, out):
    def body(t, carry):
        rows = pl.ds(pl.multiple_of(t * 8, 8), 8)
        r = [r2[k, rows, :] for k in range(NXL)]
        a = [s + vu[k, rows, :] for k, s in enumerate(average_x(r))]
        a[0] = a[0] + 0.5 * lo_ref[0, rows, :]
        a[15] = a[15] + 0.5 * hi_ref[0, rows, :]
        f = even_odd(FM, a[:8], 1) + even_odd(FM, a[8:], 1)
        f = average_x(f)
        f[0] = f[0] + 0.5 * (lo_ref[1, rows, :] + float(0.5 * FM[7, 7]) * r[0])
        f[15] = f[15] + 0.5 * (hi_ref[1, rows, :] + float(0.5 * FM[0, 0]) * r[15])
        for k in range(NXL):
            out[k, rows, :] = f[k]
        return carry

    lax.fori_loop(0, TILES, body, 0)


LY = Line(NYL)
LZ = Line(NZL)


def shift(val, axis, step):
    count = lax.axis_size(axis)
    return lax.ppermute(val, axis, [(i, (i + step) % count) for i in range(count)])


def exchange(lo, hi, axis):
    return shift(hi, axis, 1), shift(lo, axis, -1)


def const(mat):
    return [jnp.asarray(p) for p in parts(mat)]


def on_device(u, velocity):
    full = (NXL, NYL, NZL)
    scr = lambda dt: pltpu.VMEM(full, dt)
    face_x = (2, NYL, NZL)
    face_y = (3, NXL, NZL)
    colshape = (NYL, 128)

    sz = jnp.asarray(LZ.avg.T.astype(jnp.bfloat16))
    sy = jnp.asarray(LY.avg.astype(jnp.bfloat16))
    dz = const(LZ.grad.T)
    fz = const(LZ.filt.T)
    dy = const(LY.grad)
    fy = const(LY.filt)
    inj = np.zeros((128, NZL))
    inj[0::2, 0] = 1.0
    inj[1::2, NZL - 1] = 1.0
    inj = jnp.asarray(inj.astype(jnp.bfloat16))

    lo, hi = call(face_x_kernel, [face_x, face_x], u, flops=10**7, nbytes=2 * 10**6, name="face_x")
    xlo, xhi = exchange(lo, hi, "gx")
    z1, z2, z3, z4, cols = call(
        local_z_kernel, [full] * 4 + [colshape], u, sz, *dz, *fz,
        scratch=[scr(BF)] * 4, flops=2 * 10**9, nbytes=8 * 10**6, name="local_z",
    )
    h = call(product_kernel, (3,) + full, u, velocity, flops=10**6, nbytes=8 * 10**6, name="product")
    dlt, cols = call(face_z_kernel, [(2, 3, NYL, NZL), colshape], xlo, xhi, cols, sz, *dz, name="face_z")
    clo, chi = shift(cols, "gz", 1), shift(cols, "gz", -1)
    sx_, sy_, sz_, rlo, rhi = call(
        local_y_kernel, [full] * 3 + [face_y] * 2, z1, z2, z3, dlt, sy, *dy,
        flops=10**9, nbytes=9 * 10**6, name="local_y",
    )
    hcols, rlo, rhi = call(
        face_y_kernel, [colshape, face_y, face_y], clo, chi, rlo, rhi, sy, *dy, inj, name="face_y"
    )
    ylo, yhi = exchange(rlo, rhi, "gy")
    sx_, sy_, sz_, vu = call(
        columns_kernel, [full] * 4, sx_, sy_, sz_, z4, hcols, *fy,
        flops=10**9, nbytes=9 * 10**6, name="columns",
    )
    r, rlo, rhi = call(
        residue_kernel, [full, face_y, face_y],
        sx_, sy_, sz_, h, ylo, yhi, vu, *const(LY.res), *const(LZ.res.T),
        scratch=[scr(F32)] + [scr(BF)] * 4 + [pltpu.VMEM(face_y, F32)] * 2,
        flops=2 * 10**9, nbytes=12 * 10**6, name="residue",
    )
    ylo, yhi = exchange(rlo, rhi, "gy")
    pay = np.zeros((NZL, 128))
    pay[NZL - 1, 0] = 1.0
    pay[0, 1] = 1.0
    pay[:, 32] = LZ.face[-1]
    pay[:, 33] = LZ.face[0]
    pay = const(pay)
    halo_y = jnp.asarray(LY.halo.T.astype(np.float32))
    r1, cols = call(
        filter_y_kernel, [full, colshape], r, *const(LY.both), *pay,
        flops=10**9, nbytes=4 * 10**6, name="filter_y",
    )
    cols = call(face_z2_kernel, colshape, cols, ylo, yhi, *pay, halo_y, name="face_z2")
    clo, chi = shift(cols, "gz", 1), shift(cols, "gz", -1)
    r2, vu = call(
        filter_z_kernel, [full, full], r1, vu, ylo, yhi, halo_y, *const(LZ.both.T),
        scratch=[scr(F32)], flops=10**9, nbytes=6 * 10**6, name="filter_z",
    )
    add = np.zeros((128, NZL))
    add[0], add[32], add[1], add[33] = LZ.halo[0], LZ.halo[1], LZ.halo[2], LZ.halo[3]
    r3, lo, hi = call(
        add_z_kernel, [full, face_x, face_x], r2, vu, clo, chi, *const(add),
        scratch=[pltpu.VMEM(colshape, F32)], name="add_z",
    )
    xlo, xhi = exchange(lo, hi, "gx")
    return call(final_kernel, full, r3, vu, xlo, xhi, name="final")


def solution(mesh):
    return jax.shard_map(
        on_device,
        mesh=mesh,
        in_specs=(P("gx", "gy", "gz"), P(None, "gx", "gy", "gz")),
        out_specs=P("gx", "gy", "gz"),
        check_vma=False,
    )
```

```python
import functools

import jax
import jax.numpy as jnp
import numpy as np
from jax import lax
from jax.experimental import pallas as pl
from jax.experimental.pallas import tpu as pltpu
from jax.sharding import PartitionSpec as P

DT = 0.002
NU_BASE = 0.3
SGS_COEF = 0.01
FILTER_STRENGTH = 0.3
GLL_POINTS = [
    -1.0,
    -0.8717401485096066,
    -0.5917001814331423,
    -0.2092992179024789,
    0.2092992179024789,
    0.5917001814331423,
    0.8717401485096066,
    1.0,
]
BF = jnp.bfloat16
F32 = jnp.float32
VM = pl.BlockSpec(memory_space=pltpu.VMEM)


def legendre_all(point):
    values_list = [1.0, point]
    for order in range(1, 7):
        values_list.append(
            ((2 * order + 1) * point * values_list[order] - order * values_list[order - 1])
            / (order + 1)
        )
    return values_list


def gll_tables():
    degree = 7
    table = [legendre_all(p) for p in GLL_POINTS]
    top = [table[i][degree] for i in range(8)]
    weights = [2.0 / (degree * (degree + 1) * top[i] * top[i]) for i in range(8)]
    derivative = [[0.0] * 8 for i in range(8)]
    for i in range(8):
        for j in range(8):
            if i != j:
                derivative[i][j] = top[i] / (top[j] * (GLL_POINTS[i] - GLL_POINTS[j]))
    derivative[0][0] = -degree * (degree + 1) / 4.0
    derivative[7][7] = degree * (degree + 1) / 4.0
    damping = [1.0] * 8
    for k in (6, 7):
        damping[k] = 1.0 - FILTER_STRENGTH * ((k - 5) / 2.0) ** 2
    gammas = [2.0 / (2 * k + 1) for k in range(7)] + [2.0 / degree]
    filter_mat = [[0.0] * 8 for i in range(8)]
    for i in range(8):
        for j in range(8):
            total = 0.0
            for k in range(8):
                total += table[i][k] * damping[k] * weights[j] * table[j][k] / gammas[k]
            filter_mat[i][j] = total
    return np.array(derivative), np.array(weights), np.array(filter_mat)


D, WT, FM = gll_tables()
DR = -DT * (D.T * WT[None, :]) / WT[:, None]


def block(mat, length):
    return np.kron(np.eye(length // 8), mat)


def average(length):
    mat = np.eye(length)
    for k in range(8, length, 8):
        mat[k - 1 : k + 1, k - 1 : k + 1] = 0.5
    mat[0, 0] = mat[-1, -1] = 0.5
    return mat


class Line:
    def __init__(self, length):
        avg = average(length)
        filt = block(FM, length)
        self.avg = avg
        self.grad = avg @ block(D, length)
        self.res = block(DR, length)
        self.filt = avg @ filt
        self.both = avg @ filt @ avg
        self.both[0, 0] += 0.25 * FM[7, 7]
        self.both[-1, -1] += 0.25 * FM[0, 0]
        self.face = filt @ avg
        first, last = np.eye(length)[0], np.eye(length)[-1]
        self.halo = np.stack([self.filt[:, 0] * 0.5, 0.5 * first, self.filt[:, -1] * 0.5, 0.5 * last])


def halves(mat):
    mat = np.asarray(mat, np.float64)
    high = mat.astype(jnp.bfloat16)
    low = (mat - high.astype(np.float64)).astype(jnp.bfloat16)
    return high, low


def on_right(mat):
    high, low = halves(mat)
    return jnp.asarray(np.concatenate([high, high, low], axis=0))


def on_left(mat):
    high, low = halves(mat)
    return jnp.asarray(np.concatenate([high, high, low], axis=1))


def exact_right(mat):
    mat = np.asarray(mat).astype(jnp.bfloat16)
    return jnp.asarray(np.concatenate([mat, mat], axis=0))


def exact_left(mat):
    mat = np.asarray(mat).astype(jnp.bfloat16)
    return jnp.asarray(np.concatenate([mat, mat], axis=1))


def split(val):
    high = val.astype(BF)
    return high, (val - high.astype(F32)).astype(BF)


def mm(a, b):
    return jnp.dot(a, b, preferred_element_type=F32)


def right(pair, mat):
    return mm(jnp.concatenate([pair[0], pair[1], pair[0]], axis=1), mat)


def right_exact(pair, mat):
    return mm(jnp.concatenate(pair, axis=1), mat)


def left(mat, pair):
    return mm(mat, jnp.concatenate([pair[0], pair[1], pair[0]], axis=0))


def left_exact(mat, pair):
    return mm(mat, jnp.concatenate(pair, axis=0))


def call(kernel, outs, *args, scratch=(), flops=0, nbytes=0, name=None, hbm=(), hbm_out=False, smem=()):
    single = not isinstance(outs, list)
    shapes = [jax.ShapeDtypeStruct(o, F32) for o in ([outs] if single else outs)]
    kinds = {i: pl.BlockSpec(memory_space=pl.ANY) for i in hbm}
    kinds.update({i: pl.BlockSpec(memory_space=pltpu.SMEM) for i in smem})
    res = pl.pallas_call(
        kernel,
        out_shape=shapes,
        in_specs=[kinds.get(i, VM) for i in range(len(args))],
        out_specs=[pl.BlockSpec(memory_space=pl.ANY) if hbm_out else VM] * len(shapes),
        scratch_shapes=list(scratch),
        compiler_params=pltpu.CompilerParams(vmem_limit_bytes=20 << 20),
        cost_estimate=pl.CostEstimate(flops=flops, bytes_accessed=nbytes, transcendentals=0),
        name=name,
    )(*args)
    return res[0] if single else res


NXL, NYL, NZL = 16, 96, 256
ROWS = NXL * NYL
TILES = NYL // 8


LX, LY, LZ = Line(NXL), Line(NYL), Line(NZL)


def face_x_kernel(u_hbm, u_ref, lo_ref, hi_ref, sems):
    copies = []
    for c in range(4):
        rows = slice(c * 24, c * 24 + 24)
        for s in range(2):
            xs = slice(8 * s, 8 * s + 8)
            copies.append(
                pltpu.make_async_copy(u_hbm.at[xs, rows, :], u_ref.at[xs, rows, :], sems.at[2 * c + s])
            )
    for copy in copies:
        copy.start()
    for c in range(4):
        copies[2 * c].wait()
        copies[2 * c + 1].wait()
        for t in range(3):
            rows = slice(c * 24 + t * 8, c * 24 + t * 8 + 8)
            nodes = [u_ref[k, rows, :] for k in range(NXL)]
            lo_ref[0, rows, :] = 0.5 * nodes[0]
            lo_ref[1, rows, :] = sum(float(0.5 * D[0, j]) * nodes[j] for j in range(8))
            hi_ref[0, rows, :] = 0.5 * nodes[15]
            hi_ref[1, rows, :] = sum(float(0.5 * D[7, j]) * nodes[8 + j] for j in range(8))


def even_odd(mat, nodes, sign):
    even = [nodes[j] + nodes[7 - j] for j in range(4)]
    odd = [nodes[j] - nodes[7 - j] for j in range(4)]
    out = [None] * 8
    for i in range(4):
        a = sum(float(0.5 * (mat[i, j] + mat[i, 7 - j])) * even[j] for j in range(4))
        b = sum(float(0.5 * (mat[i, j] - mat[i, 7 - j])) * odd[j] for j in range(4))
        out[i] = a + b
        out[7 - i] = (a - b) if sign > 0 else (b - a)
    return out


def average_x(vals):
    vals = list(vals)
    mid = 0.5 * (vals[7] + vals[8])
    vals[7] = vals[8] = mid
    vals[0] = 0.5 * vals[0]
    vals[15] = 0.5 * vals[15]
    return vals


def lane_iota(rows):
    return lax.broadcasted_iota(jnp.int32, (rows, 128), 1)


def pack_columns(fields, x, lane):
    total = None
    for q, field in enumerate(fields):
        ends = jnp.where(lane == 127, field[:, 128:256], field[:, 0:128])
        pos = 2 * (16 * q + x)
        rolled = pltpu.roll(ends, (pos - 127) % 128, 1)
        piece = jnp.where((lane == pos) | (lane == pos + 1), rolled, 0.0)
        total = piece if total is None else total + piece
    return total


def received(par_ref, near_ref, far_ref):
    first = par_ref[0, 0] == 0
    near, far = near_ref[...], far_ref[...]
    return jnp.where(first, far, near), jnp.where(first, near, far)


def halo_columns(par_ref, near_ref, far_ref):
    low, high = received(par_ref, near_ref, far_ref)
    return jnp.where((lane_iota(NYL) % 2) == 0, low, pltpu.roll(high, 126, 1))


def local_z_kernel(u_ref, sz_ref, dz_ref, fz_ref, z1, z2, z3, z4, cols):
    lane = lane_iota(16)
    for t in range(NYL // 16):
        rows = slice(t * 16, t * 16 + 16)
        nodes = [u_ref[k, rows, :] for k in range(NXL)]
        grads = even_odd(D, nodes[:8], -1) + even_odd(D, nodes[8:], -1)
        flat = lambda vals: jnp.concatenate(vals, axis=0)
        p = split(flat(average_x(nodes)))
        g = split(flat(average_x(grads)))
        outs = [
            right_exact(p, sz_ref[...]),
            right(p, dz_ref[...]),
            right_exact(g, sz_ref[...]),
            right(split(flat(nodes)), fz_ref[...]),
        ]
        acc = None
        for k in range(NXL):
            vals = [o[16 * k : 16 * k + 16] for o in outs]
            for ref, val in zip((z1, z2, z3, z4), vals):
                ref[k, rows, :] = val
            piece = pack_columns(vals, k, lane)
            acc = piece if acc is None else acc + piece
        cols[rows, :] = acc


def face_z_kernel(lo_ref, hi_ref, cols_ref, sz_ref, dz_ref, dlt, cols):
    p = split(jnp.concatenate([lo_ref[0], hi_ref[0]], axis=0))
    g = split(jnp.concatenate([lo_ref[1], hi_ref[1]], axis=0))
    outs = [right_exact(p, sz_ref[...]), right(p, dz_ref[...]), right_exact(g, sz_ref[...])]
    lane = lane_iota(NYL)
    acc = cols_ref[...]
    for s, x in ((0, 0), (1, NXL - 1)):
        vals = [o[s * NYL : (s + 1) * NYL] for o in outs]
        for q in range(3):
            dlt[s, q] = vals[q]
        acc = acc + pack_columns(vals, x, lane)
    cols[...] = acc


def local_y_kernel(z1, z2, z3, dlt, sy_ref, dy_ref, sx_, sy_, sz_):
    for x in range(NXL):
        vals = [z1[x], z2[x], z3[x]]
        if x in (0, NXL - 1):
            vals = [v + dlt[0 if x == 0 else 1, q] for q, v in enumerate(vals)]
        sy_[x] = left(dy_ref[...], split(vals[0]))
        sz_[x] = left_exact(sy_ref[...], split(vals[1]))
        sx_[x] = left_exact(sy_ref[...], split(vals[2]))


def row_sum(vals, coefs):
    row = lax.broadcasted_iota(jnp.int32, vals.shape, 0)
    weight = jnp.zeros(vals.shape, F32)
    for k, c in enumerate(coefs):
        weight = jnp.where(row == k, float(c), weight)
    return jnp.sum(vals * weight, axis=0, keepdims=True)


def eddy(sx, sy, sz):
    mag = 1.0 + sx * sx + sy * sy + sz * sz
    return NU_BASE + SGS_COEF * (mag * lax.rsqrt(mag))


def residue_kernel(
    par, near, far, sx_, sy_, sz_, z4, u_ref, v_ref, avg_ref, dy_ref, ry_ref, rz_ref,
    r_ref, out_lo, out_hi, hcols, fx, fyh, fyl,
):
    lane = lane_iota(NYL)
    halo = halo_columns(par, near, far)
    pair = split(halo)
    grad = left(dy_ref[...], pair)
    avg = left_exact(avg_ref[...], pair)
    which = ((lane + 1) % 128) // 32
    hcols[...] = jnp.where(which == 0, grad, jnp.where(which == 3, halo, avg))
    lane16 = lane_iota(16)
    row16 = lax.broadcasted_iota(jnp.int32, (16, NZL), 0)

    def inject(val, rows, q, x):
        rolled = pltpu.roll(hcols[rows, :], (-2 * (16 * q + x)) % 128, 1)
        return jnp.concatenate(
            [
                val[:, 0:128] + jnp.where(lane16 == 0, rolled, 0.0),
                val[:, 128:256] + jnp.where(lane16 == 127, rolled, 0.0),
            ],
            axis=1,
        )

    last = NYL // 16 - 1
    for t in range(last + 1):
        rows = slice(t * 16, t * 16 + 16)
        fz = []
        for x in range(NXL):
            sy = inject(sy_[x, rows, :], rows, 0, x)
            sz = inject(sz_[x, rows, :], rows, 1, x)
            sx = inject(sx_[x, rows, :], rows, 2, x)
            nu = eddy(sx, sy, sz)
            if t in (0, last):
                face, edge, out = (0, 0, out_lo) if t == 0 else (15, -1, out_hi)
                coefs = 0.5 * FM[0] if t == 0 else np.concatenate([np.zeros(8), 0.5 * FM[7]])
                nu = jnp.where(row16 == face, 0.0, nu)
                one = slice(x, x + 1)
                for q, s in enumerate((sx, sy, sz)):
                    out[q, one, :] = s[face : face + 1, :]
                out[5, one, :] = row_sum(inject(z4[x, rows, :], rows, 3, x), coefs)
            uval = u_ref[x, rows, :]
            fx[x, rows, :] = nu * sx - v_ref[0, x, rows, :].astype(F32) * uval
            a, b = split(nu * sy - v_ref[1, x, rows, :].astype(F32) * uval)
            fyh[x, rows, :] = a
            fyl[x, rows, :] = b
            fz.append(nu * sz - v_ref[2, x, rows, :].astype(F32) * uval)
        nodes = [fx[k, rows, :] for k in range(NXL)]
        rx = jnp.concatenate(even_odd(DR, nodes[:8], -1) + even_odd(DR, nodes[8:], -1), axis=0)
        val = rx + right(split(jnp.concatenate(fz, axis=0)), rz_ref[...])
        for x in range(NXL):
            fx[x, rows, :] = val[16 * x : 16 * x + 16]
    face = LY.face
    for x in range(NXL):
        r_ref[x] = fx[x] + left(ry_ref[...], (fyh[x], fyl[x]))
        one = slice(x, x + 1)
        out_lo[3, one, :] = r_ref[x, 0:1, :]
        out_hi[3, one, :] = r_ref[x, NYL - 1 : NYL, :]
        out_lo[4, one, :] = row_sum(r_ref[x, 0:16, :], face[0, 0:16])
        out_hi[4, one, :] = row_sum(r_ref[x, NYL - 16 : NYL, :], face[-1, NYL - 16 :])


def place(pay, x, lane):
    keep = ((lane % 32) // 2) == x
    return jnp.where(keep, pltpu.roll(pay, 2 * x, 1) if x else pay, 0.0)


def filter_kernel(r_ref, z4, hcols, ty_ref, fy_ref, pay_ref, tz_ref, r2, vu, cols):
    lane = lane_iota(NYL)
    acc = None
    for x in range(NXL):
        pair = split(left(ty_ref[...], split(r_ref[x])))
        r2[x] = right(pair, tz_ref[...])
        piece = place(right(pair, pay_ref[...]), x, lane)
        acc = piece if acc is None else acc + piece
        rolled = pltpu.roll(hcols[...], (-2 * (48 + x)) % 128, 1)
        field = z4[x]
        vu[x, :, 0:128] = left(fy_ref[...], split(field[:, 0:128] + jnp.where(lane == 0, rolled, 0.0)))
        vu[x, :, 128:256] = left(fy_ref[...], split(field[:, 128:256] + jnp.where(lane == 127, rolled, 0.0)))
    cols[...] = acc


def y_spread():
    low_t = LY.both[:, 0] + LY.halo[0] + LY.face[-1, -1] * LY.halo[1]
    low_g = (
        LY.both @ LY.res[:, 0] + DR[7, 7] * LY.halo[0] + (LY.face[-1] @ LY.res[:, -1]) * LY.halo[1]
    )
    high_t = LY.both[:, -1] + LY.halo[2] + LY.face[0, 0] * LY.halo[3]
    high_g = (
        LY.both @ LY.res[:, -1] + DR[0, 0] * LY.halo[2] + (LY.face[0] @ LY.res[:, 0]) * LY.halo[3]
    )
    return np.stack(
        [low_t, low_g, LY.halo[0], LY.halo[1], high_t, high_g, LY.halo[2], LY.halo[3]], axis=1
    )


SPREAD = y_spread()


def face_z2_kernel(
    cols_ref, own_lo, own_hi, lo_ref, hi_ref, rx_ref, rz_ref, pay_ref, ay_ref, cols, rows_ref
):
    sides = ((own_lo, lo_ref), (own_hi, hi_ref))
    flux = []
    for own, ref in sides:
        s = [own[q] + ref[q] for q in range(3)]
        nu = eddy(*s)
        flux.append([nu * v for v in s])
    along_x = left(rx_ref[...], split(jnp.concatenate([flux[0][0], flux[1][0]], axis=1)))
    along_z = right(split(jnp.concatenate([flux[0][2], flux[1][2]], axis=0)), rz_ref[...])
    vals = []
    for s, (own, ref) in enumerate(sides):
        tau = along_x[:, s * NZL : (s + 1) * NZL] + along_z[s * NXL : (s + 1) * NXL]
        vals += [tau, flux[s][1], ref[3], ref[4]]
    for k, val in enumerate(vals):
        rows_ref[k] = val
    pay = right(split(jnp.concatenate(vals, axis=0)), pay_ref[...])
    lane16 = lane_iota(NXL)
    row16 = lax.broadcasted_iota(jnp.int32, (NXL, 128), 0)
    keep = ((lane16 % 32) // 2) == row16
    acc = cols_ref[...]
    for k in range(8):
        val = pay[16 * k : 16 * k + 16]
        moved = val
        for bit in (1, 2, 4, 8):
            moved = jnp.where((row16 & bit) != 0, pltpu.roll(moved, 2 * bit, 1), moved)
        vec = jnp.sum(jnp.where(keep, moved, 0.0), axis=0, keepdims=True)
        acc = acc + ay_ref[:, k : k + 1] * vec
    cols[...] = acc


def spread_kernel(r2, vu, rows_ref, lo_ref, hi_ref, ay_ref, tz_ref, out, vout, pay_lo, pay_hi, zr):
    zr[...] = right(split(rows_ref[...].reshape(8 * NXL, NZL)), tz_ref[...]).reshape(8, NXL, NZL)
    row8 = lax.broadcasted_iota(jnp.int32, (8, NZL), 0)
    for t in range(TILES):
        rows = slice(t * 8, t * 8 + 8)
        r, w = [], []
        for x in range(NXL):
            one = slice(x, x + 1)
            val, wal = r2[x, rows, :], vu[x, rows, :]
            if t in (0, 1, 2, TILES - 3, TILES - 2, TILES - 1):
                for k in range(4):
                    k = k if t < 3 else k + 4
                    if np.any(SPREAD[rows, k]):
                        val = val + ay_ref[rows, k : k + 1] * zr[k, one, :]
                out[x, rows, :] = val
            else:
                out[x, rows, :] = val
            if t == 0:
                wal = wal + jnp.where(row8 == 0, lo_ref[5, one, :], 0.0)
            if t == TILES - 1:
                wal = wal + jnp.where(row8 == 7, hi_ref[5, one, :], 0.0)
            vout[x, rows, :] = wal
            r.append(val)
            w.append(wal)
        a = [s + v for s, v in zip(average_x(r), w)]
        pay_lo[0, rows, :] = r[0]
        pay_hi[0, rows, :] = r[15]
        pay_lo[1, rows, :] = sum(float(FM[0, j]) * a[j] for j in range(8))
        pay_hi[1, rows, :] = sum(float(FM[7, j]) * a[8 + j] for j in range(8))


def z_spread():
    add = np.zeros((128, NZL))
    add[0], add[32], add[1], add[33] = LZ.halo
    return add


def z_to_x():
    out = np.zeros((128, 4 * NZL))
    low = np.zeros(16)
    low[:] = LX.face[0]
    high = LX.face[-1]
    for x in range(NXL):
        for q in range(2):
            for side in range(2):
                lane = 2 * (16 * q + x) + side
                vec = LZ.halo[2 * side + q]
                if x == 0:
                    out[lane, 0:NZL] = vec
                if x == NXL - 1:
                    out[lane, 2 * NZL : 3 * NZL] = vec
                out[lane, NZL : 2 * NZL] = low[x] * vec
                out[lane, 3 * NZL :] = high[x] * vec
    return out


def face_x2_kernel(par, near, far, lo_ref, hi_ref, mat_ref, pay_lo, pay_hi, hs):
    low, high = received(par, near, far)
    halo = jnp.where((lane_iota(NYL) % 2) == 0, low, high)
    hs[...] = halo
    add = right(split(halo), mat_ref[...])
    pay_lo[0] = lo_ref[0] + add[:, 0:NZL]
    pay_lo[1] = lo_ref[1] + add[:, NZL : 2 * NZL]
    pay_hi[0] = hi_ref[0] + add[:, 2 * NZL : 3 * NZL]
    pay_hi[1] = hi_ref[1] + add[:, 3 * NZL :]


def local_x_kernel(r2, vu, hs, add_ref, out):
    for t in range(NYL // 16):
        rows = slice(t * 16, t * 16 + 16)
        col = hs[rows, :]
        rolled = [pltpu.roll(col, (-2 * x) % 128, 1) if x else col for x in range(NXL)]
        add = right(split(jnp.concatenate(rolled, axis=0)), add_ref[...])
        r = [r2[x, rows, :] + add[16 * x : 16 * x + 16] for x in range(NXL)]
        a = [s + vu[k, rows, :] for k, s in enumerate(average_x(r))]
        f = average_x(even_odd(FM, a[:8], 1) + even_odd(FM, a[8:], 1))
        f[0] = f[0] + float(0.25 * FM[7, 7]) * r[0]
        f[15] = f[15] + float(0.25 * FM[0, 0]) * r[15]
        for k in range(NXL):
            out[k, rows, :] = f[k]


def final_kernel(val_ref, lo_ref, hi_ref, out_hbm, buf, sems):
    copies = []
    for c in range(4):
        for t in range(3):
            rows = slice(c * 24 + t * 8, c * 24 + t * 8 + 8)
            halo = [lo_ref[0, rows, :], lo_ref[1, rows, :], hi_ref[0, rows, :], hi_ref[1, rows, :]]
            for k in range(NXL):
                val = val_ref[k, rows, :]
                for j in range(4):
                    if LX.halo[j][k] != 0.0:
                        val = val + float(LX.halo[j][k]) * halo[j]
                buf[k, rows, :] = val
        rows = slice(c * 24, c * 24 + 24)
        copies.append(pltpu.make_async_copy(buf.at[:, rows, :], out_hbm.at[:, rows, :], sems.at[c]))
        copies[-1].start()
    for copy in copies:
        copy.wait()


def shift(val, axis, step):
    count = lax.axis_size(axis)
    return lax.ppermute(val, axis, [(i, (i + step) % count) for i in range(count)])


def exchange(lo, hi, axis):
    return shift(hi, axis, 1), shift(lo, axis, -1)


def swap(val, axis, start):
    count = lax.axis_size(axis)
    pairs = [(k % count, (k + 1) % count) for k in range(start, count + start, 2)]
    return lax.ppermute(val, axis, pairs + [(b, a) for a, b in pairs])


def on_device(u, velocity):
    full = (NXL, NYL, NZL)
    face_x = (2, NYL, NZL)
    face_y = (6, NXL, NZL)
    colshape = (NYL, 128)
    par = (lax.axis_index("gz") % 2).astype(jnp.int32).reshape(1, 1)

    sz, dz, fz = exact_right(LZ.avg.T), on_right(LZ.grad.T), on_right(LZ.filt.T)
    sy, dy, fy = exact_left(LY.avg), on_left(LY.grad), on_left(LY.filt)
    ry, rz, rx = on_left(LY.res), on_right(LZ.res.T), on_left(LX.res)
    pay = np.zeros((NZL, 128))
    pay[NZL - 1, 0] = pay[0, 1] = 1.0
    pay[:, 32], pay[:, 33] = LZ.face[-1], LZ.face[0]
    pay = on_right(pay)
    ay = jnp.asarray(SPREAD.astype(np.float32))
    ty, tz = on_left(LY.both), on_right(LZ.both.T)

    u, lo, hi = call(
        face_x_kernel, [full, face_x, face_x], u, hbm=(0,),
        scratch=[pltpu.SemaphoreType.DMA((8,))], name="face_x",
    )
    xlo, xhi = exchange(lo, hi, "gx")
    z1, z2, z3, z4, cols = call(
        local_z_kernel, [full] * 4 + [colshape], u, sz, dz, fz,
        flops=3 * 10**9, nbytes=8 * 10**6, name="local_z",
    )
    dlt, cols = call(face_z_kernel, [(2, 3, NYL, NZL), colshape], xlo, xhi, cols, sz, dz, name="face_z")
    near, far = swap(cols, "gz", 0), swap(cols, "gz", 1)
    sx_, sy_, sz_ = call(
        local_y_kernel, [full] * 3, z1, z2, z3, dlt, sy, dy,
        flops=10**9, nbytes=9 * 10**6, name="local_y",
    )
    r, lo, hi, hcols = call(
        residue_kernel, [full, face_y, face_y, colshape],
        par, near, far, sx_, sy_, sz_, z4, u, velocity, sy, dy, ry, rz, smem=(0,),
        scratch=[pltpu.VMEM(full, F32)] + [pltpu.VMEM(full, BF)] * 2,
        flops=2 * 10**9, nbytes=12 * 10**6, name="residue",
    )
    ylo, yhi = exchange(lo, hi, "gy")
    r2, vu, cols = call(
        filter_kernel, [full, full, colshape], r, z4, hcols, ty, fy, pay, tz,
        flops=2 * 10**9, nbytes=9 * 10**6, name="filter",
    )
    cols, rows = call(
        face_z2_kernel, [colshape, (8, NXL, NZL)], cols, lo, hi, ylo, yhi, rx, rz, pay, ay, name="face_z2"
    )
    near, far = swap(cols, "gz", 0), swap(cols, "gz", 1)
    r2, vu, lo, hi = call(
        spread_kernel, [full, full, face_x, face_x], r2, vu, rows, ylo, yhi, ay, tz,
        scratch=[pltpu.VMEM((8, NXL, NZL), F32)], flops=10**9, nbytes=6 * 10**6, name="spread",
    )
    lo, hi, hs = call(
        face_x2_kernel, [face_x, face_x, colshape], par, near, far, lo, hi, on_right(z_to_x()),
        smem=(0,), name="face_x2",
    )
    xlo, xhi = exchange(lo, hi, "gx")
    val = call(
        local_x_kernel, full, r2, vu, hs, on_right(z_spread()),
        flops=10**9, nbytes=6 * 10**6, name="local_x",
    )
    return call(
        final_kernel, full, val, xlo, xhi, hbm_out=True,
        scratch=[pltpu.VMEM(full, F32), pltpu.SemaphoreType.DMA((4,))], name="final",
    )


def solution(mesh):
    return jax.shard_map(
        on_device,
        mesh=mesh,
        in_specs=(P("gx", "gy", "gz"), P(None, "gx", "gy", "gz")),
        out_specs=P("gx", "gy", "gz"),
        check_vma=False,
    )
```

```python
import functools

import jax
import jax.numpy as jnp
import numpy as np
from jax import lax
from jax.experimental import pallas as pl
from jax.experimental.pallas import tpu as pltpu
from jax.sharding import PartitionSpec as P

DT = 0.002
NU_BASE = 0.3
SGS_COEF = 0.01
FILTER_STRENGTH = 0.3
GLL_POINTS = [
    -1.0,
    -0.8717401485096066,
    -0.5917001814331423,
    -0.2092992179024789,
    0.2092992179024789,
    0.5917001814331423,
    0.8717401485096066,
    1.0,
]
BF = jnp.bfloat16
F32 = jnp.float32
VM = pl.BlockSpec(memory_space=pltpu.VMEM)


def legendre_all(point):
    values_list = [1.0, point]
    for order in range(1, 7):
        values_list.append(
            ((2 * order + 1) * point * values_list[order] - order * values_list[order - 1])
            / (order + 1)
        )
    return values_list


def gll_tables():
    degree = 7
    table = [legendre_all(p) for p in GLL_POINTS]
    top = [table[i][degree] for i in range(8)]
    weights = [2.0 / (degree * (degree + 1) * top[i] * top[i]) for i in range(8)]
    derivative = [[0.0] * 8 for i in range(8)]
    for i in range(8):
        for j in range(8):
            if i != j:
                derivative[i][j] = top[i] / (top[j] * (GLL_POINTS[i] - GLL_POINTS[j]))
    derivative[0][0] = -degree * (degree + 1) / 4.0
    derivative[7][7] = degree * (degree + 1) / 4.0
    damping = [1.0] * 8
    for k in (6, 7):
        damping[k] = 1.0 - FILTER_STRENGTH * ((k - 5) / 2.0) ** 2
    gammas = [2.0 / (2 * k + 1) for k in range(7)] + [2.0 / degree]
    filter_mat = [[0.0] * 8 for i in range(8)]
    for i in range(8):
        for j in range(8):
            total = 0.0
            for k in range(8):
                total += table[i][k] * damping[k] * weights[j] * table[j][k] / gammas[k]
            filter_mat[i][j] = total
    return np.array(derivative), np.array(weights), np.array(filter_mat)


D, WT, FM = gll_tables()
DR = -DT * (D.T * WT[None, :]) / WT[:, None]


def block(mat, length):
    return np.kron(np.eye(length // 8), mat)


def average(length):
    mat = np.eye(length)
    for k in range(8, length, 8):
        mat[k - 1 : k + 1, k - 1 : k + 1] = 0.5
    mat[0, 0] = mat[-1, -1] = 0.5
    return mat


class Line:
    def __init__(self, length):
        avg = average(length)
        filt = block(FM, length)
        self.avg = avg
        self.grad = avg @ block(D, length)
        self.res = block(DR, length)
        self.filt = avg @ filt
        self.both = avg @ filt @ avg
        self.both[0, 0] += 0.25 * FM[7, 7]
        self.both[-1, -1] += 0.25 * FM[0, 0]
        self.face = filt @ avg
        first, last = np.eye(length)[0], np.eye(length)[-1]
        self.halo = np.stack([self.filt[:, 0] * 0.5, 0.5 * first, self.filt[:, -1] * 0.5, 0.5 * last])


def halves(mat):
    mat = np.asarray(mat, np.float64)
    high = mat.astype(jnp.bfloat16)
    low = (mat - high.astype(np.float64)).astype(jnp.bfloat16)
    return high, low


def on_right(mat):
    high, low = halves(mat)
    return jnp.asarray(np.concatenate([high, high, low], axis=0))


def on_left(mat):
    high, low = halves(mat)
    return jnp.asarray(np.concatenate([high, high, low], axis=1))


def exact_right(mat):
    mat = np.asarray(mat).astype(jnp.bfloat16)
    return jnp.asarray(np.concatenate([mat, mat], axis=0))


def exact_left(mat):
    mat = np.asarray(mat).astype(jnp.bfloat16)
    return jnp.asarray(np.concatenate([mat, mat], axis=1))


def split(val):
    high = val.astype(BF)
    return high, (val - high.astype(F32)).astype(BF)


def mm(a, b):
    return jnp.dot(a, b, preferred_element_type=F32)


def right(pair, mat):
    return mm(jnp.concatenate([pair[0], pair[1], pair[0]], axis=1), mat)


def right_exact(pair, mat):
    return mm(jnp.concatenate(pair, axis=1), mat)


def left(mat, pair):
    return mm(mat, jnp.concatenate([pair[0], pair[1], pair[0]], axis=0))


def left_exact(mat, pair):
    return mm(mat, jnp.concatenate(pair, axis=0))


def call(kernel, outs, *args, scratch=(), flops=0, nbytes=0, name=None, hbm=(), hbm_out=False, smem=(), limit=6 << 20):
    single = not isinstance(outs, list)
    place_at = pltpu.HBM if hbm_out else pltpu.VMEM
    shapes = [place_at(tuple(o), F32) for o in ([outs] if single else outs)]
    kinds = {i: pl.BlockSpec(memory_space=pltpu.HBM) for i in hbm}
    kinds.update({i: pl.BlockSpec(memory_space=pltpu.SMEM) for i in smem})
    res = pl.pallas_call(
        kernel,
        out_shape=shapes,
        in_specs=[kinds.get(i, VM) for i in range(len(args))],
        out_specs=[pl.BlockSpec(memory_space=pltpu.HBM) if hbm_out else VM] * len(shapes),
        scratch_shapes=list(scratch),
        compiler_params=pltpu.CompilerParams(vmem_limit_bytes=limit),
        cost_estimate=pl.CostEstimate(flops=flops, bytes_accessed=nbytes, transcendentals=0),
        name=name,
    )(*args)
    return res[0] if single else res


NXL, NYL, NZL = 16, 96, 256
ROWS = NXL * NYL
TILES = NYL // 8


LX, LY, LZ = Line(NXL), Line(NYL), Line(NZL)


def face_hi_kernel(u_ref, hi_ref):
    for t in range(TILES):
        rows = slice(t * 8, t * 8 + 8)
        hi_ref[0, rows, :] = 0.5 * u_ref[7, rows, :]
        hi_ref[1, rows, :] = sum(float(0.5 * D[7, j]) * u_ref[j, rows, :] for j in range(8))


def face_lo_kernel(u_ref, lo_ref):
    for t in range(TILES):
        rows = slice(t * 8, t * 8 + 8)
        lo_ref[0, rows, :] = 0.5 * u_ref[0, rows, :]
        lo_ref[1, rows, :] = sum(float(0.5 * D[0, j]) * u_ref[j, rows, :] for j in range(8))


def even_odd(mat, nodes, sign):
    even = [nodes[j] + nodes[7 - j] for j in range(4)]
    odd = [nodes[j] - nodes[7 - j] for j in range(4)]
    out = [None] * 8
    for i in range(4):
        a = sum(float(0.5 * (mat[i, j] + mat[i, 7 - j])) * even[j] for j in range(4))
        b = sum(float(0.5 * (mat[i, j] - mat[i, 7 - j])) * odd[j] for j in range(4))
        out[i] = a + b
        out[7 - i] = (a - b) if sign > 0 else (b - a)
    return out


def average_x(vals):
    vals = list(vals)
    mid = 0.5 * (vals[7] + vals[8])
    vals[7] = vals[8] = mid
    vals[0] = 0.5 * vals[0]
    vals[15] = 0.5 * vals[15]
    return vals


def lane_iota(rows):
    return lax.broadcasted_iota(jnp.int32, (rows, 128), 1)


def pack_columns(fields, x, lane):
    total = None
    for q, field in enumerate(fields):
        ends = jnp.where(lane == 127, field[:, 128:256], field[:, 0:128])
        pos = 2 * (16 * q + x)
        rolled = pltpu.roll(ends, (pos - 127) % 128, 1)
        piece = jnp.where((lane == pos) | (lane == pos + 1), rolled, 0.0)
        total = piece if total is None else total + piece
    return total


def received(near_ref, far_ref):
    first = lax.rem(lax.axis_index("gz"), 2) == 0
    near, far = near_ref[...], far_ref[...]
    return jnp.where(first, far, near), jnp.where(first, near, far)


def halo_columns(near_ref, far_ref):
    low, high = received(near_ref, far_ref)
    return jnp.where((lane_iota(NYL) % 2) == 0, pltpu.roll(high, 127, 1), pltpu.roll(low, 1, 1))


def local_z_kernel(ulo_ref, uhi_ref, sz_ref, dz_ref, fz_ref, z1, z2, z3, z4, cols):
    lane = lane_iota(16)
    for t in range(NYL // 16):
        rows = slice(t * 16, t * 16 + 16)
        nodes = [ref[k, rows, :] for ref in (ulo_ref, uhi_ref) for k in range(8)]
        grads = even_odd(D, nodes[:8], -1) + even_odd(D, nodes[8:], -1)
        flat = lambda vals: jnp.concatenate(vals, axis=0)
        p = split(flat(average_x(nodes)))
        g = split(flat(average_x(grads)))
        outs = [
            right_exact(p, sz_ref[...]),
            right(p, dz_ref[...]),
            right_exact(g, sz_ref[...]),
            right(split(flat(nodes)), fz_ref[...]),
        ]
        acc = None
        for k in range(NXL):
            vals = [o[16 * k : 16 * k + 16] for o in outs]
            for ref, val in zip((z1, z2, z3, z4), vals):
                ref[k, rows, :] = val
            piece = pack_columns(vals, k, lane)
            acc = piece if acc is None else acc + piece
        cols[rows, :] = acc


def face_z_kernel(lo_ref, hi_ref, cols_ref, sz_ref, dz_ref, dlt, cols):
    p = split(jnp.concatenate([lo_ref[0], hi_ref[0]], axis=0))
    g = split(jnp.concatenate([lo_ref[1], hi_ref[1]], axis=0))
    outs = [right_exact(p, sz_ref[...]), right(p, dz_ref[...]), right_exact(g, sz_ref[...])]
    lane = lane_iota(NYL)
    acc = cols_ref[...]
    for s, x in ((0, 0), (1, NXL - 1)):
        vals = [o[s * NYL : (s + 1) * NYL] for o in outs]
        for q in range(3):
            dlt[s, q] = vals[q]
        acc = acc + pack_columns(vals, x, lane)
    cols[...] = acc


def local_y_kernel(z1, z2, z3, sy_ref, dy_ref, sx_, sy_, sz_):
    for x in range(1, NXL - 1):
        sy_[x - 1] = left(dy_ref[...], split(z1[x]))
        sz_[x - 1] = left_exact(sy_ref[...], split(z2[x]))
        sx_[x - 1] = left_exact(sy_ref[...], split(z3[x]))


def product_kernel(ulo_ref, uhi_ref, v_ref, after_ref, h_ref):
    for x in range(NXL):
        u = ulo_ref[x] if x < 8 else uhi_ref[x - 8]
        for d in range(3):
            h_ref[d, x] = v_ref[d, x].astype(F32) * u


def row_sum(vals, coefs):
    row = lax.broadcasted_iota(jnp.int32, vals.shape, 0)
    weight = jnp.zeros(vals.shape, F32)
    for k, c in enumerate(coefs):
        weight = jnp.where(row == k, float(c), weight)
    return jnp.sum(vals * weight, axis=0, keepdims=True)


def eddy(sx, sy, sz):
    mag = 1.0 + sx * sx + sy * sy + sz * sz
    return NU_BASE + SGS_COEF * (mag * lax.rsqrt(mag))


def residue_kernel(
    sx_, sy_, sz_, z1, z2, z3, z4, dlt, h_ref, avg_ref, dy_ref, ry_ref, rz_ref,
    r_ref, out_lo, out_hi, fx, fyh, fyl, edge,
):
    for s, x in ((0, 0), (1, NXL - 1)):
        edge[s, 1] = left(dy_ref[...], split(z1[x] + dlt[s, 0]))
        edge[s, 2] = left_exact(avg_ref[...], split(z2[x] + dlt[s, 1]))
        edge[s, 0] = left_exact(avg_ref[...], split(z3[x] + dlt[s, 2]))
    row16 = lax.broadcasted_iota(jnp.int32, (16, NZL), 0)
    lane16 = lax.broadcasted_iota(jnp.int32, (16, NZL), 1)
    inner = (lane16 != 0) & (lane16 != NZL - 1)
    last = NYL // 16 - 1
    for t in range(last + 1):
        rows = slice(t * 16, t * 16 + 16)
        mask = inner
        if t == 0:
            mask = mask & (row16 != 0)
        if t == last:
            mask = mask & (row16 != 15)
        mask = mask.astype(F32)
        fz = []
        for x in range(NXL):
            if x in (0, NXL - 1):
                sx, sy, sz = [edge[0 if x == 0 else 1, q, rows, :] for q in range(3)]
            else:
                sx, sy, sz = [ref[x - 1, rows, :] for ref in (sx_, sy_, sz_)]
            nu = eddy(sx, sy, sz) * mask
            if t in (0, last):
                face, out = (0, out_lo) if t == 0 else (15, out_hi)
                coefs = 0.5 * FM[0] if t == 0 else np.concatenate([np.zeros(8), 0.5 * FM[7]])
                one = slice(x, x + 1)
                for q, val in enumerate((sx, sy, sz)):
                    row = val[face : face + 1, :]
                    out[q, one, :] = jnp.where(inner[0:1, :], row, 0.0)
                out[5, one, :] = row_sum(z4[x, rows, :], coefs)
            fx[x, rows, :] = nu * sx - h_ref[0, x, rows, :]
            a, b = split(nu * sy - h_ref[1, x, rows, :])
            fyh[x, rows, :] = a
            fyl[x, rows, :] = b
            fz.append(nu * sz - h_ref[2, x, rows, :])
        nodes = [fx[k, rows, :] for k in range(NXL)]
        rx = jnp.concatenate(even_odd(DR, nodes[:8], -1) + even_odd(DR, nodes[8:], -1), axis=0)
        val = rx + right(split(jnp.concatenate(fz, axis=0)), rz_ref[...])
        for x in range(NXL):
            fx[x, rows, :] = val[16 * x : 16 * x + 16]
    face = LY.face
    for x in range(NXL):
        r_ref[x] = fx[x] + left(ry_ref[...], (fyh[x], fyl[x]))
        one = slice(x, x + 1)
        out_lo[3, one, :] = r_ref[x, 0:1, :]
        out_hi[3, one, :] = r_ref[x, NYL - 1 : NYL, :]
        out_lo[4, one, :] = row_sum(r_ref[x, 0:16, :], face[0, 0:16])
        out_hi[4, one, :] = row_sum(r_ref[x, NYL - 16 : NYL, :], face[-1, NYL - 16 :])


def z_columns_x():
    mat = np.zeros((128, 128))
    for side in range(2):
        mat[side:32:2, side:32:2] = LX.res.T
    return mat


def z_face_vectors():
    mat = np.zeros((128, NZL))
    for x in range(NXL):
        for side, node in ((0, NZL - 1), (1, 0)):
            mat[2 * x + side, node] = 1.0
            mat[32 + 2 * x + side] = LZ.res[:, node]
    return mat


def y_rows():
    rows = np.zeros((8, NYL))
    rows[0], rows[1] = LY.face[0], LY.face[-1]
    rows[2, 0:8], rows[3, NYL - 8 :] = 0.5 * FM[0], 0.5 * FM[7]
    return rows


def face_y_kernel(
    near, far, cols, lo_ref, hi_ref, avg_ref, dy_ref, ry_ref, rx_ref, zv_ref, yr_ref,
    out_lo, out_hi, cval, halo_ref,
):
    lane = lane_iota(NYL)
    halo = halo_columns(near, far)
    halo_ref[...] = halo
    pair = split(cols[...] + halo)
    sy = left(dy_ref[...], pair)
    avg = left_exact(avg_ref[...], pair)
    sz, sx = pltpu.roll(avg, 96, 1), pltpu.roll(avg, 64, 1)
    row = lax.broadcasted_iota(jnp.int32, (NYL, 128), 0)
    keep = (lane < 32) & (row != 0) & (row != NYL - 1)
    nu = jnp.where(keep, eddy(sx, sy, sz), 0.0)
    tau = right(split(nu * sx), rx_ref[...]) + left(ry_ref[...], split(nu * sy))
    val = tau + pltpu.roll(nu * sz, 32, 1)
    cval[...] = val
    rows = left(yr_ref[...], split(jnp.concatenate([val, pltpu.roll(halo, 32, 1)], axis=1)))
    lane16 = lane_iota(NXL)
    row16 = lax.broadcasted_iota(jnp.int32, (NXL, 128), 0)
    diag = ((lane16 % 32) // 2) == row16
    short, long = diag & (lane16 < 32), diag & (lane16 < 64)
    parts_ = []
    for s, r in ((0, 0), (1, NYL - 1)):
        one = slice(r, r + 1)
        for vec, keep in (
            (sx[one], short), (sy[one], short), (sz[one], short), (val[one], long),
            (rows[s : s + 1, 0:128], long), (rows[2 + s : 3 + s, 128:256], short),
        ):
            parts_.append(jnp.where(keep, jnp.broadcast_to(vec, (NXL, 128)), 0.0))
    add = right(split(jnp.concatenate(parts_, axis=0)), zv_ref[...])
    for q in range(6):
        out_lo[q] = lo_ref[q] + add[16 * q : 16 * q + 16]
        out_hi[q] = hi_ref[q] + add[96 + 16 * q : 112 + 16 * q]


def place(pay, x, lane):
    keep = ((lane % 32) // 2) == x
    return jnp.where(keep, pltpu.roll(pay, 2 * x, 1) if x else pay, 0.0)


def filter_kernel(r_ref, cval, ty_ref, pay_ref, zc_ref, r1, cols, cout):
    lane = lane_iota(NYL)
    acc = None
    for c in range(4):
        for x in range(4 * c, 4 * c + 4):
            r1[x] = left(ty_ref[...], split(r_ref[x]))
        val = r1[4 * c : 4 * c + 4].reshape(4 * NYL, NZL)
        out = right(split(val), pay_ref[...])
        for k in range(4):
            piece = place(out[k * NYL : (k + 1) * NYL], 4 * c + k, lane)
            acc = piece if acc is None else acc + piece
    val = left(ty_ref[...], split(cval[...]))
    cout[...] = val
    cols[...] = acc + right(split(val), zc_ref[...])


def z_columns_z():
    mat = np.zeros((128, 128))
    for x in range(NXL):
        for side, node in ((0, NZL - 1), (1, 0)):
            at = 2 * x + side
            mat[at, at], mat[32 + at, at] = 1.0, LZ.res[node, node]
            mat[at, 32 + at] = LZ.face[node, node]
            mat[32 + at, 32 + at] = LZ.face[node] @ LZ.res[:, node]
    return mat


def y_spread():
    low_t = LY.both[:, 0] + LY.halo[0] + LY.face[-1, -1] * LY.halo[1]
    low_g = (
        LY.both @ LY.res[:, 0] + DR[7, 7] * LY.halo[0] + (LY.face[-1] @ LY.res[:, -1]) * LY.halo[1]
    )
    high_t = LY.both[:, -1] + LY.halo[2] + LY.face[0, 0] * LY.halo[3]
    high_g = (
        LY.both @ LY.res[:, -1] + DR[0, 0] * LY.halo[2] + (LY.face[0] @ LY.res[:, 0]) * LY.halo[3]
    )
    return np.stack(
        [low_t, low_g, LY.halo[0], LY.halo[1], high_t, high_g, LY.halo[2], LY.halo[3]], axis=1
    )


SPREAD = y_spread()


def face_z2_kernel(
    cols_ref, own_lo, own_hi, lo_ref, hi_ref, rx_ref, rz_ref, pay_ref, ay_ref, cols, rows_ref
):
    both = ((own_lo, lo_ref), (own_hi, hi_ref))
    flux = []
    for own, ref in both:
        s = [own[q] + ref[q] for q in range(3)]
        nu = eddy(*s)
        flux.append([nu * v for v in s])
    along_x = left(rx_ref[...], split(jnp.concatenate([flux[0][0], flux[1][0]], axis=1)))
    along_z = right(split(jnp.concatenate([flux[0][2], flux[1][2]], axis=0)), rz_ref[...])
    vals = []
    for s, (own, ref) in enumerate(both):
        tau = along_x[:, s * NZL : (s + 1) * NZL] + along_z[s * NXL : (s + 1) * NXL]
        vals += [tau, flux[s][1], ref[3], ref[4]]
    for k, val in enumerate(vals):
        rows_ref[k] = val
    pay = right(split(jnp.concatenate(vals, axis=0)), pay_ref[...])
    lane16 = lane_iota(NXL)
    row16 = lax.broadcasted_iota(jnp.int32, (NXL, 128), 0)
    keep = ((lane16 % 32) // 2) == row16
    vecs = []
    for k in range(8):
        val = pay[16 * k : 16 * k + 16]
        moved = val
        for bit in (1, 2, 4, 8):
            moved = jnp.where((row16 & bit) != 0, pltpu.roll(moved, 2 * bit, 1), moved)
        vec = jnp.sum(jnp.where(keep, moved, 0.0), axis=0, keepdims=True)
        vecs.append(vec)
    for rows, ks in ((slice(0, 24), range(4)), (slice(NYL - 24, NYL), range(4, 8))):
        acc = cols_ref[rows, :]
        for k in ks:
            acc = acc + ay_ref[rows, k : k + 1] * vecs[k]
        cols[rows, :] = acc
    cols[24 : NYL - 24, :] = cols_ref[24 : NYL - 24, :]


def spread_kernel(
    r1, z4, hcols, rows_ref, lo_ref, hi_ref, ay_ref, fy_ref, tz_ref, out, vout, pay_lo, pay_hi, zr
):
    zr[...] = right(split(rows_ref[...].reshape(8 * NXL, NZL)), tz_ref[...]).reshape(8, NXL, NZL)
    lane = lane_iota(NYL)
    row8 = lax.broadcasted_iota(jnp.int32, (8, NZL), 0)
    for c in range(4):
        xs = slice(4 * c, 4 * c + 4)
        val = r1[xs].reshape(4 * NYL, NZL)
        out[xs] = right(split(val), tz_ref[...]).reshape(4, NYL, NZL)
        for x in range(4 * c, 4 * c + 4):
            rolled = pltpu.roll(hcols[...], (-2 * (48 + x) - 1) % 128, 1)
            field = jnp.concatenate(
                [
                    z4[x, :, 0:128] + jnp.where(lane == 0, rolled, 0.0),
                    z4[x, :, 128:256] + jnp.where(lane == 127, rolled, 0.0),
                ],
                axis=1,
            )
            vout[x] = left(fy_ref[...], split(field))
    for x in range(NXL):
        one = slice(x, x + 1)
        for t in (0, 1, 2, TILES - 3, TILES - 2, TILES - 1):
            rows = slice(t * 8, t * 8 + 8)
            val = out[x, rows, :]
            for k in range(4) if t < 3 else range(4, 8):
                if np.any(SPREAD[rows, k]):
                    val = val + ay_ref[rows, k : k + 1] * zr[k, one, :]
            out[x, rows, :] = val
        low, high = slice(0, 8), slice(NYL - 8, NYL)
        vout[x, low, :] = vout[x, low, :] + jnp.where(row8 == 0, lo_ref[5, one, :], 0.0)
        vout[x, high, :] = vout[x, high, :] + jnp.where(row8 == 7, hi_ref[5, one, :], 0.0)
    for t in range(TILES):
        rows = slice(t * 8, t * 8 + 8)
        r = [out[x, rows, :] for x in range(NXL)]
        a = [s + vout[x, rows, :] for x, s in enumerate(average_x(r))]
        pay_lo[0, rows, :] = r[0]
        pay_hi[0, rows, :] = r[15]
        pay_lo[1, rows, :] = sum(float(FM[0, j]) * a[j] for j in range(8))
        pay_hi[1, rows, :] = sum(float(FM[7, j]) * a[8 + j] for j in range(8))


def z_vectors():
    vecs = [[LZ.halo[0], LZ.halo[2]], [LZ.halo[1], LZ.halo[3]]]
    vecs.append([LZ.both[:, -1], LZ.both[:, 0]])
    vecs.append([LZ.both @ LZ.res[:, -1], LZ.both @ LZ.res[:, 0]])
    return vecs


def z_spread():
    add = np.zeros((128, NZL))
    for q, pair in enumerate(z_vectors()):
        for side in range(2):
            add[32 * q + side] = pair[side]
    return add


def z_to_x():
    out = np.zeros((128, 4 * NZL))
    low, high = LX.face[0], LX.face[-1]
    for x in range(NXL):
        for q, pair in enumerate(z_vectors()):
            for side in range(2):
                lane, vec = 2 * (16 * q + x) + side, pair[side]
                if x == 0:
                    out[lane, 0:NZL] = vec
                if x == NXL - 1:
                    out[lane, 2 * NZL : 3 * NZL] = vec
                out[lane, NZL : 2 * NZL] = low[x] * vec
                out[lane, 3 * NZL :] = high[x] * vec
    return out


def face_x2_kernel(near, far, cval, lo_ref, hi_ref, mat_ref, pay_lo, pay_hi, hs):
    low, high = received(near, far)
    lane = lane_iota(NYL)
    halo = jnp.where((lane % 2) == 0, low, high)
    halo = jnp.where(lane < 64, halo, pltpu.roll(cval[...], 64, 1))
    hs[...] = halo
    add = right(split(halo), mat_ref[...])
    for q in range(2):
        pay_lo[q] = lo_ref[q] + add[:, q * NZL : (q + 1) * NZL]
        pay_hi[q] = hi_ref[q] + add[:, (q + 2) * NZL : (q + 3) * NZL]


def local_x_kernel(r2, vu, hs, add_ref, out):
    for t in range(NYL // 16):
        rows = slice(t * 16, t * 16 + 16)
        col = hs[rows, :]
        rolled = [pltpu.roll(col, (-2 * x) % 128, 1) if x else col for x in range(NXL)]
        add = right(split(jnp.concatenate(rolled, axis=0)), add_ref[...])
        r = [r2[x, rows, :] + add[16 * x : 16 * x + 16] for x in range(NXL)]
        a = [s + vu[k, rows, :] for k, s in enumerate(average_x(r))]
        f = average_x(even_odd(FM, a[:8], 1) + even_odd(FM, a[8:], 1))
        f[0] = f[0] + float(0.25 * FM[7, 7]) * r[0]
        f[15] = f[15] + float(0.25 * FM[0, 0]) * r[15]
        for k in range(NXL):
            out[k, rows, :] = f[k]


def final_kernel(val_ref, lo_ref, hi_ref, out_hbm, buf, sems):
    copies = []
    for c in range(4):
        for t in range(3):
            rows = slice(c * 24 + t * 8, c * 24 + t * 8 + 8)
            halo = [lo_ref[0, rows, :], lo_ref[1, rows, :], hi_ref[0, rows, :], hi_ref[1, rows, :]]
            for k in range(NXL):
                val = val_ref[k, rows, :]
                for j in range(4):
                    if LX.halo[j][k] != 0.0:
                        val = val + float(LX.halo[j][k]) * halo[j]
                buf[k, rows, :] = val
        rows = slice(c * 24, c * 24 + 24)
        copies.append(pltpu.make_async_copy(buf.at[:, rows, :], out_hbm.at[:, rows, :], sems.at[c]))
        copies[-1].start()
    for copy in copies:
        copy.wait()


def shift(val, axis, step):
    count = lax.axis_size(axis)
    return lax.ppermute(val, axis, [(i, (i + step) % count) for i in range(count)])


def exchange(lo, hi, axis):
    return shift(hi, axis, 1), shift(lo, axis, -1)


def swap(val, axis, start):
    count = lax.axis_size(axis)
    pairs = [(k % count, (k + 1) % count) for k in range(start, count + start, 2)]
    return lax.ppermute(val, axis, pairs + [(b, a) for a, b in pairs])


def on_device(u, velocity):
    full = (NXL, NYL, NZL)
    face_x = (2, NYL, NZL)
    face_y = (6, NXL, NZL)
    colshape = (NYL, 128)

    sz, dz, fz = exact_right(LZ.avg.T), on_right(LZ.grad.T), on_right(LZ.filt.T)
    sy, dy, fy = exact_left(LY.avg), on_left(LY.grad), on_left(LY.filt)
    ry, rz, rx = on_left(LY.res), on_right(LZ.res.T), on_left(LX.res)
    pay = np.zeros((NZL, 128))
    pay[NZL - 1, 0] = pay[0, 1] = 1.0
    pay[:, 32], pay[:, 33] = LZ.face[-1], LZ.face[0]
    pay = on_right(pay)
    ay = jnp.asarray(SPREAD.astype(np.float32))
    ty, tz = on_left(LY.both), on_right(LZ.both.T)

    ulo, uhi = u[:8], u[8:]
    hi = call(face_hi_kernel, face_x, uhi, name="face_hi")
    xlo = shift(hi, "gx", 1)
    lo = call(face_lo_kernel, face_x, ulo, name="face_lo")
    xhi = shift(lo, "gx", -1)
    z1, z2, z3, z4, cols = call(
        local_z_kernel, [full] * 4 + [colshape], ulo, uhi, sz, dz, fz,
        flops=3 * 10**9, nbytes=8 * 10**6, name="local_z",
    )
    h = call(
        product_kernel, (3,) + full, ulo, uhi, velocity, cols, flops=10**9, nbytes=8 * 10**6, name="product"
    )
    inner = (NXL - 2, NYL, NZL)
    sx_, sy_, sz_ = call(
        local_y_kernel, [inner] * 3, z1, z2, z3, sy, dy,
        flops=10**9, nbytes=9 * 10**6, name="local_y",
    )
    dlt, cols = call(
        face_z_kernel, [(2, 3, NYL, NZL), colshape], xlo, xhi, cols, sz, dz, name="face_z"
    )
    near, far = swap(cols, "gz", 0), swap(cols, "gz", 1)
    r, lo, hi = call(
        residue_kernel, [full, face_y, face_y],
        sx_, sy_, sz_, z1, z2, z3, z4, dlt, h, sy, dy, ry, rz,
        scratch=[pltpu.VMEM(full, F32)] + [pltpu.VMEM(full, BF)] * 2 + [pltpu.VMEM((2, 3, NYL, NZL), F32)],
        flops=3 * 10**9, nbytes=12 * 10**6, name="residue",
    )
    lo, hi, cval, hcols = call(
        face_y_kernel, [face_y, face_y, colshape, colshape], near, far, cols, lo, hi, sy, dy, ry,
        on_right(z_columns_x()), on_right(z_face_vectors()), on_left(y_rows()), name="face_y",
    )
    ylo, yhi = exchange(lo, hi, "gy")
    r1, cols, cval = call(
        filter_kernel, [full, colshape, colshape], r, cval, ty, pay, on_right(z_columns_z()),
        flops=2 * 10**9, nbytes=9 * 10**6, name="filter",
    )
    cols, rows = call(
        face_z2_kernel, [colshape, (8, NXL, NZL)], cols, lo, hi, ylo, yhi, rx, rz, pay, ay,
        name="face_z2",
    )
    near, far = swap(cols, "gz", 0), swap(cols, "gz", 1)
    r2, vu, lo, hi = call(
        spread_kernel, [full, full, face_x, face_x], r1, z4, hcols, rows, ylo, yhi, ay, fy, tz,
        scratch=[pltpu.VMEM((8, NXL, NZL), F32)], flops=2 * 10**9, nbytes=9 * 10**6, name="spread",
    )
    lo, hi, hs = call(
        face_x2_kernel, [face_x, face_x, colshape], near, far, cval, lo, hi, on_right(z_to_x()),
        name="face_x2",
    )
    xlo, xhi = exchange(lo, hi, "gx")
    val = call(
        local_x_kernel, full, r2, vu, hs, on_right(z_spread()),
        flops=10**9, nbytes=6 * 10**6, name="local_x",
    )
    return call(
        final_kernel, full, val, xlo, xhi, hbm_out=True,
        scratch=[pltpu.VMEM(full, F32), pltpu.SemaphoreType.DMA((4,))], name="final",
    )


def solution(mesh):
    return jax.shard_map(
        on_device,
        mesh=mesh,
        in_specs=(P("gx", "gy", "gz"), P(None, "gx", "gy", "gz")),
        out_specs=P("gx", "gy", "gz"),
        check_vma=False,
    )
```

```python
import functools

import jax
import jax.numpy as jnp
import numpy as np
from jax import lax
from jax.experimental import pallas as pl
from jax.experimental.pallas import tpu as pltpu
from jax.sharding import PartitionSpec as P

DT = 0.002
NU_BASE = 0.3
SGS_COEF = 0.01
FILTER_STRENGTH = 0.3
GLL_POINTS = [
    -1.0,
    -0.8717401485096066,
    -0.5917001814331423,
    -0.2092992179024789,
    0.2092992179024789,
    0.5917001814331423,
    0.8717401485096066,
    1.0,
]
BF = jnp.bfloat16
F32 = jnp.float32
VM = pl.BlockSpec(memory_space=pltpu.VMEM)


def legendre_all(point):
    values_list = [1.0, point]
    for order in range(1, 7):
        values_list.append(
            ((2 * order + 1) * point * values_list[order] - order * values_list[order - 1])
            / (order + 1)
        )
    return values_list


def gll_tables():
    degree = 7
    table = [legendre_all(p) for p in GLL_POINTS]
    top = [table[i][degree] for i in range(8)]
    weights = [2.0 / (degree * (degree + 1) * top[i] * top[i]) for i in range(8)]
    derivative = [[0.0] * 8 for i in range(8)]
    for i in range(8):
        for j in range(8):
            if i != j:
                derivative[i][j] = top[i] / (top[j] * (GLL_POINTS[i] - GLL_POINTS[j]))
    derivative[0][0] = -degree * (degree + 1) / 4.0
    derivative[7][7] = degree * (degree + 1) / 4.0
    damping = [1.0] * 8
    for k in (6, 7):
        damping[k] = 1.0 - FILTER_STRENGTH * ((k - 5) / 2.0) ** 2
    gammas = [2.0 / (2 * k + 1) for k in range(7)] + [2.0 / degree]
    filter_mat = [[0.0] * 8 for i in range(8)]
    for i in range(8):
        for j in range(8):
            total = 0.0
            for k in range(8):
                total += table[i][k] * damping[k] * weights[j] * table[j][k] / gammas[k]
            filter_mat[i][j] = total
    return np.array(derivative), np.array(weights), np.array(filter_mat)


D, WT, FM = gll_tables()
DR = -DT * (D.T * WT[None, :]) / WT[:, None]


def block(mat, length):
    return np.kron(np.eye(length // 8), mat)


def average(length):
    mat = np.eye(length)
    for k in range(8, length, 8):
        mat[k - 1 : k + 1, k - 1 : k + 1] = 0.5
    mat[0, 0] = mat[-1, -1] = 0.5
    return mat


class Line:
    def __init__(self, length):
        avg = average(length)
        filt = block(FM, length)
        self.avg = avg
        self.grad = avg @ block(D, length)
        self.res = block(DR, length)
        self.filt = avg @ filt
        self.both = avg @ filt @ avg
        self.both[0, 0] += 0.25 * FM[7, 7]
        self.both[-1, -1] += 0.25 * FM[0, 0]
        self.face = filt @ avg
        first, last = np.eye(length)[0], np.eye(length)[-1]
        self.halo = np.stack([self.filt[:, 0] * 0.5, 0.5 * first, self.filt[:, -1] * 0.5, 0.5 * last])


def halves(mat):
    mat = np.asarray(mat, np.float64)
    high = mat.astype(jnp.bfloat16)
    low = (mat - high.astype(np.float64)).astype(jnp.bfloat16)
    return high, low


def on_right(mat):
    high, low = halves(mat)
    return jnp.asarray(np.concatenate([high, high, low], axis=0))


def on_left(mat):
    high, low = halves(mat)
    return jnp.asarray(np.concatenate([high, high, low], axis=1))


def exact_right(mat):
    mat = np.asarray(mat).astype(jnp.bfloat16)
    return jnp.asarray(np.concatenate([mat, mat], axis=0))


def exact_left(mat):
    mat = np.asarray(mat).astype(jnp.bfloat16)
    return jnp.asarray(np.concatenate([mat, mat], axis=1))


def split(val):
    high = val.astype(BF)
    return high, (val - high.astype(F32)).astype(BF)


def mm(a, b):
    return jnp.dot(a, b, preferred_element_type=F32)


def right(pair, mat):
    return mm(jnp.concatenate([pair[0], pair[1], pair[0]], axis=1), mat)


def right_exact(pair, mat):
    return mm(jnp.concatenate(pair, axis=1), mat)


def left(mat, pair):
    return mm(mat, jnp.concatenate([pair[0], pair[1], pair[0]], axis=0))


def left_exact(mat, pair):
    return mm(mat, jnp.concatenate(pair, axis=0))


def call(kernel, outs, *args, scratch=(), flops=0, nbytes=0, name=None, hbm=(), hbm_out=False, smem=(), limit=6 << 20):
    single = not isinstance(outs, list)
    place_at = pltpu.HBM if hbm_out else pltpu.VMEM
    shapes = [place_at(tuple(o), F32) for o in ([outs] if single else outs)]
    kinds = {i: pl.BlockSpec(memory_space=pltpu.HBM) for i in hbm}
    kinds.update({i: pl.BlockSpec(memory_space=pltpu.SMEM) for i in smem})
    res = pl.pallas_call(
        kernel,
        out_shape=shapes,
        in_specs=[kinds.get(i, VM) for i in range(len(args))],
        out_specs=[pl.BlockSpec(memory_space=pltpu.HBM) if hbm_out else VM] * len(shapes),
        scratch_shapes=list(scratch),
        compiler_params=pltpu.CompilerParams(vmem_limit_bytes=limit),
        cost_estimate=pl.CostEstimate(flops=flops, bytes_accessed=nbytes, transcendentals=0),
        name=name,
    )(*args)
    return res[0] if single else res


NXL, NYL, NZL = 16, 96, 256
ROWS = NXL * NYL
TILES = NYL // 8


LX, LY, LZ = Line(NXL), Line(NYL), Line(NZL)


def face_hi_kernel(u_ref, hi_ref):
    for t in range(TILES):
        rows = slice(t * 8, t * 8 + 8)
        hi_ref[0, rows, :] = 0.5 * u_ref[7, rows, :]
        hi_ref[1, rows, :] = sum(float(0.5 * D[7, j]) * u_ref[j, rows, :] for j in range(8))


def face_lo_kernel(u_ref, lo_ref):
    for t in range(TILES):
        rows = slice(t * 8, t * 8 + 8)
        lo_ref[0, rows, :] = 0.5 * u_ref[0, rows, :]
        lo_ref[1, rows, :] = sum(float(0.5 * D[0, j]) * u_ref[j, rows, :] for j in range(8))


def even_odd(mat, nodes, sign):
    even = [nodes[j] + nodes[7 - j] for j in range(4)]
    odd = [nodes[j] - nodes[7 - j] for j in range(4)]
    out = [None] * 8
    for i in range(4):
        a = sum(float(0.5 * (mat[i, j] + mat[i, 7 - j])) * even[j] for j in range(4))
        b = sum(float(0.5 * (mat[i, j] - mat[i, 7 - j])) * odd[j] for j in range(4))
        out[i] = a + b
        out[7 - i] = (a - b) if sign > 0 else (b - a)
    return out


def average_x(vals):
    vals = list(vals)
    mid = 0.5 * (vals[7] + vals[8])
    vals[7] = vals[8] = mid
    vals[0] = 0.5 * vals[0]
    vals[15] = 0.5 * vals[15]
    return vals


def lane_iota(rows):
    return lax.broadcasted_iota(jnp.int32, (rows, 128), 1)


def pack_columns(fields, x, lane):
    total = None
    for q, field in enumerate(fields):
        ends = jnp.where(lane == 127, field[:, 128:256], field[:, 0:128])
        pos = 2 * (16 * q + x)
        rolled = pltpu.roll(ends, (pos - 127) % 128, 1)
        piece = jnp.where((lane == pos) | (lane == pos + 1), rolled, 0.0)
        total = piece if total is None else total + piece
    return total


def received(near_ref, far_ref):
    first = lax.rem(lax.axis_index("gz"), 2) == 0
    near, far = near_ref[...], far_ref[...]
    return jnp.where(first, far, near), jnp.where(first, near, far)


def halo_columns(near_ref, far_ref):
    low, high = received(near_ref, far_ref)
    return jnp.where((lane_iota(NYL) % 2) == 0, pltpu.roll(high, 127, 1), pltpu.roll(low, 1, 1))


def local_z_kernel(ulo_ref, uhi_ref, sz_ref, dz_ref, fz_ref, z1, z2, z3, z4, cols):
    lane = lane_iota(16)
    for t in range(NYL // 16):
        rows = slice(t * 16, t * 16 + 16)
        nodes = [ref[k, rows, :] for ref in (ulo_ref, uhi_ref) for k in range(8)]
        grads = even_odd(D, nodes[:8], -1) + even_odd(D, nodes[8:], -1)
        flat = lambda vals: jnp.concatenate(vals, axis=0)
        p = split(flat(average_x(nodes)))
        g = split(flat(average_x(grads)))
        outs = [
            right_exact(p, sz_ref[...]),
            right(p, dz_ref[...]),
            right_exact(g, sz_ref[...]),
            right(split(flat(nodes)), fz_ref[...]),
        ]
        acc = None
        for k in range(NXL):
            vals = [o[16 * k : 16 * k + 16] for o in outs]
            for ref, val in zip((z1, z2, z3, z4), vals):
                ref[k, rows, :] = val
            piece = pack_columns(vals, k, lane)
            acc = piece if acc is None else acc + piece
        cols[rows, :] = acc


def face_z_kernel(lo_ref, hi_ref, cols_ref, sz_ref, dz_ref, dlt, cols):
    p = split(jnp.concatenate([lo_ref[0], hi_ref[0]], axis=0))
    g = split(jnp.concatenate([lo_ref[1], hi_ref[1]], axis=0))
    outs = [right_exact(p, sz_ref[...]), right(p, dz_ref[...]), right_exact(g, sz_ref[...])]
    lane = lane_iota(NYL)
    acc = cols_ref[...]
    for s, x in ((0, 0), (1, NXL - 1)):
        vals = [o[s * NYL : (s + 1) * NYL] for o in outs]
        for q in range(3):
            dlt[s, q] = vals[q]
        acc = acc + pack_columns(vals, x, lane)
    cols[...] = acc


def local_y_kernel(z1, z2, z3, sy_ref, dy_ref, sx_, sy_, sz_):
    for x in range(1, NXL - 1):
        sy_[x - 1] = left(dy_ref[...], split(z1[x]))
        sz_[x - 1] = left_exact(sy_ref[...], split(z2[x]))
        sx_[x - 1] = left_exact(sy_ref[...], split(z3[x]))


def product_kernel(ulo_ref, uhi_ref, v_ref, after_ref, h_ref):
    for x in range(NXL):
        u = ulo_ref[x] if x < 8 else uhi_ref[x - 8]
        for d in range(3):
            h_ref[d, x] = v_ref[d, x].astype(F32) * u


def row_sum(vals, coefs):
    row = lax.broadcasted_iota(jnp.int32, vals.shape, 0)
    weight = jnp.zeros(vals.shape, F32)
    for k, c in enumerate(coefs):
        weight = jnp.where(row == k, float(c), weight)
    return jnp.sum(vals * weight, axis=0, keepdims=True)


def eddy(sx, sy, sz):
    mag = 1.0 + sx * sx + sy * sy + sz * sz
    return NU_BASE + SGS_COEF * (mag * lax.rsqrt(mag))


def residue_kernel(
    sx_, sy_, sz_, z1, z2, z3, z4, dlt, h_ref, avg_ref, dy_ref, ry_ref, rz_ref,
    r_ref, out_lo, out_hi, fx, fyh, fyl, edge,
):
    for s, x in ((0, 0), (1, NXL - 1)):
        edge[s, 1] = left(dy_ref[...], split(z1[x] + dlt[s, 0]))
        edge[s, 2] = left_exact(avg_ref[...], split(z2[x] + dlt[s, 1]))
        edge[s, 0] = left_exact(avg_ref[...], split(z3[x] + dlt[s, 2]))
    row16 = lax.broadcasted_iota(jnp.int32, (16, NZL), 0)
    lane16 = lax.broadcasted_iota(jnp.int32, (16, NZL), 1)
    inner = (lane16 != 0) & (lane16 != NZL - 1)
    last = NYL // 16 - 1
    for t in range(last + 1):
        rows = slice(t * 16, t * 16 + 16)
        mask = inner
        if t == 0:
            mask = mask & (row16 != 0)
        if t == last:
            mask = mask & (row16 != 15)
        mask = mask.astype(F32)
        fz = []
        for x in range(NXL):
            if x in (0, NXL - 1):
                sx, sy, sz = [edge[0 if x == 0 else 1, q, rows, :] for q in range(3)]
            else:
                sx, sy, sz = [ref[x - 1, rows, :] for ref in (sx_, sy_, sz_)]
            nu = eddy(sx, sy, sz) * mask
            if t in (0, last):
                face, out = (0, out_lo) if t == 0 else (15, out_hi)
                coefs = 0.5 * FM[0] if t == 0 else np.concatenate([np.zeros(8), 0.5 * FM[7]])
                one = slice(x, x + 1)
                for q, val in enumerate((sx, sy, sz)):
                    row = val[face : face + 1, :]
                    out[q, one, :] = jnp.where(inner[0:1, :], row, 0.0)
                out[5, one, :] = row_sum(z4[x, rows, :], coefs)
            fx[x, rows, :] = nu * sx - h_ref[0, x, rows, :]
            a, b = split(nu * sy - h_ref[1, x, rows, :])
            fyh[x, rows, :] = a
            fyl[x, rows, :] = b
            fz.append(nu * sz - h_ref[2, x, rows, :])
        nodes = [fx[k, rows, :] for k in range(NXL)]
        rx = jnp.concatenate(even_odd(DR, nodes[:8], -1) + even_odd(DR, nodes[8:], -1), axis=0)
        val = rx + right(split(jnp.concatenate(fz, axis=0)), rz_ref[...])
        for x in range(NXL):
            fx[x, rows, :] = val[16 * x : 16 * x + 16]
    face = LY.face
    for x in range(NXL):
        r_ref[x] = fx[x] + left(ry_ref[...], (fyh[x], fyl[x]))
        one = slice(x, x + 1)
        out_lo[3, one, :] = r_ref[x, 0:1, :]
        out_hi[3, one, :] = r_ref[x, NYL - 1 : NYL, :]
        out_lo[4, one, :] = row_sum(r_ref[x, 0:16, :], face[0, 0:16])
        out_hi[4, one, :] = row_sum(r_ref[x, NYL - 16 : NYL, :], face[-1, NYL - 16 :])


def z_columns_x():
    mat = np.zeros((128, 128))
    for side in range(2):
        mat[side:32:2, side:32:2] = LX.res.T
    return mat


def z_face_vectors():
    mat = np.zeros((128, NZL))
    for x in range(NXL):
        for side, node in ((0, NZL - 1), (1, 0)):
            mat[2 * x + side, node] = 1.0
            mat[32 + 2 * x + side] = LZ.res[:, node]
    return mat


def y_rows():
    rows = np.zeros((8, NYL))
    rows[0], rows[1] = LY.face[0], LY.face[-1]
    rows[2, 0:8], rows[3, NYL - 8 :] = 0.5 * FM[0], 0.5 * FM[7]
    return rows


def face_y_kernel(
    near, far, cols, lo_ref, hi_ref, avg_ref, dy_ref, ry_ref, rx_ref, zv_ref, yr_ref,
    out_lo, out_hi, cval, halo_ref,
):
    lane = lane_iota(NYL)
    halo = halo_columns(near, far)
    halo_ref[...] = halo
    pair = split(cols[...] + halo)
    sy = left(dy_ref[...], pair)
    avg = left_exact(avg_ref[...], pair)
    sz, sx = pltpu.roll(avg, 96, 1), pltpu.roll(avg, 64, 1)
    row = lax.broadcasted_iota(jnp.int32, (NYL, 128), 0)
    keep = (lane < 32) & (row != 0) & (row != NYL - 1)
    nu = jnp.where(keep, eddy(sx, sy, sz), 0.0)
    tau = right(split(nu * sx), rx_ref[...]) + left(ry_ref[...], split(nu * sy))
    val = tau + pltpu.roll(nu * sz, 32, 1)
    cval[...] = val
    rows = left(yr_ref[...], split(jnp.concatenate([val, pltpu.roll(halo, 32, 1)], axis=1)))
    lane16 = lane_iota(NXL)
    row16 = lax.broadcasted_iota(jnp.int32, (NXL, 128), 0)
    diag = ((lane16 % 32) // 2) == row16
    short, long = diag & (lane16 < 32), diag & (lane16 < 64)
    parts_ = []
    for s, r in ((0, 0), (1, NYL - 1)):
        one = slice(r, r + 1)
        for vec, keep in (
            (sx[one], short), (sy[one], short), (sz[one], short), (val[one], long),
            (rows[s : s + 1, 0:128], long), (rows[2 + s : 3 + s, 128:256], short),
        ):
            parts_.append(jnp.where(keep, jnp.broadcast_to(vec, (NXL, 128)), 0.0))
    add = right(split(jnp.concatenate(parts_, axis=0)), zv_ref[...])
    for q in range(6):
        out_lo[q] = lo_ref[q] + add[16 * q : 16 * q + 16]
        out_hi[q] = hi_ref[q] + add[96 + 16 * q : 112 + 16 * q]


def place(pay, x, lane):
    keep = ((lane % 32) // 2) == x
    return jnp.where(keep, pltpu.roll(pay, 2 * x, 1) if x else pay, 0.0)


def filter_kernel(r_ref, cval, ty_ref, pay_ref, zc_ref, r1, cols, cout):
    lane = lane_iota(NYL)
    acc = None
    for c in range(4):
        for x in range(4 * c, 4 * c + 4):
            r1[x] = left(ty_ref[...], split(r_ref[x]))
        val = r1[4 * c : 4 * c + 4].reshape(4 * NYL, NZL)
        out = right(split(val), pay_ref[...])
        for k in range(4):
            piece = place(out[k * NYL : (k + 1) * NYL], 4 * c + k, lane)
            acc = piece if acc is None else acc + piece
    val = left(ty_ref[...], split(cval[...]))
    cout[...] = val
    cols[...] = acc + right(split(val), zc_ref[...])


def z_columns_z():
    mat = np.zeros((128, 128))
    for x in range(NXL):
        for side, node in ((0, NZL - 1), (1, 0)):
            at = 2 * x + side
            mat[at, at], mat[32 + at, at] = 1.0, LZ.res[node, node]
            mat[at, 32 + at] = LZ.face[node, node]
            mat[32 + at, 32 + at] = LZ.face[node] @ LZ.res[:, node]
    return mat


def y_spread():
    low_t = LY.both[:, 0] + LY.halo[0] + LY.face[-1, -1] * LY.halo[1]
    low_g = (
        LY.both @ LY.res[:, 0] + DR[7, 7] * LY.halo[0] + (LY.face[-1] @ LY.res[:, -1]) * LY.halo[1]
    )
    high_t = LY.both[:, -1] + LY.halo[2] + LY.face[0, 0] * LY.halo[3]
    high_g = (
        LY.both @ LY.res[:, -1] + DR[0, 0] * LY.halo[2] + (LY.face[0] @ LY.res[:, 0]) * LY.halo[3]
    )
    return np.stack(
        [low_t, low_g, LY.halo[0], LY.halo[1], high_t, high_g, LY.halo[2], LY.halo[3]], axis=1
    )


SPREAD = y_spread()


def face_z2_kernel(
    cols_ref, after_ref, own_lo, own_hi, lo_ref, hi_ref, rx_ref, rz_ref, pay_ref, ay_ref, cols, rows_ref
):
    both = ((own_lo, lo_ref), (own_hi, hi_ref))
    flux = []
    for own, ref in both:
        s = [own[q] + ref[q] for q in range(3)]
        nu = eddy(*s)
        flux.append([nu * v for v in s])
    along_x = left(rx_ref[...], split(jnp.concatenate([flux[0][0], flux[1][0]], axis=1)))
    along_z = right(split(jnp.concatenate([flux[0][2], flux[1][2]], axis=0)), rz_ref[...])
    vals = []
    for s, (own, ref) in enumerate(both):
        tau = along_x[:, s * NZL : (s + 1) * NZL] + along_z[s * NXL : (s + 1) * NXL]
        vals += [tau, flux[s][1], ref[3], ref[4]]
    for k, val in enumerate(vals):
        rows_ref[k] = val
    pay = right(split(jnp.concatenate(vals, axis=0)), pay_ref[...])
    lane16 = lane_iota(NXL)
    row16 = lax.broadcasted_iota(jnp.int32, (NXL, 128), 0)
    keep = ((lane16 % 32) // 2) == row16
    vecs = []
    for k in range(8):
        val = pay[16 * k : 16 * k + 16]
        moved = val
        for bit in (1, 2, 4, 8):
            moved = jnp.where((row16 & bit) != 0, pltpu.roll(moved, 2 * bit, 1), moved)
        vec = jnp.sum(jnp.where(keep, moved, 0.0), axis=0, keepdims=True)
        vecs.append(vec)
    for rows, ks in ((slice(0, 24), range(4)), (slice(NYL - 24, NYL), range(4, 8))):
        acc = cols_ref[rows, :]
        for k in ks:
            acc = acc + ay_ref[rows, k : k + 1] * vecs[k]
        cols[rows, :] = acc
    cols[24 : NYL - 24, :] = cols_ref[24 : NYL - 24, :]


def filter_z_kernel(r1, z4, hcols, fy_ref, tz_ref, out, vout):
    lane = lane_iota(NYL)
    for c in range(4):
        xs = slice(4 * c, 4 * c + 4)
        val = r1[xs].reshape(4 * NYL, NZL)
        out[xs] = right(split(val), tz_ref[...]).reshape(4, NYL, NZL)
        for x in range(4 * c, 4 * c + 4):
            rolled = pltpu.roll(hcols[...], (-2 * (48 + x) - 1) % 128, 1)
            field = jnp.concatenate(
                [
                    z4[x, :, 0:128] + jnp.where(lane == 0, rolled, 0.0),
                    z4[x, :, 128:256] + jnp.where(lane == 127, rolled, 0.0),
                ],
                axis=1,
            )
            vout[x] = left(fy_ref[...], split(field))


def spread_kernel(
    r2, vu, rows_ref, lo_ref, hi_ref, cval, ay_ref, tz_ref, mat_ref, out, vout, pay_lo, pay_hi, zr
):
    zr[...] = right(split(rows_ref[...].reshape(8 * NXL, NZL)), tz_ref[...]).reshape(8, NXL, NZL)
    add = right(split(cval[...]), mat_ref[...])
    row8 = lax.broadcasted_iota(jnp.int32, (8, NZL), 0)
    for t in range(TILES):
        rows = slice(t * 8, t * 8 + 8)
        r, w = [], []
        for x in range(NXL):
            one = slice(x, x + 1)
            val, wal = r2[x, rows, :], vu[x, rows, :]
            for k in range(8):
                if np.any(SPREAD[rows, k]):
                    val = val + ay_ref[rows, k : k + 1] * zr[k, one, :]
            if t == 0:
                wal = wal + jnp.where(row8 == 0, lo_ref[5, one, :], 0.0)
            if t == TILES - 1:
                wal = wal + jnp.where(row8 == 7, hi_ref[5, one, :], 0.0)
            out[x, rows, :] = val
            vout[x, rows, :] = wal
            r.append(val)
            w.append(wal)
        a = [s + v for s, v in zip(average_x(r), w)]
        low = sum(float(FM[0, j]) * a[j] for j in range(8))
        high = sum(float(FM[7, j]) * a[8 + j] for j in range(8))
        for q, (ref, val) in enumerate(((pay_lo, r[0]), (pay_lo, low), (pay_hi, r[15]), (pay_hi, high))):
            ref[q % 2, rows, :] = val + add[rows, q * NZL : (q + 1) * NZL]


def z_vectors():
    vecs = [[LZ.halo[0], LZ.halo[2]], [LZ.halo[1], LZ.halo[3]]]
    vecs.append([LZ.both[:, -1], LZ.both[:, 0]])
    vecs.append([LZ.both @ LZ.res[:, -1], LZ.both @ LZ.res[:, 0]])
    return vecs


def z_spread():
    add = np.zeros((128, NZL))
    for q, pair in enumerate(z_vectors()):
        for side in range(2):
            add[32 * q + side] = pair[side]
    return add


def z_to_x():
    out = np.zeros((128, 4 * NZL))
    low, high = LX.face[0], LX.face[-1]
    for x in range(NXL):
        for q, pair in enumerate(z_vectors()[2:]):
            for side in range(2):
                lane, vec = 2 * (16 * q + x) + side, pair[side]
                if x == 0:
                    out[lane, 0:NZL] = vec
                if x == NXL - 1:
                    out[lane, 2 * NZL : 3 * NZL] = vec
                out[lane, NZL : 2 * NZL] = low[x] * vec
                out[lane, 3 * NZL :] = high[x] * vec
    return out


def z_short():
    out = np.zeros((128, 128))
    low, high = LX.face[0], LX.face[-1]
    for x in range(NXL):
        for q in range(2):
            for side in range(2):
                lane, c = 2 * (16 * q + x) + side, 2 * q + side
                if x == 0:
                    out[lane, c] = 1.0
                if x == NXL - 1:
                    out[lane, 8 + c] = 1.0
                out[lane, 4 + c], out[lane, 12 + c] = low[x], high[x]
    return out


def z_long():
    out = np.zeros((16, 4 * NZL))
    for q, pair in enumerate(z_vectors()[:2]):
        for side in range(2):
            for k in range(4):
                out[4 * k + 2 * q + side, k * NZL : (k + 1) * NZL] = pair[side]
    high, low = halves(out)
    rest = np.zeros((80, 4 * NZL)).astype(jnp.bfloat16)
    return jnp.asarray(np.concatenate([high, high, low, rest], axis=0))


def forward_kernel(near, far, cval, mat_ref, flo, fhi, hs):
    low, high = received(near, far)
    lane = lane_iota(NYL)
    halo = jnp.where((lane % 2) == 0, low, high)
    hs[...] = jnp.where(lane < 64, halo, pltpu.roll(cval[...], 64, 1))
    short = right(split(halo), mat_ref[...])
    lane8 = lane_iota(8)
    for ref, base in ((flo, 0), (fhi, 8)):
        acc = None
        for t in range(TILES):
            piece = pltpu.roll(short[8 * t : 8 * t + 8], (8 * t - base) % 128, 1)
            piece = jnp.where((lane8 // 8) == t, piece, 0.0)
            acc = piece if acc is None else acc + piece
        ref[...] = acc


def forwarded(glo, ghi, mat):
    lane8 = lane_iota(8)
    tiles = []
    for t in range(TILES):
        low = pltpu.roll(glo, (-8 * t) % 128, 1)
        high = pltpu.roll(ghi, (8 - 8 * t) % 128, 1)
        tiles.append(jnp.where(lane8 < 8, low, jnp.where(lane8 < 16, high, 0.0)))
    val = jnp.concatenate(tiles, axis=0)
    top = val.astype(BF).astype(F32)
    val = top + pltpu.roll(val - top, 16, 1) + pltpu.roll(top, 32, 1)
    return mm(val.astype(BF), mat)


def local_x_kernel(r2, vu, hs, add_ref, out):
    for t in range(NYL // 16):
        rows = slice(t * 16, t * 16 + 16)
        col = hs[rows, :]
        rolled = [pltpu.roll(col, (-2 * x) % 128, 1) if x else col for x in range(NXL)]
        add = right(split(jnp.concatenate(rolled, axis=0)), add_ref[...])
        r = [r2[x, rows, :] + add[16 * x : 16 * x + 16] for x in range(NXL)]
        a = [s + vu[k, rows, :] for k, s in enumerate(average_x(r))]
        f = average_x(even_odd(FM, a[:8], 1) + even_odd(FM, a[8:], 1))
        f[0] = f[0] + float(0.25 * FM[7, 7]) * r[0]
        f[15] = f[15] + float(0.25 * FM[0, 0]) * r[15]
        for k in range(NXL):
            out[k, rows, :] = f[k]


def final_kernel(val_ref, lo_ref, hi_ref, glo_ref, ghi_ref, mat_ref, out_hbm, buf, sems):
    copies = []
    add = forwarded(glo_ref[...], ghi_ref[...], mat_ref[...])
    for c in range(4):
        for t in range(3):
            rows = slice(c * 24 + t * 8, c * 24 + t * 8 + 8)
            halo = [lo_ref[0, rows, :], lo_ref[1, rows, :], hi_ref[0, rows, :], hi_ref[1, rows, :]]
            halo = [v + add[rows, j * NZL : (j + 1) * NZL] for j, v in enumerate(halo)]
            for k in range(NXL):
                val = val_ref[k, rows, :]
                for j in range(4):
                    if LX.halo[j][k] != 0.0:
                        val = val + float(LX.halo[j][k]) * halo[j]
                buf[k, rows, :] = val
        rows = slice(c * 24, c * 24 + 24)
        copies.append(pltpu.make_async_copy(buf.at[:, rows, :], out_hbm.at[:, rows, :], sems.at[c]))
        copies[-1].start()
    for copy in copies:
        copy.wait()


def shift(val, axis, step):
    count = lax.axis_size(axis)
    return lax.ppermute(val, axis, [(i, (i + step) % count) for i in range(count)])


def exchange(lo, hi, axis):
    return shift(hi, axis, 1), shift(lo, axis, -1)


def swap(val, axis, start):
    count = lax.axis_size(axis)
    pairs = [(k % count, (k + 1) % count) for k in range(start, count + start, 2)]
    return lax.ppermute(val, axis, pairs + [(b, a) for a, b in pairs])


def on_device(u, velocity):
    full = (NXL, NYL, NZL)
    face_x = (2, NYL, NZL)
    face_y = (6, NXL, NZL)
    colshape = (NYL, 128)

    sz, dz, fz = exact_right(LZ.avg.T), on_right(LZ.grad.T), on_right(LZ.filt.T)
    sy, dy, fy = exact_left(LY.avg), on_left(LY.grad), on_left(LY.filt)
    ry, rz, rx = on_left(LY.res), on_right(LZ.res.T), on_left(LX.res)
    pay = np.zeros((NZL, 128))
    pay[NZL - 1, 0] = pay[0, 1] = 1.0
    pay[:, 32], pay[:, 33] = LZ.face[-1], LZ.face[0]
    pay = on_right(pay)
    ay = jnp.asarray(SPREAD.astype(np.float32))
    ty, tz = on_left(LY.both), on_right(LZ.both.T)

    ulo, uhi = u[:8], u[8:]
    hi = call(face_hi_kernel, face_x, uhi, name="face_hi")
    xlo = shift(hi, "gx", 1)
    lo = call(face_lo_kernel, face_x, ulo, name="face_lo")
    xhi = shift(lo, "gx", -1)
    z1, z2, z3, z4, cols = call(
        local_z_kernel, [full] * 4 + [colshape], ulo, uhi, sz, dz, fz,
        flops=3 * 10**9, nbytes=8 * 10**6, name="local_z",
    )
    h = call(
        product_kernel, (3,) + full, ulo, uhi, velocity, cols, flops=10**9, nbytes=8 * 10**6, name="product"
    )
    inner = (NXL - 2, NYL, NZL)
    sx_, sy_, sz_ = call(
        local_y_kernel, [inner] * 3, z1, z2, z3, sy, dy,
        flops=10**9, nbytes=9 * 10**6, name="local_y",
    )
    dlt, cols = call(
        face_z_kernel, [(2, 3, NYL, NZL), colshape], xlo, xhi, cols, sz, dz, name="face_z"
    )
    near, far = swap(cols, "gz", 0), swap(cols, "gz", 1)
    r, lo, hi = call(
        residue_kernel, [full, face_y, face_y],
        sx_, sy_, sz_, z1, z2, z3, z4, dlt, h, sy, dy, ry, rz,
        scratch=[pltpu.VMEM(full, F32)] + [pltpu.VMEM(full, BF)] * 2 + [pltpu.VMEM((2, 3, NYL, NZL), F32)],
        flops=3 * 10**9, nbytes=12 * 10**6, name="residue",
    )
    lo, hi, cval, hcols = call(
        face_y_kernel, [face_y, face_y, colshape, colshape], near, far, cols, lo, hi, sy, dy, ry,
        on_right(z_columns_x()), on_right(z_face_vectors()), on_left(y_rows()), name="face_y",
    )
    ylo, yhi = exchange(lo, hi, "gy")
    r1, cols, cval = call(
        filter_kernel, [full, colshape, colshape], r, cval, ty, pay, on_right(z_columns_z()),
        flops=2 * 10**9, nbytes=9 * 10**6, name="filter",
    )
    r2, vu = call(
        filter_z_kernel, [full, full], r1, z4, hcols, fy, tz, flops=2 * 10**9, nbytes=9 * 10**6, name="filter_z"
    )
    cols, rows = call(
        face_z2_kernel, [colshape, (8, NXL, NZL)], cols, r2, lo, hi, ylo, yhi, rx, rz, pay, ay,
        name="face_z2",
    )
    near, far = swap(cols, "gz", 0), swap(cols, "gz", 1)
    r2, vu, lo, hi = call(
        spread_kernel, [full, full, face_x, face_x], r2, vu, rows, ylo, yhi, cval, ay, tz, on_right(z_to_x()),
        scratch=[pltpu.VMEM((8, NXL, NZL), F32)], flops=10**9, nbytes=9 * 10**6, name="spread",
    )
    xlo, xhi = exchange(lo, hi, "gx")
    flo, fhi, hs = call(
        forward_kernel, [(8, 128), (8, 128), colshape], near, far, cval, on_right(z_short()), name="forward"
    )
    glo, ghi = exchange(flo, fhi, "gx")
    val = call(
        local_x_kernel, full, r2, vu, hs, on_right(z_spread()),
        flops=10**11, nbytes=10**8, name="local_x",
    )
    return call(
        final_kernel, full, val, xlo, xhi, glo, ghi, z_long(), hbm_out=True,
        scratch=[pltpu.VMEM(full, F32), pltpu.SemaphoreType.DMA((4,))], name="final",
    )


def solution(mesh):
    return jax.shard_map(
        on_device,
        mesh=mesh,
        in_specs=(P("gx", "gy", "gz"), P(None, "gx", "gy", "gz")),
        out_specs=P("gx", "gy", "gz"),
        check_vma=False,
    )
```

```python
import functools

import jax
import jax.numpy as jnp
import numpy as np
from jax import lax
from jax.experimental import pallas as pl
from jax.experimental.pallas import tpu as pltpu
from jax.sharding import PartitionSpec as P

DT = 0.002
NU_BASE = 0.3
SGS_COEF = 0.01
FILTER_STRENGTH = 0.3
GLL_POINTS = [
    -1.0,
    -0.8717401485096066,
    -0.5917001814331423,
    -0.2092992179024789,
    0.2092992179024789,
    0.5917001814331423,
    0.8717401485096066,
    1.0,
]
BF = jnp.bfloat16
F32 = jnp.float32
VM = pl.BlockSpec(memory_space=pltpu.VMEM)


def legendre_all(point):
    values_list = [1.0, point]
    for order in range(1, 7):
        values_list.append(
            ((2 * order + 1) * point * values_list[order] - order * values_list[order - 1])
            / (order + 1)
        )
    return values_list


def gll_tables():
    degree = 7
    table = [legendre_all(p) for p in GLL_POINTS]
    top = [table[i][degree] for i in range(8)]
    weights = [2.0 / (degree * (degree + 1) * top[i] * top[i]) for i in range(8)]
    derivative = [[0.0] * 8 for i in range(8)]
    for i in range(8):
        for j in range(8):
            if i != j:
                derivative[i][j] = top[i] / (top[j] * (GLL_POINTS[i] - GLL_POINTS[j]))
    derivative[0][0] = -degree * (degree + 1) / 4.0
    derivative[7][7] = degree * (degree + 1) / 4.0
    damping = [1.0] * 8
    for k in (6, 7):
        damping[k] = 1.0 - FILTER_STRENGTH * ((k - 5) / 2.0) ** 2
    gammas = [2.0 / (2 * k + 1) for k in range(7)] + [2.0 / degree]
    filter_mat = [[0.0] * 8 for i in range(8)]
    for i in range(8):
        for j in range(8):
            total = 0.0
            for k in range(8):
                total += table[i][k] * damping[k] * weights[j] * table[j][k] / gammas[k]
            filter_mat[i][j] = total
    return np.array(derivative), np.array(weights), np.array(filter_mat)


D, WT, FM = gll_tables()
DR = -DT * (D.T * WT[None, :]) / WT[:, None]


def block(mat, length):
    return np.kron(np.eye(length // 8), mat)


def average(length):
    mat = np.eye(length)
    for k in range(8, length, 8):
        mat[k - 1 : k + 1, k - 1 : k + 1] = 0.5
    mat[0, 0] = mat[-1, -1] = 0.5
    return mat


class Line:
    def __init__(self, length):
        avg = average(length)
        filt = block(FM, length)
        self.avg = avg
        self.grad = avg @ block(D, length)
        self.res = block(DR, length)
        self.filt = avg @ filt
        self.both = avg @ filt @ avg
        self.both[0, 0] += 0.25 * FM[7, 7]
        self.both[-1, -1] += 0.25 * FM[0, 0]
        self.face = filt @ avg
        first, last = np.eye(length)[0], np.eye(length)[-1]
        self.halo = np.stack([self.filt[:, 0] * 0.5, 0.5 * first, self.filt[:, -1] * 0.5, 0.5 * last])


def halves(mat):
    mat = np.asarray(mat, np.float64)
    high = mat.astype(jnp.bfloat16)
    low = (mat - high.astype(np.float64)).astype(jnp.bfloat16)
    return high, low


def on_right(mat):
    high, low = halves(mat)
    return jnp.asarray(np.concatenate([high, high, low], axis=0))


def on_left(mat):
    high, low = halves(mat)
    return jnp.asarray(np.concatenate([high, high, low], axis=1))


def exact_right(mat):
    mat = np.asarray(mat).astype(jnp.bfloat16)
    return jnp.asarray(np.concatenate([mat, mat], axis=0))


def exact_left(mat):
    mat = np.asarray(mat).astype(jnp.bfloat16)
    return jnp.asarray(np.concatenate([mat, mat], axis=1))


def split(val):
    high = val.astype(BF)
    return high, (val - high.astype(F32)).astype(BF)


def mm(a, b):
    return jnp.dot(a, b, preferred_element_type=F32)


def right(pair, mat):
    return mm(jnp.concatenate([pair[0], pair[1], pair[0]], axis=1), mat)


def right_exact(pair, mat):
    return mm(jnp.concatenate(pair, axis=1), mat)


def left(mat, pair):
    return mm(mat, jnp.concatenate([pair[0], pair[1], pair[0]], axis=0))


def left_exact(mat, pair):
    return mm(mat, jnp.concatenate(pair, axis=0))


def call(kernel, outs, *args, scratch=(), flops=0, nbytes=0, name=None, hbm=(), hbm_out=False, smem=(), limit=6 << 20):
    single = not isinstance(outs, list)
    place_at = pltpu.HBM if hbm_out else pltpu.VMEM
    pairs = [o if isinstance(o[0], tuple) else (o, F32) for o in ([outs] if single else outs)]
    shapes = [place_at(shape, dtype) for shape, dtype in pairs]
    kinds = {i: pl.BlockSpec(memory_space=pltpu.HBM) for i in hbm}
    kinds.update({i: pl.BlockSpec(memory_space=pltpu.SMEM) for i in smem})
    res = pl.pallas_call(
        kernel,
        out_shape=shapes,
        in_specs=[kinds.get(i, VM) for i in range(len(args))],
        out_specs=[pl.BlockSpec(memory_space=pltpu.HBM) if hbm_out else VM] * len(shapes),
        scratch_shapes=list(scratch),
        compiler_params=pltpu.CompilerParams(vmem_limit_bytes=limit),
        cost_estimate=pl.CostEstimate(flops=flops, bytes_accessed=nbytes, transcendentals=0),
        name=name,
    )(*args)
    return res[0] if single else res


NXL, NYL, NZL = 16, 96, 256
ROWS = NXL * NYL
TILES = NYL // 8


LX, LY, LZ = Line(NXL), Line(NYL), Line(NZL)


def face_hi_kernel(u_ref, hi_ref):
    for t in range(TILES):
        rows = slice(t * 8, t * 8 + 8)
        hi_ref[0, rows, :] = 0.5 * u_ref[7, rows, :]
        hi_ref[1, rows, :] = sum(float(0.5 * D[7, j]) * u_ref[j, rows, :] for j in range(8))


def face_lo_kernel(u_ref, lo_ref):
    for t in range(TILES):
        rows = slice(t * 8, t * 8 + 8)
        lo_ref[0, rows, :] = 0.5 * u_ref[0, rows, :]
        lo_ref[1, rows, :] = sum(float(0.5 * D[0, j]) * u_ref[j, rows, :] for j in range(8))


def even_odd(mat, nodes, sign):
    even = [nodes[j] + nodes[7 - j] for j in range(4)]
    odd = [nodes[j] - nodes[7 - j] for j in range(4)]
    out = [None] * 8
    for i in range(4):
        a = sum(float(0.5 * (mat[i, j] + mat[i, 7 - j])) * even[j] for j in range(4))
        b = sum(float(0.5 * (mat[i, j] - mat[i, 7 - j])) * odd[j] for j in range(4))
        out[i] = a + b
        out[7 - i] = (a - b) if sign > 0 else (b - a)
    return out


def average_x(vals):
    vals = list(vals)
    mid = 0.5 * (vals[7] + vals[8])
    vals[7] = vals[8] = mid
    vals[0] = 0.5 * vals[0]
    vals[15] = 0.5 * vals[15]
    return vals


def lane_iota(rows):
    return lax.broadcasted_iota(jnp.int32, (rows, 128), 1)


def pack_columns(fields, x, lane):
    total = None
    for q, field in enumerate(fields):
        ends = jnp.where(lane == 127, field[:, 128:256], field[:, 0:128])
        pos = 2 * (16 * q + x)
        rolled = pltpu.roll(ends, (pos - 127) % 128, 1)
        piece = jnp.where((lane == pos) | (lane == pos + 1), rolled, 0.0)
        total = piece if total is None else total + piece
    return total


def received(near_ref, far_ref):
    first = lax.rem(lax.axis_index("gz"), 2) == 0
    near, far = near_ref[...], far_ref[...]
    return jnp.where(first, far, near), jnp.where(first, near, far)


def halo_columns(near_ref, far_ref):
    low, high = received(near_ref, far_ref)
    return jnp.where((lane_iota(NYL) % 2) == 0, pltpu.roll(high, 127, 1), pltpu.roll(low, 1, 1))


def local_z_kernel(ulo_ref, uhi_ref, sz_ref, dfz_ref, z1, z2, z3, z4, cols):
    lane = lane_iota(16)
    for t in range(NYL // 16):
        rows = slice(t * 16, t * 16 + 16)
        p = split(jnp.concatenate([ref[k, rows, :] for ref in (ulo_ref, uhi_ref) for k in range(8)], axis=0))
        slabs = lambda val: [val[16 * k : 16 * k + 16] for k in range(NXL)]
        avg = slabs(right_exact(p, sz_ref[...]))
        both = right(p, dfz_ref[...])
        grads = even_odd(D, avg[:8], -1) + even_odd(D, avg[8:], -1)
        outs = [
            average_x(avg),
            average_x(slabs(both[:, 0:NZL])),
            average_x(grads),
            slabs(both[:, NZL:]),
        ]
        acc = None
        for k in range(NXL):
            vals = [o[k] for o in outs]
            for ref, val in zip((z1, z2, z3, z4), vals):
                ref[k, rows, :] = val
            piece = pack_columns(vals, k, lane)
            acc = piece if acc is None else acc + piece
        cols[rows, :] = acc


def face_z_kernel(lo_ref, hi_ref, cols_ref, sz_ref, dz_ref, dlt, cols):
    p = split(jnp.concatenate([lo_ref[0], hi_ref[0]], axis=0))
    g = split(jnp.concatenate([lo_ref[1], hi_ref[1]], axis=0))
    outs = [right_exact(p, sz_ref[...]), right(p, dz_ref[...]), right_exact(g, sz_ref[...])]
    lane = lane_iota(NYL)
    acc = cols_ref[...]
    for s, x in ((0, 0), (1, NXL - 1)):
        vals = [o[s * NYL : (s + 1) * NYL] for o in outs]
        for q in range(3):
            dlt[s, q] = vals[q]
        acc = acc + pack_columns(vals, x, lane)
    cols[...] = acc


def row_sum(vals, coefs):
    row = lax.broadcasted_iota(jnp.int32, vals.shape, 0)
    weight = jnp.zeros(vals.shape, F32)
    for k, c in enumerate(coefs):
        weight = jnp.where(row == k, float(c), weight)
    return jnp.sum(vals * weight, axis=0, keepdims=True)


def eddy(sx, sy, sz):
    mag = 1.0 + sx * sx + sy * sy + sz * sz
    return NU_BASE + SGS_COEF * (mag * lax.rsqrt(mag))


def face_mask():
    row = lax.broadcasted_iota(jnp.int32, (NYL, NZL), 0)
    lane = lax.broadcasted_iota(jnp.int32, (NYL, NZL), 1)
    inner = (lane != 0) & (lane != NZL - 1) & (row != 0) & (row != NYL - 1)
    return inner.astype(F32)


def flux_slab(vals, u, vel, avg, grad, mask, row_lo, row_hi):
    sy = left(grad, split(vals[0]))
    sz, sx = left_exact(avg, split(vals[1])), left_exact(avg, split(vals[2]))
    lane = lax.broadcasted_iota(jnp.int32, (1, NZL), 1)
    inner = (lane != 0) & (lane != NZL - 1)
    for q, val in enumerate((sx, sy, sz)):
        row_lo(q, jnp.where(inner, val[0:1, :], 0.0))
        row_hi(q, jnp.where(inner, val[NYL - 1 : NYL, :], 0.0))
    nu = eddy(sx, sy, sz) * mask
    return [nu * s - vel[d].astype(F32) * u for d, s in enumerate((sx, sy, sz))]


def setter(ref, x):
    def put(q, val):
        ref[q, x : x + 1, :] = val

    return put


def flux_kernel(
    z1, z2, z3, ulo_ref, uhi_ref, v_ref, avg_ref, dy_ref, fx, fyh, fyl, fzh, fzl, row_lo, row_hi
):
    mask = face_mask()
    row_lo[...] = jnp.zeros_like(row_lo)
    row_hi[...] = jnp.zeros_like(row_hi)
    for x in range(1, NXL - 1):
        u = ulo_ref[x] if x < 8 else uhi_ref[x - 8]
        f = flux_slab(
            [z1[x], z2[x], z3[x]], u, [v_ref[d, x] for d in range(3)], avg_ref[...], dy_ref[...], mask,
            setter(row_lo, x), setter(row_hi, x),
        )
        fx[x - 1] = f[0]
        fyh[x - 1], fyl[x - 1] = split(f[1])
        fzh[x - 1], fzl[x - 1] = split(f[2])


def residue_kernel(
    fx, fyh, fyl, fzh, fzl, row_lo, row_hi, z1, z2, z3, z4, dlt, ulo_ref, uhi_ref, v_ref,
    avg_ref, dy_ref, ry_ref, rz_ref, r_ref, out_lo, out_hi, edge,
):
    out_lo[0:3] = row_lo[...]
    out_hi[0:3] = row_hi[...]
    mask = face_mask()
    ends = []
    for s, x in ((0, 0), (1, NXL - 1)):
        vals = [ref[x] + dlt[s, q] for q, ref in enumerate((z1, z2, z3))]
        f = flux_slab(
            vals, ulo_ref[0] if s == 0 else uhi_ref[7], [v_ref[d, x] for d in range(3)],
            avg_ref[...], dy_ref[...], mask, setter(out_lo, x), setter(out_hi, x),
        )
        edge[s] = f[0]
        ends.append([split(f[1]), split(f[2])])
    for t in range(TILES):
        rows = slice(t * 8, t * 8 + 8)
        nodes = [edge[0, rows, :]] + [fx[k, rows, :] for k in range(NXL - 2)] + [edge[1, rows, :]]
        for e in range(2):
            for k, val in enumerate(even_odd(DR, nodes[8 * e : 8 * e + 8], -1)):
                r_ref[8 * e + k, rows, :] = val
    face = LY.face
    rz = rz_ref[...]
    groups = [(0, NXL - 1)] + [tuple(range(1 + 7 * c, 8 + 7 * c)) for c in range(2)]
    for group in groups:
        if 0 in group:
            pair = [jnp.concatenate([ends[0][1][i], ends[1][1][i]], axis=0) for i in range(2)]
        else:
            xs = slice(group[0] - 1, group[-1])
            pair = [ref[xs].reshape(len(group) * NYL, NZL) for ref in (fzh, fzl)]
        along_z = right(pair, rz)
        for i, x in enumerate(group):
            ypair = ends[i][0] if 0 in group else (fyh[x - 1], fyl[x - 1])
            r_ref[x] = r_ref[x] + (left(ry_ref[...], ypair) + along_z[i * NYL : (i + 1) * NYL])
    for x in range(NXL):
        one = slice(x, x + 1)
        out_lo[3, one, :] = r_ref[x, 0:1, :]
        out_hi[3, one, :] = r_ref[x, NYL - 1 : NYL, :]
        out_lo[4, one, :] = row_sum(r_ref[x, 0:16, :], face[0, 0:16])
        out_hi[4, one, :] = row_sum(r_ref[x, NYL - 16 : NYL, :], face[-1, NYL - 16 :])
        out_lo[5, one, :] = row_sum(z4[x, 0:8, :], 0.5 * FM[0])
        out_hi[5, one, :] = row_sum(z4[x, NYL - 8 : NYL, :], 0.5 * FM[7])


def z_columns_x():
    mat = np.zeros((128, 128))
    for side in range(2):
        mat[side:32:2, side:32:2] = LX.res.T
    return mat


def z_face_vectors():
    mat = np.zeros((128, NZL))
    for x in range(NXL):
        for side, node in ((0, NZL - 1), (1, 0)):
            mat[2 * x + side, node] = 1.0
            mat[32 + 2 * x + side] = LZ.res[:, node]
    return mat


def y_rows():
    rows = np.zeros((8, NYL))
    rows[0], rows[1] = LY.face[0], LY.face[-1]
    rows[2, 0:8], rows[3, NYL - 8 :] = 0.5 * FM[0], 0.5 * FM[7]
    return rows


def face_y_kernel(
    near, far, cols, lo_ref, hi_ref, avg_ref, dy_ref, ry_ref, rx_ref, zv_ref, yr_ref,
    out_lo, out_hi, cval, halo_ref,
):
    lane = lane_iota(NYL)
    halo = halo_columns(near, far)
    halo_ref[...] = halo
    pair = split(cols[...] + halo)
    sy = left(dy_ref[...], pair)
    avg = left_exact(avg_ref[...], pair)
    sz, sx = pltpu.roll(avg, 96, 1), pltpu.roll(avg, 64, 1)
    row = lax.broadcasted_iota(jnp.int32, (NYL, 128), 0)
    keep = (lane < 32) & (row != 0) & (row != NYL - 1)
    nu = jnp.where(keep, eddy(sx, sy, sz), 0.0)
    tau = right(split(nu * sx), rx_ref[...]) + left(ry_ref[...], split(nu * sy))
    val = tau + pltpu.roll(nu * sz, 32, 1)
    cval[...] = val
    rows = left(yr_ref[...], split(jnp.concatenate([val, pltpu.roll(halo, 32, 1)], axis=1)))
    lane16 = lane_iota(NXL)
    row16 = lax.broadcasted_iota(jnp.int32, (NXL, 128), 0)
    diag = ((lane16 % 32) // 2) == row16
    short, long = diag & (lane16 < 32), diag & (lane16 < 64)
    parts_ = []
    for s, r in ((0, 0), (1, NYL - 1)):
        one = slice(r, r + 1)
        for vec, keep in (
            (sx[one], short), (sy[one], short), (sz[one], short), (val[one], long),
            (rows[s : s + 1, 0:128], long), (rows[2 + s : 3 + s, 128:256], short),
        ):
            parts_.append(jnp.where(keep, jnp.broadcast_to(vec, (NXL, 128)), 0.0))
    add = right(split(jnp.concatenate(parts_, axis=0)), zv_ref[...])
    for q in range(6):
        out_lo[q] = lo_ref[q] + add[16 * q : 16 * q + 16]
        out_hi[q] = hi_ref[q] + add[96 + 16 * q : 112 + 16 * q]


def place(pay, x, lane):
    keep = ((lane % 32) // 2) == x
    return jnp.where(keep, pltpu.roll(pay, 2 * x, 1) if x else pay, 0.0)


def filter_kernel(r_ref, cval, ty_ref, pay_ref, zc_ref, r1, cols, cout):
    lane = lane_iota(NYL)
    acc = None
    for c in range(4):
        for x in range(4 * c, 4 * c + 4):
            r1[x] = left(ty_ref[...], split(r_ref[x]))
        val = r1[4 * c : 4 * c + 4].reshape(4 * NYL, NZL)
        out = right(split(val), pay_ref[...])
        for k in range(4):
            piece = place(out[k * NYL : (k + 1) * NYL], 4 * c + k, lane)
            acc = piece if acc is None else acc + piece
    val = left(ty_ref[...], split(cval[...]))
    cout[...] = val
    cols[...] = acc + right(split(val), zc_ref[...])


def z_columns_z():
    mat = np.zeros((128, 128))
    for x in range(NXL):
        for side, node in ((0, NZL - 1), (1, 0)):
            at = 2 * x + side
            mat[at, at], mat[32 + at, at] = 1.0, LZ.res[node, node]
            mat[at, 32 + at] = LZ.face[node, node]
            mat[32 + at, 32 + at] = LZ.face[node] @ LZ.res[:, node]
    return mat


def y_spread():
    low_t = LY.both[:, 0] + LY.halo[0] + LY.face[-1, -1] * LY.halo[1]
    low_g = (
        LY.both @ LY.res[:, 0] + DR[7, 7] * LY.halo[0] + (LY.face[-1] @ LY.res[:, -1]) * LY.halo[1]
    )
    high_t = LY.both[:, -1] + LY.halo[2] + LY.face[0, 0] * LY.halo[3]
    high_g = (
        LY.both @ LY.res[:, -1] + DR[0, 0] * LY.halo[2] + (LY.face[0] @ LY.res[:, 0]) * LY.halo[3]
    )
    return np.stack(
        [low_t, low_g, LY.halo[0], LY.halo[1], high_t, high_g, LY.halo[2], LY.halo[3]], axis=1
    )


SPREAD = y_spread()


def face_z2_kernel(
    cols_ref, after_ref, own_lo, own_hi, lo_ref, hi_ref, rx_ref, rz_ref, pay_ref, ay_ref, cols, rows_ref
):
    both = ((own_lo, lo_ref), (own_hi, hi_ref))
    flux = []
    for own, ref in both:
        s = [own[q] + ref[q] for q in range(3)]
        nu = eddy(*s)
        flux.append([nu * v for v in s])
    along_x = left(rx_ref[...], split(jnp.concatenate([flux[0][0], flux[1][0]], axis=1)))
    along_z = right(split(jnp.concatenate([flux[0][2], flux[1][2]], axis=0)), rz_ref[...])
    vals = []
    for s, (own, ref) in enumerate(both):
        tau = along_x[:, s * NZL : (s + 1) * NZL] + along_z[s * NXL : (s + 1) * NXL]
        vals += [tau, flux[s][1], ref[3], ref[4]]
    for k, val in enumerate(vals):
        rows_ref[k] = val
    pay = right(split(jnp.concatenate(vals, axis=0)), pay_ref[...])
    lane16 = lane_iota(NXL)
    row16 = lax.broadcasted_iota(jnp.int32, (NXL, 128), 0)
    keep = ((lane16 % 32) // 2) == row16
    vecs = []
    for k in range(8):
        val = pay[16 * k : 16 * k + 16]
        moved = val
        for bit in (1, 2, 4, 8):
            moved = jnp.where((row16 & bit) != 0, pltpu.roll(moved, 2 * bit, 1), moved)
        vec = jnp.sum(jnp.where(keep, moved, 0.0), axis=0, keepdims=True)
        vecs.append(vec)
    for rows, ks in ((slice(0, 24), range(4)), (slice(NYL - 24, NYL), range(4, 8))):
        acc = cols_ref[rows, :]
        for k in ks:
            acc = acc + ay_ref[rows, k : k + 1] * vecs[k]
        cols[rows, :] = acc
    cols[24 : NYL - 24, :] = cols_ref[24 : NYL - 24, :]


def filter_z_kernel(r1, z4, hcols, fy_ref, tz_ref, out, vout):
    lane = lane_iota(NYL)
    for c in range(4):
        xs = slice(4 * c, 4 * c + 4)
        val = r1[xs].reshape(4 * NYL, NZL)
        out[xs] = right(split(val), tz_ref[...]).reshape(4, NYL, NZL)
        for x in range(4 * c, 4 * c + 4):
            rolled = pltpu.roll(hcols[...], (-2 * (48 + x) - 1) % 128, 1)
            field = jnp.concatenate(
                [
                    z4[x, :, 0:128] + jnp.where(lane == 0, rolled, 0.0),
                    z4[x, :, 128:256] + jnp.where(lane == 127, rolled, 0.0),
                ],
                axis=1,
            )
            vout[x] = left(fy_ref[...], split(field))


def spread_kernel(
    r2, vu, rows_ref, lo_ref, hi_ref, cval, ay_ref, tz_ref, mat_ref, out, vout, pay_lo, pay_hi, zr
):
    zr[...] = right(split(rows_ref[...].reshape(8 * NXL, NZL)), tz_ref[...]).reshape(8, NXL, NZL)
    add = right(split(cval[...]), mat_ref[...])
    row8 = lax.broadcasted_iota(jnp.int32, (8, NZL), 0)
    for t in range(TILES):
        rows = slice(t * 8, t * 8 + 8)
        r, w = [], []
        for x in range(NXL):
            one = slice(x, x + 1)
            val, wal = r2[x, rows, :], vu[x, rows, :]
            for k in range(8):
                if np.any(SPREAD[rows, k]):
                    val = val + ay_ref[rows, k : k + 1] * zr[k, one, :]
            if t == 0:
                wal = wal + jnp.where(row8 == 0, lo_ref[5, one, :], 0.0)
            if t == TILES - 1:
                wal = wal + jnp.where(row8 == 7, hi_ref[5, one, :], 0.0)
            out[x, rows, :] = val
            vout[x, rows, :] = wal
            r.append(val)
            w.append(wal)
        a = [s + v for s, v in zip(average_x(r), w)]
        low = sum(float(FM[0, j]) * a[j] for j in range(8))
        high = sum(float(FM[7, j]) * a[8 + j] for j in range(8))
        for q, (ref, val) in enumerate(((pay_lo, r[0]), (pay_lo, low), (pay_hi, r[15]), (pay_hi, high))):
            ref[q % 2, rows, :] = val + add[rows, q * NZL : (q + 1) * NZL]


def z_vectors():
    vecs = [[LZ.halo[0], LZ.halo[2]], [LZ.halo[1], LZ.halo[3]]]
    vecs.append([LZ.both[:, -1], LZ.both[:, 0]])
    vecs.append([LZ.both @ LZ.res[:, -1], LZ.both @ LZ.res[:, 0]])
    return vecs


def z_spread():
    add = np.zeros((128, NZL))
    for q, pair in enumerate(z_vectors()):
        for side in range(2):
            add[32 * q + side] = pair[side]
    return add


def z_to_x():
    out = np.zeros((128, 4 * NZL))
    low, high = LX.face[0], LX.face[-1]
    for x in range(NXL):
        for q, pair in enumerate(z_vectors()[2:]):
            for side in range(2):
                lane, vec = 2 * (16 * q + x) + side, pair[side]
                if x == 0:
                    out[lane, 0:NZL] = vec
                if x == NXL - 1:
                    out[lane, 2 * NZL : 3 * NZL] = vec
                out[lane, NZL : 2 * NZL] = low[x] * vec
                out[lane, 3 * NZL :] = high[x] * vec
    return out


def z_short():
    out = np.zeros((128, 128))
    low, high = LX.face[0], LX.face[-1]
    for x in range(NXL):
        for q in range(2):
            for side in range(2):
                lane, c = 2 * (16 * q + x) + side, 2 * q + side
                if x == 0:
                    out[lane, c] = 1.0
                if x == NXL - 1:
                    out[lane, 8 + c] = 1.0
                out[lane, 4 + c], out[lane, 12 + c] = low[x], high[x]
    return out


def z_long():
    out = np.zeros((16, 4 * NZL))
    for q, pair in enumerate(z_vectors()[:2]):
        for side in range(2):
            for k in range(4):
                out[4 * k + 2 * q + side, k * NZL : (k + 1) * NZL] = pair[side]
    high, low = halves(out)
    rest = np.zeros((80, 4 * NZL)).astype(jnp.bfloat16)
    return jnp.asarray(np.concatenate([high, high, low, rest], axis=0))


def forward_kernel(near, far, cval, mat_ref, flo, fhi, hs):
    low, high = received(near, far)
    lane = lane_iota(NYL)
    halo = jnp.where((lane % 2) == 0, low, high)
    hs[...] = jnp.where(lane < 64, halo, pltpu.roll(cval[...], 64, 1))
    short = right(split(halo), mat_ref[...])
    lane8 = lane_iota(8)
    for ref, base in ((flo, 0), (fhi, 8)):
        acc = None
        for t in range(TILES):
            piece = pltpu.roll(short[8 * t : 8 * t + 8], (8 * t - base) % 128, 1)
            piece = jnp.where((lane8 // 8) == t, piece, 0.0)
            acc = piece if acc is None else acc + piece
        ref[...] = acc


def forwarded(glo, ghi, mat):
    lane8 = lane_iota(8)
    tiles = []
    for t in range(TILES):
        low = pltpu.roll(glo, (-8 * t) % 128, 1)
        high = pltpu.roll(ghi, (8 - 8 * t) % 128, 1)
        tiles.append(jnp.where(lane8 < 8, low, jnp.where(lane8 < 16, high, 0.0)))
    val = jnp.concatenate(tiles, axis=0)
    top = val.astype(BF).astype(F32)
    val = top + pltpu.roll(val - top, 16, 1) + pltpu.roll(top, 32, 1)
    return mm(val.astype(BF), mat)


def local_x_kernel(r2, vu, hs, add_ref, out):
    for t in range(NYL // 16):
        rows = slice(t * 16, t * 16 + 16)
        col = hs[rows, :]
        rolled = [pltpu.roll(col, (-2 * x) % 128, 1) if x else col for x in range(NXL)]
        add = right(split(jnp.concatenate(rolled, axis=0)), add_ref[...])
        r = [r2[x, rows, :] + add[16 * x : 16 * x + 16] for x in range(NXL)]
        a = [s + vu[k, rows, :] for k, s in enumerate(average_x(r))]
        f = average_x(even_odd(FM, a[:8], 1) + even_odd(FM, a[8:], 1))
        f[0] = f[0] + float(0.25 * FM[7, 7]) * r[0]
        f[15] = f[15] + float(0.25 * FM[0, 0]) * r[15]
        for k in range(NXL):
            out[k, rows, :] = f[k]


def final_kernel(val_ref, lo_ref, hi_ref, glo_ref, ghi_ref, mat_ref, out_hbm, buf, sems):
    copies = []
    add = forwarded(glo_ref[...], ghi_ref[...], mat_ref[...])
    for c in range(4):
        for t in range(3):
            rows = slice(c * 24 + t * 8, c * 24 + t * 8 + 8)
            halo = [lo_ref[0, rows, :], lo_ref[1, rows, :], hi_ref[0, rows, :], hi_ref[1, rows, :]]
            halo = [v + add[rows, j * NZL : (j + 1) * NZL] for j, v in enumerate(halo)]
            for k in range(NXL):
                val = val_ref[k, rows, :]
                for j in range(4):
                    if LX.halo[j][k] != 0.0:
                        val = val + float(LX.halo[j][k]) * halo[j]
                buf[k, rows, :] = val
        rows = slice(c * 24, c * 24 + 24)
        copies.append(pltpu.make_async_copy(buf.at[:, rows, :], out_hbm.at[:, rows, :], sems.at[c]))
        copies[-1].start()
    for copy in copies:
        copy.wait()


def shift(val, axis, step):
    count = lax.axis_size(axis)
    return lax.ppermute(val, axis, [(i, (i + step) % count) for i in range(count)])


def exchange(lo, hi, axis):
    return shift(hi, axis, 1), shift(lo, axis, -1)


def swap(val, axis, start):
    count = lax.axis_size(axis)
    pairs = [(k % count, (k + 1) % count) for k in range(start, count + start, 2)]
    return lax.ppermute(val, axis, pairs + [(b, a) for a, b in pairs])


def on_device(u, velocity):
    full = (NXL, NYL, NZL)
    face_x = (2, NYL, NZL)
    face_y = (6, NXL, NZL)
    colshape = (NYL, 128)

    sz, dz = exact_right(LZ.avg.T), on_right(LZ.grad.T)
    sy, dy, fy = exact_left(LY.avg), on_left(LY.grad), on_left(LY.filt)
    ry, rz, rx = on_left(LY.res), on_right(LZ.res.T), on_left(LX.res)
    pay = np.zeros((NZL, 128))
    pay[NZL - 1, 0] = pay[0, 1] = 1.0
    pay[:, 32], pay[:, 33] = LZ.face[-1], LZ.face[0]
    pay = on_right(pay)
    ay = jnp.asarray(SPREAD.astype(np.float32))
    ty, tz = on_left(LY.both), on_right(LZ.both.T)

    ulo, uhi = u[:8], u[8:]
    hi = call(face_hi_kernel, face_x, uhi, name="face_hi")
    xlo = shift(hi, "gx", 1)
    lo = call(face_lo_kernel, face_x, ulo, name="face_lo")
    xhi = shift(lo, "gx", -1)
    z1, z2, z3, z4, cols = call(
        local_z_kernel, [full] * 4 + [colshape], ulo, uhi, sz, on_right(np.concatenate([LZ.grad.T, LZ.filt.T], axis=1)),
        flops=3 * 10**9, nbytes=8 * 10**6, name="local_z",
    )
    inner = (NXL - 2, NYL, NZL)
    flux = call(
        flux_kernel, [inner] + [(inner, BF)] * 4 + [(3, NXL, NZL)] * 2,
        z1, z2, z3, ulo, uhi, velocity, sy, dy, flops=10**9, nbytes=12 * 10**6, name="flux",
    )
    dlt, cols = call(
        face_z_kernel, [(2, 3, NYL, NZL), colshape], xlo, xhi, cols, sz, dz, name="face_z"
    )
    near, far = swap(cols, "gz", 0), swap(cols, "gz", 1)
    r, lo, hi = call(
        residue_kernel, [full, face_y, face_y],
        *flux, z1, z2, z3, z4, dlt, ulo, uhi, velocity, sy, dy, ry, rz,
        scratch=[pltpu.VMEM((2, NYL, NZL), F32)], flops=3 * 10**9, nbytes=12 * 10**6, name="residue",
    )
    lo, hi, cval, hcols = call(
        face_y_kernel, [face_y, face_y, colshape, colshape], near, far, cols, lo, hi, sy, dy, ry,
        on_right(z_columns_x()), on_right(z_face_vectors()), on_left(y_rows()), name="face_y",
    )
    ylo, yhi = exchange(lo, hi, "gy")
    r1, cols, cval = call(
        filter_kernel, [full, colshape, colshape], r, cval, ty, pay, on_right(z_columns_z()),
        flops=2 * 10**9, nbytes=9 * 10**6, name="filter",
    )
    r2, vu = call(
        filter_z_kernel, [full, full], r1, z4, hcols, fy, tz, flops=2 * 10**9, nbytes=9 * 10**6, name="filter_z"
    )
    cols, rows = call(
        face_z2_kernel, [colshape, (8, NXL, NZL)], cols, r2, lo, hi, ylo, yhi, rx, rz, pay, ay,
        name="face_z2",
    )
    near, far = swap(cols, "gz", 0), swap(cols, "gz", 1)
    r2, vu, lo, hi = call(
        spread_kernel, [full, full, face_x, face_x], r2, vu, rows, ylo, yhi, cval, ay, tz, on_right(z_to_x()),
        scratch=[pltpu.VMEM((8, NXL, NZL), F32)], flops=10**9, nbytes=9 * 10**6, name="spread",
    )
    xlo, xhi = exchange(lo, hi, "gx")
    flo, fhi, hs = call(
        forward_kernel, [(8, 128), (8, 128), colshape], near, far, cval, on_right(z_short()), name="forward"
    )
    glo, ghi = exchange(flo, fhi, "gx")
    val = call(
        local_x_kernel, full, r2, vu, hs, on_right(z_spread()),
        flops=10**11, nbytes=10**8, name="local_x",
    )
    return call(
        final_kernel, full, val, xlo, xhi, glo, ghi, z_long(), hbm_out=True,
        scratch=[pltpu.VMEM(full, F32), pltpu.SemaphoreType.DMA((4,))], name="final",
    )


def solution(mesh):
    return jax.shard_map(
        on_device,
        mesh=mesh,
        in_specs=(P("gx", "gy", "gz"), P(None, "gx", "gy", "gz")),
        out_specs=P("gx", "gy", "gz"),
        check_vma=False,
    )
```

```python
import functools

import jax
import jax.numpy as jnp
import numpy as np
from jax import lax
from jax.experimental import pallas as pl
from jax.experimental.pallas import tpu as pltpu
from jax.sharding import PartitionSpec as P

DT = 0.002
NU_BASE = 0.3
SGS_COEF = 0.01
FILTER_STRENGTH = 0.3
GLL_POINTS = [
    -1.0,
    -0.8717401485096066,
    -0.5917001814331423,
    -0.2092992179024789,
    0.2092992179024789,
    0.5917001814331423,
    0.8717401485096066,
    1.0,
]
BF = jnp.bfloat16
F32 = jnp.float32
VM = pl.BlockSpec(memory_space=pltpu.VMEM)


def legendre_all(point):
    values_list = [1.0, point]
    for order in range(1, 7):
        values_list.append(
            ((2 * order + 1) * point * values_list[order] - order * values_list[order - 1])
            / (order + 1)
        )
    return values_list


def gll_tables():
    degree = 7
    table = [legendre_all(p) for p in GLL_POINTS]
    top = [table[i][degree] for i in range(8)]
    weights = [2.0 / (degree * (degree + 1) * top[i] * top[i]) for i in range(8)]
    derivative = [[0.0] * 8 for i in range(8)]
    for i in range(8):
        for j in range(8):
            if i != j:
                derivative[i][j] = top[i] / (top[j] * (GLL_POINTS[i] - GLL_POINTS[j]))
    derivative[0][0] = -degree * (degree + 1) / 4.0
    derivative[7][7] = degree * (degree + 1) / 4.0
    damping = [1.0] * 8
    for k in (6, 7):
        damping[k] = 1.0 - FILTER_STRENGTH * ((k - 5) / 2.0) ** 2
    gammas = [2.0 / (2 * k + 1) for k in range(7)] + [2.0 / degree]
    filter_mat = [[0.0] * 8 for i in range(8)]
    for i in range(8):
        for j in range(8):
            total = 0.0
            for k in range(8):
                total += table[i][k] * damping[k] * weights[j] * table[j][k] / gammas[k]
            filter_mat[i][j] = total
    return np.array(derivative), np.array(weights), np.array(filter_mat)


D, WT, FM = gll_tables()
DR = -DT * (D.T * WT[None, :]) / WT[:, None]


def block(mat, length):
    return np.kron(np.eye(length // 8), mat)


def average(length):
    mat = np.eye(length)
    for k in range(8, length, 8):
        mat[k - 1 : k + 1, k - 1 : k + 1] = 0.5
    mat[0, 0] = mat[-1, -1] = 0.5
    return mat


class Line:
    def __init__(self, length):
        avg = average(length)
        filt = block(FM, length)
        self.avg = avg
        self.grad = avg @ block(D, length)
        self.res = block(DR, length)
        self.filt = avg @ filt
        self.both = avg @ filt @ avg
        self.both[0, 0] += 0.25 * FM[7, 7]
        self.both[-1, -1] += 0.25 * FM[0, 0]
        self.face = filt @ avg
        first, last = np.eye(length)[0], np.eye(length)[-1]
        self.halo = np.stack([self.filt[:, 0] * 0.5, 0.5 * first, self.filt[:, -1] * 0.5, 0.5 * last])


def halves(mat):
    mat = np.asarray(mat, np.float64)
    high = mat.astype(jnp.bfloat16)
    low = (mat - high.astype(np.float64)).astype(jnp.bfloat16)
    return high, low


def on_right(mat):
    high, low = halves(mat)
    return jnp.asarray(np.concatenate([high, high, low], axis=0))


def on_left(mat):
    high, low = halves(mat)
    return jnp.asarray(np.concatenate([high, high, low], axis=1))


def exact_right(mat):
    mat = np.asarray(mat).astype(jnp.bfloat16)
    return jnp.asarray(np.concatenate([mat, mat], axis=0))


def exact_left(mat):
    mat = np.asarray(mat).astype(jnp.bfloat16)
    return jnp.asarray(np.concatenate([mat, mat], axis=1))


def split(val):
    high = val.astype(BF)
    return high, (val - high.astype(F32)).astype(BF)


def mm(a, b):
    return jnp.dot(a, b, preferred_element_type=F32)


def right(pair, mat):
    return mm(jnp.concatenate([pair[0], pair[1], pair[0]], axis=1), mat)


def right_exact(pair, mat):
    return mm(jnp.concatenate(pair, axis=1), mat)


def left(mat, pair):
    return mm(mat, jnp.concatenate([pair[0], pair[1], pair[0]], axis=0))


def left_exact(mat, pair):
    return mm(mat, jnp.concatenate(pair, axis=0))


def call(kernel, outs, *args, scratch=(), flops=0, nbytes=0, name=None, hbm=(), hbm_out=False, smem=(), limit=6 << 20):
    single = not isinstance(outs, list)
    place_at = pltpu.HBM if hbm_out else pltpu.VMEM
    pairs = [o if isinstance(o[0], tuple) else (o, F32) for o in ([outs] if single else outs)]
    shapes = [place_at(shape, dtype) for shape, dtype in pairs]
    kinds = {i: pl.BlockSpec(memory_space=pltpu.HBM) for i in hbm}
    kinds.update({i: pl.BlockSpec(memory_space=pltpu.SMEM) for i in smem})
    res = pl.pallas_call(
        kernel,
        out_shape=shapes,
        in_specs=[kinds.get(i, VM) for i in range(len(args))],
        out_specs=[pl.BlockSpec(memory_space=pltpu.HBM) if hbm_out else VM] * len(shapes),
        scratch_shapes=list(scratch),
        compiler_params=pltpu.CompilerParams(vmem_limit_bytes=limit),
        cost_estimate=pl.CostEstimate(flops=flops, bytes_accessed=nbytes, transcendentals=0),
        name=name,
    )(*args)
    return res[0] if single else res


NXL, NYL, NZL = 16, 96, 256
ROWS = NXL * NYL
TILES = NYL // 8


LX, LY, LZ = Line(NXL), Line(NYL), Line(NZL)


def face_hi_kernel(u_hbm, hi_ref, u_ref, sems):
    copies = []
    for c in range(4):
        rows = slice(c * 24, c * 24 + 24)
        copies.append(pltpu.make_async_copy(u_hbm.at[8:16, rows, :], u_ref.at[:, rows, :], sems.at[c]))
        copies[-1].start()
    for t in range(TILES):
        if t % 3 == 0:
            copies[t // 3].wait()
        rows = slice(t * 8, t * 8 + 8)
        hi_ref[0, rows, :] = 0.5 * u_ref[7, rows, :]
        hi_ref[1, rows, :] = sum(float(0.5 * D[7, j]) * u_ref[j, rows, :] for j in range(8))


def face_lo_kernel(u_ref, lo_ref):
    for t in range(TILES):
        rows = slice(t * 8, t * 8 + 8)
        lo_ref[0, rows, :] = 0.5 * u_ref[0, rows, :]
        lo_ref[1, rows, :] = sum(float(0.5 * D[0, j]) * u_ref[j, rows, :] for j in range(8))


def even_odd(mat, nodes, sign):
    even = [nodes[j] + nodes[7 - j] for j in range(4)]
    odd = [nodes[j] - nodes[7 - j] for j in range(4)]
    out = [None] * 8
    for i in range(4):
        a = sum(float(0.5 * (mat[i, j] + mat[i, 7 - j])) * even[j] for j in range(4))
        b = sum(float(0.5 * (mat[i, j] - mat[i, 7 - j])) * odd[j] for j in range(4))
        out[i] = a + b
        out[7 - i] = (a - b) if sign > 0 else (b - a)
    return out


def average_x(vals):
    vals = list(vals)
    mid = 0.5 * (vals[7] + vals[8])
    vals[7] = vals[8] = mid
    vals[0] = 0.5 * vals[0]
    vals[15] = 0.5 * vals[15]
    return vals


def lane_iota(rows):
    return lax.broadcasted_iota(jnp.int32, (rows, 128), 1)


def pack_columns(fields, x, lane):
    total = None
    for q, field in enumerate(fields):
        ends = jnp.where(lane == 127, field[:, 128:256], field[:, 0:128])
        pos = 2 * (16 * q + x)
        rolled = pltpu.roll(ends, (pos - 127) % 128, 1)
        piece = jnp.where((lane == pos) | (lane == pos + 1), rolled, 0.0)
        total = piece if total is None else total + piece
    return total


def received(near_ref, far_ref):
    first = lax.rem(lax.axis_index("gz"), 2) == 0
    near, far = near_ref[...], far_ref[...]
    return jnp.where(first, far, near), jnp.where(first, near, far)


def halo_columns(near_ref, far_ref):
    low, high = received(near_ref, far_ref)
    return jnp.where((lane_iota(NYL) % 2) == 0, pltpu.roll(high, 127, 1), pltpu.roll(low, 1, 1))


def local_z_kernel(u_ref, sz_ref, dfz_ref, z1, z2, z3, z4, cols):
    lane = lane_iota(16)
    for t in range(NYL // 16):
        rows = slice(t * 16, t * 16 + 16)
        p = split(jnp.concatenate([u_ref[k, rows, :] for k in range(NXL)], axis=0))
        slabs = lambda val: [val[16 * k : 16 * k + 16] for k in range(NXL)]
        avg = slabs(right_exact(p, sz_ref[...]))
        both = right(p, dfz_ref[...])
        grads = even_odd(D, avg[:8], -1) + even_odd(D, avg[8:], -1)
        outs = [
            average_x(avg),
            average_x(slabs(both[:, 0:NZL])),
            average_x(grads),
            slabs(both[:, NZL:]),
        ]
        acc = None
        for k in range(NXL):
            vals = [o[k] for o in outs]
            for ref, val in zip((z1, z2, z3, z4), vals):
                ref[k, rows, :] = val
            piece = pack_columns(vals, k, lane)
            acc = piece if acc is None else acc + piece
        cols[rows, :] = acc


def face_z_kernel(lo_ref, hi_ref, cols_ref, sz_ref, dz_ref, dlt, cols):
    p = split(jnp.concatenate([lo_ref[0], hi_ref[0]], axis=0))
    g = split(jnp.concatenate([lo_ref[1], hi_ref[1]], axis=0))
    outs = [right_exact(p, sz_ref[...]), right(p, dz_ref[...]), right_exact(g, sz_ref[...])]
    lane = lane_iota(NYL)
    acc = cols_ref[...]
    for s, x in ((0, 0), (1, NXL - 1)):
        vals = [o[s * NYL : (s + 1) * NYL] for o in outs]
        for q in range(3):
            dlt[s, q] = vals[q]
        acc = acc + pack_columns(vals, x, lane)
    cols[...] = acc


def row_sum(vals, coefs):
    row = lax.broadcasted_iota(jnp.int32, vals.shape, 0)
    weight = jnp.zeros(vals.shape, F32)
    for k, c in enumerate(coefs):
        weight = jnp.where(row == k, float(c), weight)
    return jnp.sum(vals * weight, axis=0, keepdims=True)


def eddy(sx, sy, sz):
    mag = 1.0 + sx * sx + sy * sy + sz * sz
    return NU_BASE + SGS_COEF * (mag * lax.rsqrt(mag))


def face_mask():
    row = lax.broadcasted_iota(jnp.int32, (NYL, NZL), 0)
    lane = lax.broadcasted_iota(jnp.int32, (NYL, NZL), 1)
    inner = (lane != 0) & (lane != NZL - 1) & (row != 0) & (row != NYL - 1)
    return inner.astype(F32)


def flux_slab(vals, u, vel, avg, grad, mask, row_lo, row_hi):
    sy = left(grad, split(vals[0]))
    sz, sx = left_exact(avg, split(vals[1])), left_exact(avg, split(vals[2]))
    lane = lax.broadcasted_iota(jnp.int32, (1, NZL), 1)
    inner = (lane != 0) & (lane != NZL - 1)
    for q, val in enumerate((sx, sy, sz)):
        row_lo(q, jnp.where(inner, val[0:1, :], 0.0))
        row_hi(q, jnp.where(inner, val[NYL - 1 : NYL, :], 0.0))
    nu = eddy(sx, sy, sz) * mask
    return [nu * s - vel[d].astype(F32) * u for d, s in enumerate((sx, sy, sz))]


def setter(ref, x):
    def put(q, val):
        ref[q, x : x + 1, :] = val

    return put


def flux_kernel(
    z1, z2, z3, u_ref, v_ref, avg_ref, dy_ref, fx, fyh, fyl, fzh, fzl, row_lo, row_hi
):
    mask = face_mask()
    row_lo[...] = jnp.zeros_like(row_lo)
    row_hi[...] = jnp.zeros_like(row_hi)
    for x in range(1, NXL - 1):
        u = u_ref[x]
        f = flux_slab(
            [z1[x], z2[x], z3[x]], u, [v_ref[d, x] for d in range(3)], avg_ref[...], dy_ref[...], mask,
            setter(row_lo, x), setter(row_hi, x),
        )
        fx[x - 1] = f[0]
        fyh[x - 1], fyl[x - 1] = split(f[1])
        fzh[x - 1], fzl[x - 1] = split(f[2])


def residue_kernel(
    fx, fyh, fyl, fzh, fzl, row_lo, row_hi, z1, z2, z3, z4, dlt, u_ref, v_ref,
    avg_ref, dy_ref, ry_ref, rz_ref, r_ref, out_lo, out_hi, edge,
):
    out_lo[0:3] = row_lo[...]
    out_hi[0:3] = row_hi[...]
    mask = face_mask()
    ends = []
    for s, x in ((0, 0), (1, NXL - 1)):
        vals = [ref[x] + dlt[s, q] for q, ref in enumerate((z1, z2, z3))]
        f = flux_slab(
            vals, u_ref[x], [v_ref[d, x] for d in range(3)],
            avg_ref[...], dy_ref[...], mask, setter(out_lo, x), setter(out_hi, x),
        )
        edge[s] = f[0]
        ends.append([split(f[1]), split(f[2])])
    for t in range(TILES):
        rows = slice(t * 8, t * 8 + 8)
        nodes = [edge[0, rows, :]] + [fx[k, rows, :] for k in range(NXL - 2)] + [edge[1, rows, :]]
        for e in range(2):
            for k, val in enumerate(even_odd(DR, nodes[8 * e : 8 * e + 8], -1)):
                r_ref[8 * e + k, rows, :] = val
    face = LY.face
    rz = rz_ref[...]
    groups = [(0, NXL - 1)] + [tuple(range(1 + 7 * c, 8 + 7 * c)) for c in range(2)]
    for group in groups:
        if 0 in group:
            pair = [jnp.concatenate([ends[0][1][i], ends[1][1][i]], axis=0) for i in range(2)]
        else:
            xs = slice(group[0] - 1, group[-1])
            pair = [ref[xs].reshape(len(group) * NYL, NZL) for ref in (fzh, fzl)]
        along_z = right(pair, rz)
        for i, x in enumerate(group):
            ypair = ends[i][0] if 0 in group else (fyh[x - 1], fyl[x - 1])
            r_ref[x] = r_ref[x] + (left(ry_ref[...], ypair) + along_z[i * NYL : (i + 1) * NYL])
    for x in range(NXL):
        one = slice(x, x + 1)
        out_lo[3, one, :] = r_ref[x, 0:1, :]
        out_hi[3, one, :] = r_ref[x, NYL - 1 : NYL, :]
        out_lo[4, one, :] = row_sum(r_ref[x, 0:16, :], face[0, 0:16])
        out_hi[4, one, :] = row_sum(r_ref[x, NYL - 16 : NYL, :], face[-1, NYL - 16 :])
        out_lo[5, one, :] = row_sum(z4[x, 0:8, :], 0.5 * FM[0])
        out_hi[5, one, :] = row_sum(z4[x, NYL - 8 : NYL, :], 0.5 * FM[7])


def z_columns_x():
    mat = np.zeros((128, 128))
    for side in range(2):
        mat[side:32:2, side:32:2] = LX.res.T
    return mat


def z_face_vectors():
    mat = np.zeros((128, NZL))
    for x in range(NXL):
        for side, node in ((0, NZL - 1), (1, 0)):
            mat[2 * x + side, node] = 1.0
            mat[32 + 2 * x + side] = LZ.res[:, node]
    return mat


def y_rows():
    rows = np.zeros((8, NYL))
    rows[0], rows[1] = LY.face[0], LY.face[-1]
    rows[2, 0:8], rows[3, NYL - 8 :] = 0.5 * FM[0], 0.5 * FM[7]
    return rows


def face_y_kernel(
    near, far, cols, lo_ref, hi_ref, avg_ref, dy_ref, ry_ref, rx_ref, zv_ref, yr_ref,
    out_lo, out_hi, cval, halo_ref,
):
    lane = lane_iota(NYL)
    halo = halo_columns(near, far)
    halo_ref[...] = halo
    pair = split(cols[...] + halo)
    sy = left(dy_ref[...], pair)
    avg = left_exact(avg_ref[...], pair)
    sz, sx = pltpu.roll(avg, 96, 1), pltpu.roll(avg, 64, 1)
    row = lax.broadcasted_iota(jnp.int32, (NYL, 128), 0)
    keep = (lane < 32) & (row != 0) & (row != NYL - 1)
    nu = jnp.where(keep, eddy(sx, sy, sz), 0.0)
    tau = right(split(nu * sx), rx_ref[...]) + left(ry_ref[...], split(nu * sy))
    val = tau + pltpu.roll(nu * sz, 32, 1)
    cval[...] = val
    rows = left(yr_ref[...], split(jnp.concatenate([val, pltpu.roll(halo, 32, 1)], axis=1)))
    lane16 = lane_iota(NXL)
    row16 = lax.broadcasted_iota(jnp.int32, (NXL, 128), 0)
    diag = ((lane16 % 32) // 2) == row16
    short, long = diag & (lane16 < 32), diag & (lane16 < 64)
    parts_ = []
    for s, r in ((0, 0), (1, NYL - 1)):
        one = slice(r, r + 1)
        for vec, keep in (
            (sx[one], short), (sy[one], short), (sz[one], short), (val[one], long),
            (rows[s : s + 1, 0:128], long), (rows[2 + s : 3 + s, 128:256], short),
        ):
            parts_.append(jnp.where(keep, jnp.broadcast_to(vec, (NXL, 128)), 0.0))
    add = right(split(jnp.concatenate(parts_, axis=0)), zv_ref[...])
    for q in range(6):
        out_lo[q] = lo_ref[q] + add[16 * q : 16 * q + 16]
        out_hi[q] = hi_ref[q] + add[96 + 16 * q : 112 + 16 * q]


def place(pay, x, lane):
    return jnp.where(((lane % 32) // 2) == x, pay, 0.0)


def filter_kernel(r_ref, cval, z4, hcols, ty_ref, fy_ref, tp_ref, zc_ref, r2, vu, cols, cout):
    lane = lane_iota(NYL)
    acc = None
    for c in range(4):
        xs = range(4 * c, 4 * c + 4)
        val = jnp.concatenate([left(ty_ref[...], split(r_ref[x])) for x in xs], axis=0)
        out = right(split(val), tp_ref[...])
        for k, x in enumerate(xs):
            part = out[k * NYL : (k + 1) * NYL]
            r2[x] = part[:, 0:NZL]
            piece = place(part[:, NZL:], x, lane)
            acc = piece if acc is None else acc + piece
            rolled = pltpu.roll(hcols[...], (-2 * (48 + x) - 1) % 128, 1)
            field = jnp.concatenate(
                [
                    z4[x, :, 0:128] + jnp.where(lane == 0, rolled, 0.0),
                    z4[x, :, 128:256] + jnp.where(lane == 127, rolled, 0.0),
                ],
                axis=1,
            )
            vu[x] = left(fy_ref[...], split(field))
    val = left(ty_ref[...], split(cval[...]))
    cout[...] = val
    cols[...] = acc + right(split(val), zc_ref[...])


def z_columns_z():
    mat = np.zeros((128, 128))
    for x in range(NXL):
        for side, node in ((0, NZL - 1), (1, 0)):
            at = 2 * x + side
            mat[at, at], mat[32 + at, at] = 1.0, LZ.res[node, node]
            mat[at, 32 + at] = LZ.face[node, node]
            mat[32 + at, 32 + at] = LZ.face[node] @ LZ.res[:, node]
    return mat


def y_spread():
    low_t = LY.both[:, 0] + LY.halo[0] + LY.face[-1, -1] * LY.halo[1]
    low_g = (
        LY.both @ LY.res[:, 0] + DR[7, 7] * LY.halo[0] + (LY.face[-1] @ LY.res[:, -1]) * LY.halo[1]
    )
    high_t = LY.both[:, -1] + LY.halo[2] + LY.face[0, 0] * LY.halo[3]
    high_g = (
        LY.both @ LY.res[:, -1] + DR[0, 0] * LY.halo[2] + (LY.face[0] @ LY.res[:, 0]) * LY.halo[3]
    )
    return np.stack(
        [low_t, low_g, LY.halo[0], LY.halo[1], high_t, high_g, LY.halo[2], LY.halo[3]], axis=1
    )


SPREAD = y_spread()


def face_z2_kernel(
    cols_ref, after_ref, own_lo, own_hi, lo_ref, hi_ref, rx_ref, rz_ref, pay_ref, ay_ref, cols, rows_ref
):
    both = ((own_lo, lo_ref), (own_hi, hi_ref))
    flux = []
    for own, ref in both:
        s = [own[q] + ref[q] for q in range(3)]
        nu = eddy(*s)
        flux.append([nu * v for v in s])
    along_x = left(rx_ref[...], split(jnp.concatenate([flux[0][0], flux[1][0]], axis=1)))
    along_z = right(split(jnp.concatenate([flux[0][2], flux[1][2]], axis=0)), rz_ref[...])
    vals = []
    for s, (own, ref) in enumerate(both):
        tau = along_x[:, s * NZL : (s + 1) * NZL] + along_z[s * NXL : (s + 1) * NXL]
        vals += [tau, flux[s][1], ref[3], ref[4]]
    for k, val in enumerate(vals):
        rows_ref[k] = val
    pay = right(split(jnp.concatenate(vals, axis=0)), pay_ref[...])
    lane16 = lane_iota(NXL)
    row16 = lax.broadcasted_iota(jnp.int32, (NXL, 128), 0)
    keep = ((lane16 % 32) // 2) == row16
    vecs = []
    for k in range(8):
        val = pay[16 * k : 16 * k + 16]
        vec = jnp.sum(jnp.where(keep, val, 0.0), axis=0, keepdims=True)
        vecs.append(vec)
    for rows, ks in ((slice(0, 24), range(4)), (slice(NYL - 24, NYL), range(4, 8))):
        acc = cols_ref[rows, :]
        for k in ks:
            acc = acc + ay_ref[rows, k : k + 1] * vecs[k]
        cols[rows, :] = acc
    cols[24 : NYL - 24, :] = cols_ref[24 : NYL - 24, :]


def spread_kernel(
    r2, vu, rows_ref, lo_ref, hi_ref, cval, ay_ref, tz_ref, mat_ref, out, vout, pay_lo, pay_hi, zr
):
    zr[...] = right(split(rows_ref[...].reshape(8 * NXL, NZL)), tz_ref[...]).reshape(8, NXL, NZL)
    add = right(split(cval[...]), mat_ref[...])
    row8 = lax.broadcasted_iota(jnp.int32, (8, NZL), 0)
    for t in range(TILES):
        rows = slice(t * 8, t * 8 + 8)
        r, w = [], []
        for x in range(NXL):
            one = slice(x, x + 1)
            val, wal = r2[x, rows, :], vu[x, rows, :]
            for k in range(8):
                if np.any(SPREAD[rows, k]):
                    val = val + ay_ref[rows, k : k + 1] * zr[k, one, :]
            if t == 0:
                wal = wal + jnp.where(row8 == 0, lo_ref[5, one, :], 0.0)
            if t == TILES - 1:
                wal = wal + jnp.where(row8 == 7, hi_ref[5, one, :], 0.0)
            out[x, rows, :] = val
            vout[x, rows, :] = wal
            r.append(val)
            w.append(wal)
        a = [s + v for s, v in zip(average_x(r), w)]
        low = sum(float(FM[0, j]) * a[j] for j in range(8))
        high = sum(float(FM[7, j]) * a[8 + j] for j in range(8))
        for q, (ref, val) in enumerate(((pay_lo, r[0]), (pay_lo, low), (pay_hi, r[15]), (pay_hi, high))):
            ref[q % 2, rows, :] = val + add[rows, q * NZL : (q + 1) * NZL]


def z_vectors():
    vecs = [[LZ.halo[0], LZ.halo[2]], [LZ.halo[1], LZ.halo[3]]]
    vecs.append([LZ.both[:, -1], LZ.both[:, 0]])
    vecs.append([LZ.both @ LZ.res[:, -1], LZ.both @ LZ.res[:, 0]])
    return vecs


def z_spread():
    add = np.zeros((128, NZL))
    for q, pair in enumerate(z_vectors()):
        for side in range(2):
            add[32 * q + side] = pair[side]
    return add


def z_to_x():
    out = np.zeros((128, 4 * NZL))
    low, high = LX.face[0], LX.face[-1]
    for x in range(NXL):
        for q, pair in enumerate(z_vectors()[2:]):
            for side in range(2):
                lane, vec = 2 * (16 * q + x) + side, pair[side]
                if x == 0:
                    out[lane, 0:NZL] = vec
                if x == NXL - 1:
                    out[lane, 2 * NZL : 3 * NZL] = vec
                out[lane, NZL : 2 * NZL] = low[x] * vec
                out[lane, 3 * NZL :] = high[x] * vec
    return out


def z_short():
    out = np.zeros((128, 128))
    low, high = LX.face[0], LX.face[-1]
    for x in range(NXL):
        for q in range(2):
            for side in range(2):
                lane, c = 2 * (16 * q + x) + side, 2 * q + side
                if x == 0:
                    out[lane, c] = 1.0
                if x == NXL - 1:
                    out[lane, 8 + c] = 1.0
                out[lane, 4 + c], out[lane, 12 + c] = low[x], high[x]
    return out


def z_long():
    out = np.zeros((16, 4 * NZL))
    for q, pair in enumerate(z_vectors()[:2]):
        for side in range(2):
            for k in range(4):
                out[4 * k + 2 * q + side, k * NZL : (k + 1) * NZL] = pair[side]
    high, low = halves(out)
    rest = np.zeros((80, 4 * NZL)).astype(jnp.bfloat16)
    return jnp.asarray(np.concatenate([high, high, low, rest], axis=0))


def forward_kernel(near, far, cval, mat_ref, flo, fhi, hs):
    low, high = received(near, far)
    lane = lane_iota(NYL)
    halo = jnp.where((lane % 2) == 0, low, high)
    hs[...] = jnp.where(lane < 64, halo, pltpu.roll(cval[...], 64, 1))
    short = right(split(halo), mat_ref[...])
    lane8 = lane_iota(8)
    for ref, base in ((flo, 0), (fhi, 8)):
        acc = None
        for t in range(TILES):
            piece = pltpu.roll(short[8 * t : 8 * t + 8], (8 * t - base) % 128, 1)
            piece = jnp.where((lane8 // 8) == t, piece, 0.0)
            acc = piece if acc is None else acc + piece
        ref[...] = acc


def forwarded(glo, ghi, mat):
    lane8 = lane_iota(8)
    tiles = []
    for t in range(TILES):
        low = pltpu.roll(glo, (-8 * t) % 128, 1)
        high = pltpu.roll(ghi, (8 - 8 * t) % 128, 1)
        tiles.append(jnp.where(lane8 < 8, low, jnp.where(lane8 < 16, high, 0.0)))
    val = jnp.concatenate(tiles, axis=0)
    top = val.astype(BF).astype(F32)
    val = top + pltpu.roll(val - top, 16, 1) + pltpu.roll(top, 32, 1)
    return mm(val.astype(BF), mat)


def local_x_kernel(r2, vu, hs, add_ref, out):
    for t in range(NYL // 16):
        rows = slice(t * 16, t * 16 + 16)
        col = hs[rows, :]
        rolled = [pltpu.roll(col, (-2 * x) % 128, 1) if x else col for x in range(NXL)]
        add = right(split(jnp.concatenate(rolled, axis=0)), add_ref[...])
        r = [r2[x, rows, :] + add[16 * x : 16 * x + 16] for x in range(NXL)]
        a = [s + vu[k, rows, :] for k, s in enumerate(average_x(r))]
        f = average_x(even_odd(FM, a[:8], 1) + even_odd(FM, a[8:], 1))
        f[0] = f[0] + float(0.25 * FM[7, 7]) * r[0]
        f[15] = f[15] + float(0.25 * FM[0, 0]) * r[15]
        for k in range(NXL):
            out[k, rows, :] = f[k]


def final_kernel(val_ref, lo_ref, hi_ref, glo_ref, ghi_ref, mat_ref, out_hbm, buf, sems):
    copies = []
    add = forwarded(glo_ref[...], ghi_ref[...], mat_ref[...])
    for c in range(4):
        for t in range(3):
            rows = slice(c * 24 + t * 8, c * 24 + t * 8 + 8)
            halo = [lo_ref[0, rows, :], lo_ref[1, rows, :], hi_ref[0, rows, :], hi_ref[1, rows, :]]
            halo = [v + add[rows, j * NZL : (j + 1) * NZL] for j, v in enumerate(halo)]
            for k in range(NXL):
                val = val_ref[k, rows, :]
                for j in range(4):
                    if LX.halo[j][k] != 0.0:
                        val = val + float(LX.halo[j][k]) * halo[j]
                buf[k, rows, :] = val
        rows = slice(c * 24, c * 24 + 24)
        copies.append(pltpu.make_async_copy(buf.at[:, rows, :], out_hbm.at[:, rows, :], sems.at[c]))
        copies[-1].start()
    for copy in copies:
        copy.wait()


def shift(val, axis, step):
    count = lax.axis_size(axis)
    return lax.ppermute(val, axis, [(i, (i + step) % count) for i in range(count)])


def exchange(lo, hi, axis):
    return shift(hi, axis, 1), shift(lo, axis, -1)


def swap(val, axis, start):
    count = lax.axis_size(axis)
    pairs = [(k % count, (k + 1) % count) for k in range(start, count + start, 2)]
    return lax.ppermute(val, axis, pairs + [(b, a) for a, b in pairs])


def on_device(u, velocity):
    full = (NXL, NYL, NZL)
    face_x = (2, NYL, NZL)
    face_y = (6, NXL, NZL)
    colshape = (NYL, 128)

    sz, dz = exact_right(LZ.avg.T), on_right(LZ.grad.T)
    sy, dy, fy = exact_left(LY.avg), on_left(LY.grad), on_left(LY.filt)
    ry, rz, rx = on_left(LY.res), on_right(LZ.res.T), on_left(LX.res)
    pay = np.zeros((NZL, 128))
    pay[NZL - 1, 0:32:2] = pay[0, 1:32:2] = 1.0
    pay[:, 32:64:2], pay[:, 33:64:2] = LZ.face[-1][:, None], LZ.face[0][:, None]
    pay_mat = pay
    pay = on_right(pay)
    ay = jnp.asarray(SPREAD.astype(np.float32))
    ty, tz = on_left(LY.both), on_right(LZ.both.T)

    hi = call(
        face_hi_kernel, face_x, pltpu.with_memory_space_constraint(u, pltpu.HBM), hbm=(0,),
        scratch=[pltpu.VMEM((8, NYL, NZL), F32), pltpu.SemaphoreType.DMA((4,))], name="face_hi",
    )
    xlo = shift(hi, "gx", 1)
    lo = call(face_lo_kernel, face_x, u, name="face_lo")
    xhi = shift(lo, "gx", -1)
    z1, z2, z3, z4, cols = call(
        local_z_kernel, [full] * 4 + [colshape], u, sz, on_right(np.concatenate([LZ.grad.T, LZ.filt.T], axis=1)),
        flops=3 * 10**9, nbytes=8 * 10**6, name="local_z",
    )
    inner = (NXL - 2, NYL, NZL)
    flux = call(
        flux_kernel, [inner] + [(inner, BF)] * 4 + [(3, NXL, NZL)] * 2,
        z1, z2, z3, u, velocity, sy, dy, flops=10**9, nbytes=12 * 10**6, name="flux",
    )
    dlt, cols = call(
        face_z_kernel, [(2, 3, NYL, NZL), colshape], xlo, xhi, cols, sz, dz, name="face_z"
    )
    near, far = swap(cols, "gz", 0), swap(cols, "gz", 1)
    r, lo, hi = call(
        residue_kernel, [full, face_y, face_y],
        *flux, z1, z2, z3, z4, dlt, u, velocity, sy, dy, ry, rz,
        scratch=[pltpu.VMEM((2, NYL, NZL), F32)], flops=3 * 10**9, nbytes=12 * 10**6, name="residue",
    )
    lo, hi, cval, hcols = call(
        face_y_kernel, [face_y, face_y, colshape, colshape], near, far, cols, lo, hi, sy, dy, ry,
        on_right(z_columns_x()), on_right(z_face_vectors()), on_left(y_rows()), name="face_y",
    )
    ylo, yhi = exchange(lo, hi, "gy")
    both = np.concatenate([LZ.both.T, pay_mat], axis=1)
    r2, vu, cols, cval = call(
        filter_kernel, [full, full, colshape, colshape],
        r, cval, z4, hcols, ty, fy, on_right(both), on_right(z_columns_z()),
        flops=3 * 10**9, nbytes=9 * 10**6, name="filter",
    )
    cols, rows = call(
        face_z2_kernel, [colshape, (8, NXL, NZL)], cols, r2, lo, hi, ylo, yhi, rx, rz, pay, ay,
        name="face_z2",
    )
    near, far = swap(cols, "gz", 0), swap(cols, "gz", 1)
    r2, vu, lo, hi = call(
        spread_kernel, [full, full, face_x, face_x], r2, vu, rows, ylo, yhi, cval, ay, tz, on_right(z_to_x()),
        scratch=[pltpu.VMEM((8, NXL, NZL), F32)], flops=10**9, nbytes=9 * 10**6, name="spread",
    )
    xlo, xhi = exchange(lo, hi, "gx")
    flo, fhi, hs = call(
        forward_kernel, [(8, 128), (8, 128), colshape], near, far, cval, on_right(z_short()), name="forward"
    )
    glo, ghi = exchange(flo, fhi, "gx")
    val = call(
        local_x_kernel, full, r2, vu, hs, on_right(z_spread()),
        flops=10**11, nbytes=10**8, name="local_x",
    )
    return call(
        final_kernel, full, val, xlo, xhi, glo, ghi, z_long(), hbm_out=True,
        scratch=[pltpu.VMEM(full, F32), pltpu.SemaphoreType.DMA((4,))], name="final",
    )


def solution(mesh):
    return jax.shard_map(
        on_device,
        mesh=mesh,
        in_specs=(P("gx", "gy", "gz"), P(None, "gx", "gy", "gz")),
        out_specs=P("gx", "gy", "gz"),
        check_vma=False,
    )
```

```python
import functools

import jax
import jax.numpy as jnp
import numpy as np
from jax import lax
from jax.experimental import pallas as pl
from jax.experimental.pallas import tpu as pltpu
from jax.sharding import PartitionSpec as P

DT = 0.002
NU_BASE = 0.3
SGS_COEF = 0.01
FILTER_STRENGTH = 0.3
GLL_POINTS = [
    -1.0,
    -0.8717401485096066,
    -0.5917001814331423,
    -0.2092992179024789,
    0.2092992179024789,
    0.5917001814331423,
    0.8717401485096066,
    1.0,
]
BF = jnp.bfloat16
F32 = jnp.float32
VM = pl.BlockSpec(memory_space=pltpu.VMEM)


def legendre_all(point):
    values_list = [1.0, point]
    for order in range(1, 7):
        values_list.append(
            ((2 * order + 1) * point * values_list[order] - order * values_list[order - 1])
            / (order + 1)
        )
    return values_list


def gll_tables():
    degree = 7
    table = [legendre_all(p) for p in GLL_POINTS]
    top = [table[i][degree] for i in range(8)]
    weights = [2.0 / (degree * (degree + 1) * top[i] * top[i]) for i in range(8)]
    derivative = [[0.0] * 8 for i in range(8)]
    for i in range(8):
        for j in range(8):
            if i != j:
                derivative[i][j] = top[i] / (top[j] * (GLL_POINTS[i] - GLL_POINTS[j]))
    derivative[0][0] = -degree * (degree + 1) / 4.0
    derivative[7][7] = degree * (degree + 1) / 4.0
    damping = [1.0] * 8
    for k in (6, 7):
        damping[k] = 1.0 - FILTER_STRENGTH * ((k - 5) / 2.0) ** 2
    gammas = [2.0 / (2 * k + 1) for k in range(7)] + [2.0 / degree]
    filter_mat = [[0.0] * 8 for i in range(8)]
    for i in range(8):
        for j in range(8):
            total = 0.0
            for k in range(8):
                total += table[i][k] * damping[k] * weights[j] * table[j][k] / gammas[k]
            filter_mat[i][j] = total
    return np.array(derivative), np.array(weights), np.array(filter_mat)


D, WT, FM = gll_tables()
DR = -DT * (D.T * WT[None, :]) / WT[:, None]


def block(mat, length):
    return np.kron(np.eye(length // 8), mat)


def average(length):
    mat = np.eye(length)
    for k in range(8, length, 8):
        mat[k - 1 : k + 1, k - 1 : k + 1] = 0.5
    mat[0, 0] = mat[-1, -1] = 0.5
    return mat


class Line:
    def __init__(self, length):
        avg = average(length)
        filt = block(FM, length)
        self.avg = avg
        self.grad = avg @ block(D, length)
        self.res = block(DR, length)
        self.filt = avg @ filt
        self.both = avg @ filt @ avg
        self.both[0, 0] += 0.25 * FM[7, 7]
        self.both[-1, -1] += 0.25 * FM[0, 0]
        self.face = filt @ avg
        first, last = np.eye(length)[0], np.eye(length)[-1]
        self.halo = np.stack([self.filt[:, 0] * 0.5, 0.5 * first, self.filt[:, -1] * 0.5, 0.5 * last])


def halves(mat):
    mat = np.asarray(mat, np.float64)
    high = mat.astype(jnp.bfloat16)
    low = (mat - high.astype(np.float64)).astype(jnp.bfloat16)
    return high, low


def on_right(mat):
    high, low = halves(mat)
    return jnp.asarray(np.concatenate([high, high, low], axis=0))


def on_left(mat):
    high, low = halves(mat)
    return jnp.asarray(np.concatenate([high, high, low], axis=1))


def exact_right(mat):
    mat = np.asarray(mat).astype(jnp.bfloat16)
    return jnp.asarray(np.concatenate([mat, mat], axis=0))


def exact_left(mat):
    mat = np.asarray(mat).astype(jnp.bfloat16)
    return jnp.asarray(np.concatenate([mat, mat], axis=1))


def split(val):
    high = val.astype(BF)
    return high, (val - high.astype(F32)).astype(BF)


def mm(a, b):
    return jnp.dot(a, b, preferred_element_type=F32)


def right(pair, mat):
    return mm(jnp.concatenate([pair[0], pair[1], pair[0]], axis=1), mat)


def right_exact(pair, mat):
    return mm(jnp.concatenate(pair, axis=1), mat)


def left(mat, pair):
    return mm(mat, jnp.concatenate([pair[0], pair[1], pair[0]], axis=0))


def left_exact(mat, pair):
    return mm(mat, jnp.concatenate(pair, axis=0))


def call(kernel, outs, *args, scratch=(), flops=0, nbytes=0, name=None, hbm=(), hbm_out=False, smem=(), limit=6 << 20):
    single = not isinstance(outs, list)
    place_at = pltpu.HBM if hbm_out else pltpu.VMEM
    pairs = [o if isinstance(o[0], tuple) else (o, F32) for o in ([outs] if single else outs)]
    shapes = [place_at(shape, dtype) for shape, dtype in pairs]
    kinds = {i: pl.BlockSpec(memory_space=pltpu.HBM) for i in hbm}
    kinds.update({i: pl.BlockSpec(memory_space=pltpu.SMEM) for i in smem})
    res = pl.pallas_call(
        kernel,
        out_shape=shapes,
        in_specs=[kinds.get(i, VM) for i in range(len(args))],
        out_specs=[pl.BlockSpec(memory_space=pltpu.HBM) if hbm_out else VM] * len(shapes),
        scratch_shapes=list(scratch),
        compiler_params=pltpu.CompilerParams(vmem_limit_bytes=limit),
        cost_estimate=pl.CostEstimate(flops=flops, bytes_accessed=nbytes, transcendentals=0),
        name=name,
    )(*args)
    return res[0] if single else res


NXL, NYL, NZL = 16, 96, 256
ROWS = NXL * NYL
TILES = NYL // 8


LX, LY, LZ = Line(NXL), Line(NYL), Line(NZL)


def face_hi_kernel(u_hbm, hi_ref, u_ref, sems):
    copies = []
    for c in range(4):
        rows = slice(c * 24, c * 24 + 24)
        copies.append(pltpu.make_async_copy(u_hbm.at[8:16, rows, :], u_ref.at[:, rows, :], sems.at[c]))
        copies[-1].start()
    for t in range(TILES):
        if t % 3 == 0:
            copies[t // 3].wait()
        rows = slice(t * 8, t * 8 + 8)
        hi_ref[0, rows, :] = 0.5 * u_ref[7, rows, :]
        hi_ref[1, rows, :] = sum(float(0.5 * D[7, j]) * u_ref[j, rows, :] for j in range(8))


def face_lo_kernel(u_ref, lo_ref):
    for t in range(TILES):
        rows = slice(t * 8, t * 8 + 8)
        lo_ref[0, rows, :] = 0.5 * u_ref[0, rows, :]
        lo_ref[1, rows, :] = sum(float(0.5 * D[0, j]) * u_ref[j, rows, :] for j in range(8))


def even_odd(mat, nodes, sign):
    even = [nodes[j] + nodes[7 - j] for j in range(4)]
    odd = [nodes[j] - nodes[7 - j] for j in range(4)]
    out = [None] * 8
    for i in range(4):
        a = sum(float(0.5 * (mat[i, j] + mat[i, 7 - j])) * even[j] for j in range(4))
        b = sum(float(0.5 * (mat[i, j] - mat[i, 7 - j])) * odd[j] for j in range(4))
        out[i] = a + b
        out[7 - i] = (a - b) if sign > 0 else (b - a)
    return out


def average_x(vals):
    vals = list(vals)
    mid = 0.5 * (vals[7] + vals[8])
    vals[7] = vals[8] = mid
    vals[0] = 0.5 * vals[0]
    vals[15] = 0.5 * vals[15]
    return vals


def lane_iota(rows):
    return lax.broadcasted_iota(jnp.int32, (rows, 128), 1)


def pack_columns(fields, x, lane):
    total = None
    for q, field in enumerate(fields):
        ends = jnp.where(lane == 127, field[:, 128:256], field[:, 0:128])
        pos = 2 * (16 * q + x)
        rolled = pltpu.roll(ends, (pos - 127) % 128, 1)
        piece = jnp.where((lane == pos) | (lane == pos + 1), rolled, 0.0)
        total = piece if total is None else total + piece
    return total


def received(near_ref, far_ref):
    first = lax.rem(lax.axis_index("gz"), 2) == 0
    near, far = near_ref[...], far_ref[...]
    return jnp.where(first, far, near), jnp.where(first, near, far)


def halo_columns(near_ref, far_ref):
    low, high = received(near_ref, far_ref)
    return jnp.where((lane_iota(NYL) % 2) == 0, pltpu.roll(high, 127, 1), pltpu.roll(low, 1, 1))


def local_z_kernel(u_ref, sz_ref, dfz_ref, z1, z2, z3, z4, cols):
    lane = lane_iota(16)
    for t in range(NYL // 16):
        rows = slice(t * 16, t * 16 + 16)
        p = split(jnp.concatenate([u_ref[k, rows, :] for k in range(NXL)], axis=0))
        slabs = lambda val: [val[16 * k : 16 * k + 16] for k in range(NXL)]
        avg = slabs(right_exact(p, sz_ref[...]))
        both = right(p, dfz_ref[...])
        grads = even_odd(D, avg[:8], -1) + even_odd(D, avg[8:], -1)
        outs = [
            average_x(avg),
            average_x(slabs(both[:, 0:NZL])),
            average_x(grads),
            slabs(both[:, NZL:]),
        ]
        acc = None
        for k in range(NXL):
            vals = [o[k] for o in outs]
            for ref, val in zip((z1, z2, z3, z4), vals):
                ref[k, rows, :] = val
            piece = pack_columns(vals, k, lane)
            acc = piece if acc is None else acc + piece
        cols[rows, :] = acc


def face_z_kernel(lo_ref, hi_ref, cols_ref, sz_ref, dz_ref, dlt, cols):
    p = split(jnp.concatenate([lo_ref[0], hi_ref[0]], axis=0))
    g = split(jnp.concatenate([lo_ref[1], hi_ref[1]], axis=0))
    outs = [right_exact(p, sz_ref[...]), right(p, dz_ref[...]), right_exact(g, sz_ref[...])]
    lane = lane_iota(NYL)
    acc = cols_ref[...]
    for s, x in ((0, 0), (1, NXL - 1)):
        vals = [o[s * NYL : (s + 1) * NYL] for o in outs]
        for q in range(3):
            dlt[s, q] = vals[q]
        acc = acc + pack_columns(vals, x, lane)
    cols[...] = acc


def row_sum(vals, coefs):
    row = lax.broadcasted_iota(jnp.int32, vals.shape, 0)
    weight = jnp.zeros(vals.shape, F32)
    for k, c in enumerate(coefs):
        weight = jnp.where(row == k, float(c), weight)
    return jnp.sum(vals * weight, axis=0, keepdims=True)


def eddy(sx, sy, sz):
    mag = 1.0 + sx * sx + sy * sy + sz * sz
    return NU_BASE + SGS_COEF * (mag * lax.rsqrt(mag))


def face_mask():
    row = lax.broadcasted_iota(jnp.int32, (NYL, NZL), 0)
    lane = lax.broadcasted_iota(jnp.int32, (NYL, NZL), 1)
    inner = (lane != 0) & (lane != NZL - 1) & (row != 0) & (row != NYL - 1)
    return inner.astype(F32)


def flux_slab(vals, u, vel, avg, grad, mask, row_lo, row_hi):
    sy = left(grad, split(vals[0]))
    sz, sx = left_exact(avg, split(vals[1])), left_exact(avg, split(vals[2]))
    lane = lax.broadcasted_iota(jnp.int32, (1, NZL), 1)
    inner = (lane != 0) & (lane != NZL - 1)
    for q, val in enumerate((sx, sy, sz)):
        row_lo(q, jnp.where(inner, val[0:1, :], 0.0))
        row_hi(q, jnp.where(inner, val[NYL - 1 : NYL, :], 0.0))
    nu = eddy(sx, sy, sz) * mask
    return [nu * s - vel[d].astype(F32) * u for d, s in enumerate((sx, sy, sz))]


def setter(ref, x):
    def put(q, val):
        ref[q, x : x + 1, :] = val

    return put


def flux_kernel(
    z1, z2, z3, u_ref, v_ref, avg_ref, dy_ref, fx, fyh, fyl, fzh, fzl, row_lo, row_hi
):
    mask = face_mask()
    row_lo[...] = jnp.zeros_like(row_lo)
    row_hi[...] = jnp.zeros_like(row_hi)
    for x in range(1, NXL - 1):
        u = u_ref[x]
        f = flux_slab(
            [z1[x], z2[x], z3[x]], u, [v_ref[d, x] for d in range(3)], avg_ref[...], dy_ref[...], mask,
            setter(row_lo, x), setter(row_hi, x),
        )
        fx[x - 1] = f[0]
        fyh[x - 1], fyl[x - 1] = split(f[1])
        fzh[x - 1], fzl[x - 1] = split(f[2])


def residue_kernel(
    fx, fyh, fyl, fzh, fzl, row_lo, row_hi, z1, z2, z3, z4, dlt, u_ref, v_ref,
    avg_ref, dy_ref, ry_ref, rz_ref, r_ref, out_lo, out_hi, edge,
):
    out_lo[0:3] = row_lo[...]
    out_hi[0:3] = row_hi[...]
    mask = face_mask()
    ends = []
    for s, x in ((0, 0), (1, NXL - 1)):
        vals = [ref[x] + dlt[s, q] for q, ref in enumerate((z1, z2, z3))]
        f = flux_slab(
            vals, u_ref[x], [v_ref[d, x] for d in range(3)],
            avg_ref[...], dy_ref[...], mask, setter(out_lo, x), setter(out_hi, x),
        )
        edge[s] = f[0]
        ends.append([split(f[1]), split(f[2])])
    for t in range(TILES):
        rows = slice(t * 8, t * 8 + 8)
        nodes = [edge[0, rows, :]] + [fx[k, rows, :] for k in range(NXL - 2)] + [edge[1, rows, :]]
        for e in range(2):
            for k, val in enumerate(even_odd(DR, nodes[8 * e : 8 * e + 8], -1)):
                r_ref[8 * e + k, rows, :] = val
    face = LY.face
    rz = rz_ref[...]
    groups = [(0, NXL - 1)] + [tuple(range(1 + 7 * c, 8 + 7 * c)) for c in range(2)]
    for group in groups:
        if 0 in group:
            pair = [jnp.concatenate([ends[0][1][i], ends[1][1][i]], axis=0) for i in range(2)]
        else:
            xs = slice(group[0] - 1, group[-1])
            pair = [ref[xs].reshape(len(group) * NYL, NZL) for ref in (fzh, fzl)]
        along_z = right(pair, rz)
        for i, x in enumerate(group):
            ypair = ends[i][0] if 0 in group else (fyh[x - 1], fyl[x - 1])
            r_ref[x] = r_ref[x] + (left(ry_ref[...], ypair) + along_z[i * NYL : (i + 1) * NYL])
    for x in range(NXL):
        one = slice(x, x + 1)
        out_lo[3, one, :] = r_ref[x, 0:1, :]
        out_hi[3, one, :] = r_ref[x, NYL - 1 : NYL, :]
        out_lo[4, one, :] = row_sum(r_ref[x, 0:16, :], face[0, 0:16])
        out_hi[4, one, :] = row_sum(r_ref[x, NYL - 16 : NYL, :], face[-1, NYL - 16 :])
        out_lo[5, one, :] = row_sum(z4[x, 0:8, :], 0.5 * FM[0])
        out_hi[5, one, :] = row_sum(z4[x, NYL - 8 : NYL, :], 0.5 * FM[7])


def z_columns_x():
    mat = np.zeros((128, 128))
    for side in range(2):
        mat[side:32:2, side:32:2] = LX.res.T
    return mat


def z_face_vectors():
    mat = np.zeros((128, NZL))
    for x in range(NXL):
        for side, node in ((0, NZL - 1), (1, 0)):
            mat[2 * x + side, node] = 1.0
            mat[32 + 2 * x + side] = LZ.res[:, node]
    return mat


def y_rows():
    rows = np.zeros((8, NYL))
    rows[0], rows[1] = LY.face[0], LY.face[-1]
    rows[2, 0:8], rows[3, NYL - 8 :] = 0.5 * FM[0], 0.5 * FM[7]
    return rows


def face_y_kernel(
    near, far, cols, lo_ref, hi_ref, avg_ref, dy_ref, ry_ref, rx_ref, zv_ref, yr_ref,
    out_lo, out_hi, cval, halo_ref,
):
    lane = lane_iota(NYL)
    halo = halo_columns(near, far)
    halo_ref[...] = halo
    pair = split(cols[...] + halo)
    sy = left(dy_ref[...], pair)
    avg = left_exact(avg_ref[...], pair)
    sz, sx = pltpu.roll(avg, 96, 1), pltpu.roll(avg, 64, 1)
    row = lax.broadcasted_iota(jnp.int32, (NYL, 128), 0)
    keep = (lane < 32) & (row != 0) & (row != NYL - 1)
    nu = jnp.where(keep, eddy(sx, sy, sz), 0.0)
    tau = right(split(nu * sx), rx_ref[...]) + left(ry_ref[...], split(nu * sy))
    val = tau + pltpu.roll(nu * sz, 32, 1)
    cval[...] = val
    rows = left(yr_ref[...], split(jnp.concatenate([val, pltpu.roll(halo, 32, 1)], axis=1)))
    lane16 = lane_iota(NXL)
    row16 = lax.broadcasted_iota(jnp.int32, (NXL, 128), 0)
    diag = ((lane16 % 32) // 2) == row16
    short, long = diag & (lane16 < 32), diag & (lane16 < 64)
    parts_ = []
    for s, r in ((0, 0), (1, NYL - 1)):
        one = slice(r, r + 1)
        for vec, keep in (
            (sx[one], short), (sy[one], short), (sz[one], short), (val[one], long),
            (rows[s : s + 1, 0:128], long), (rows[2 + s : 3 + s, 128:256], short),
        ):
            parts_.append(jnp.where(keep, jnp.broadcast_to(vec, (NXL, 128)), 0.0))
    add = right(split(jnp.concatenate(parts_, axis=0)), zv_ref[...])
    for q in range(6):
        out_lo[q] = lo_ref[q] + add[16 * q : 16 * q + 16]
        out_hi[q] = hi_ref[q] + add[96 + 16 * q : 112 + 16 * q]


def place(pay, x, lane):
    return jnp.where(((lane % 32) // 2) == x, pay, 0.0)


def filter_kernel(r_ref, cval, z4, hcols, ty_ref, fy_ref, tp_ref, zc_ref, r2, vu, cols, cout):
    lane = lane_iota(NYL)
    acc = None
    for c in range(4):
        xs = range(4 * c, 4 * c + 4)
        val = jnp.concatenate([left(ty_ref[...], split(r_ref[x])) for x in xs], axis=0)
        out = right(split(val), tp_ref[...])
        for k, x in enumerate(xs):
            part = out[k * NYL : (k + 1) * NYL]
            r2[x] = part[:, 0:NZL]
            piece = place(part[:, NZL:], x, lane)
            acc = piece if acc is None else acc + piece
            rolled = pltpu.roll(hcols[...], (-2 * (48 + x) - 1) % 128, 1)
            field = jnp.concatenate(
                [
                    z4[x, :, 0:128] + jnp.where(lane == 0, rolled, 0.0),
                    z4[x, :, 128:256] + jnp.where(lane == 127, rolled, 0.0),
                ],
                axis=1,
            )
            vu[x] = left(fy_ref[...], split(field))
    val = left(ty_ref[...], split(cval[...]))
    cout[...] = val
    cols[...] = acc + right(split(val), zc_ref[...])


def z_columns_z():
    mat = np.zeros((128, 128))
    for x in range(NXL):
        for side, node in ((0, NZL - 1), (1, 0)):
            at = 2 * x + side
            mat[at, at], mat[32 + at, at] = 1.0, LZ.res[node, node]
            mat[at, 32 + at] = LZ.face[node, node]
            mat[32 + at, 32 + at] = LZ.face[node] @ LZ.res[:, node]
    return mat


def y_spread():
    low_t = LY.both[:, 0] + LY.halo[0] + LY.face[-1, -1] * LY.halo[1]
    low_g = (
        LY.both @ LY.res[:, 0] + DR[7, 7] * LY.halo[0] + (LY.face[-1] @ LY.res[:, -1]) * LY.halo[1]
    )
    high_t = LY.both[:, -1] + LY.halo[2] + LY.face[0, 0] * LY.halo[3]
    high_g = (
        LY.both @ LY.res[:, -1] + DR[0, 0] * LY.halo[2] + (LY.face[0] @ LY.res[:, 0]) * LY.halo[3]
    )
    return np.stack(
        [low_t, low_g, LY.halo[0], LY.halo[1], high_t, high_g, LY.halo[2], LY.halo[3]], axis=1
    )


SPREAD = y_spread()


def face_z2_kernel(
    cols_ref, after_ref, own_lo, own_hi, lo_ref, hi_ref, rx_ref, rz_ref, pay_ref, ay_ref, cols, rows_ref
):
    both = ((own_lo, lo_ref), (own_hi, hi_ref))
    flux = []
    for own, ref in both:
        s = [own[q] + ref[q] for q in range(3)]
        nu = eddy(*s)
        flux.append([nu * v for v in s])
    along_x = left(rx_ref[...], split(jnp.concatenate([flux[0][0], flux[1][0]], axis=1)))
    along_z = right(split(jnp.concatenate([flux[0][2], flux[1][2]], axis=0)), rz_ref[...])
    vals = []
    for s, (own, ref) in enumerate(both):
        tau = along_x[:, s * NZL : (s + 1) * NZL] + along_z[s * NXL : (s + 1) * NXL]
        vals += [tau, flux[s][1], ref[3], ref[4]]
    for k, val in enumerate(vals):
        rows_ref[k] = val
    pay = right(split(jnp.concatenate(vals, axis=0)), pay_ref[...])
    lane16 = lane_iota(NXL)
    row16 = lax.broadcasted_iota(jnp.int32, (NXL, 128), 0)
    keep = ((lane16 % 32) // 2) == row16
    vecs = []
    for k in range(8):
        val = pay[16 * k : 16 * k + 16]
        vec = jnp.sum(jnp.where(keep, val, 0.0), axis=0, keepdims=True)
        vecs.append(vec)
    for rows, ks in ((slice(0, 24), range(4)), (slice(NYL - 24, NYL), range(4, 8))):
        acc = cols_ref[rows, :]
        for k in ks:
            acc = acc + ay_ref[rows, k : k + 1] * vecs[k]
        cols[rows, :] = acc
    cols[24 : NYL - 24, :] = cols_ref[24 : NYL - 24, :]


def spread_kernel(
    r2, vu, rows_ref, lo_ref, hi_ref, cval, ay_ref, tz_ref, mat_ref, out, vout, pay_lo, pay_hi, zr
):
    zr[...] = right(split(rows_ref[...].reshape(8 * NXL, NZL)), tz_ref[...]).reshape(8, NXL, NZL)
    add = right(split(cval[...]), mat_ref[...])
    row8 = lax.broadcasted_iota(jnp.int32, (8, NZL), 0)
    for t in range(TILES):
        rows = slice(t * 8, t * 8 + 8)
        r, w = [], []
        for x in range(NXL):
            one = slice(x, x + 1)
            val, wal = r2[x, rows, :], vu[x, rows, :]
            for k in range(8):
                if np.any(SPREAD[rows, k]):
                    val = val + ay_ref[rows, k : k + 1] * zr[k, one, :]
            if t == 0:
                wal = wal + jnp.where(row8 == 0, lo_ref[5, one, :], 0.0)
            if t == TILES - 1:
                wal = wal + jnp.where(row8 == 7, hi_ref[5, one, :], 0.0)
            out[x, rows, :] = val
            vout[x, rows, :] = wal
            r.append(val)
            w.append(wal)
        a = [s + v for s, v in zip(average_x(r), w)]
        low = sum(float(FM[0, j]) * a[j] for j in range(8))
        high = sum(float(FM[7, j]) * a[8 + j] for j in range(8))
        for q, (ref, val) in enumerate(((pay_lo, r[0]), (pay_lo, low), (pay_hi, r[15]), (pay_hi, high))):
            ref[q % 2, rows, :] = val + add[rows, q * NZL : (q + 1) * NZL]


def z_vectors():
    vecs = [[LZ.halo[0], LZ.halo[2]], [LZ.halo[1], LZ.halo[3]]]
    vecs.append([LZ.both[:, -1], LZ.both[:, 0]])
    vecs.append([LZ.both @ LZ.res[:, -1], LZ.both @ LZ.res[:, 0]])
    return vecs


def z_spread():
    add = np.zeros((128, NZL))
    for q, pair in enumerate(z_vectors()):
        for side in range(2):
            add[32 * q + side] = pair[side]
    return add


def z_to_x():
    out = np.zeros((128, 4 * NZL))
    low, high = LX.face[0], LX.face[-1]
    for x in range(NXL):
        for q, pair in enumerate(z_vectors()[2:]):
            for side in range(2):
                lane, vec = 2 * (16 * q + x) + side, pair[side]
                if x == 0:
                    out[lane, 0:NZL] = vec
                if x == NXL - 1:
                    out[lane, 2 * NZL : 3 * NZL] = vec
                out[lane, NZL : 2 * NZL] = low[x] * vec
                out[lane, 3 * NZL :] = high[x] * vec
    return out


def z_short():
    out = np.zeros((128, 128))
    low, high = LX.face[0], LX.face[-1]
    for x in range(NXL):
        for q in range(2):
            for side in range(2):
                lane, c = 2 * (16 * q + x) + side, 2 * q + side
                if x == 0:
                    out[lane, c] = 1.0
                if x == NXL - 1:
                    out[lane, 8 + c] = 1.0
                out[lane, 4 + c], out[lane, 12 + c] = low[x], high[x]
    return out


def z_long():
    out = np.zeros((16, 4 * NZL))
    for q, pair in enumerate(z_vectors()[:2]):
        for side in range(2):
            for k in range(4):
                out[4 * k + 2 * q + side, k * NZL : (k + 1) * NZL] = pair[side]
    high, low = halves(out)
    rest = np.zeros((80, 4 * NZL)).astype(jnp.bfloat16)
    return jnp.asarray(np.concatenate([high, high, low, rest], axis=0))


def forward_kernel(near, far, cval, mat_ref, flo, fhi, hs):
    low, high = received(near, far)
    lane = lane_iota(NYL)
    halo = jnp.where((lane % 2) == 0, low, high)
    hs[...] = jnp.where(lane < 64, halo, pltpu.roll(cval[...], 64, 1))
    short = right(split(halo), mat_ref[...])
    lane8 = lane_iota(8)
    for ref, base in ((flo, 0), (fhi, 8)):
        acc = None
        for t in range(TILES):
            piece = pltpu.roll(short[8 * t : 8 * t + 8], (8 * t - base) % 128, 1)
            piece = jnp.where((lane8 // 8) == t, piece, 0.0)
            acc = piece if acc is None else acc + piece
        ref[...] = acc


def forwarded(glo, ghi, mat):
    lane8 = lane_iota(8)
    tiles = []
    for t in range(TILES):
        low = pltpu.roll(glo, (-8 * t) % 128, 1)
        high = pltpu.roll(ghi, (8 - 8 * t) % 128, 1)
        tiles.append(jnp.where(lane8 < 8, low, jnp.where(lane8 < 16, high, 0.0)))
    val = jnp.concatenate(tiles, axis=0)
    top = val.astype(BF).astype(F32)
    val = top + pltpu.roll(val - top, 16, 1) + pltpu.roll(top, 32, 1)
    return mm(val.astype(BF), mat)


def local_x_kernel(r2, vu, hs, add_ref, out):
    for t in range(NYL // 16):
        rows = slice(t * 16, t * 16 + 16)
        col = hs[rows, :]
        rolled = [pltpu.roll(col, (-2 * x) % 128, 1) if x else col for x in range(NXL)]
        add = right(split(jnp.concatenate(rolled, axis=0)), add_ref[...])
        r = [r2[x, rows, :] + add[16 * x : 16 * x + 16] for x in range(NXL)]
        a = [s + vu[k, rows, :] for k, s in enumerate(average_x(r))]
        f = average_x(even_odd(FM, a[:8], 1) + even_odd(FM, a[8:], 1))
        f[0] = f[0] + float(0.25 * FM[7, 7]) * r[0]
        f[15] = f[15] + float(0.25 * FM[0, 0]) * r[15]
        for k in range(NXL):
            out[k, rows, :] = f[k]


def final_kernel(val_ref, lo_ref, hi_ref, glo_ref, ghi_ref, mat_ref, out_hbm, buf, sems):
    copies = []
    add = forwarded(glo_ref[...], ghi_ref[...], mat_ref[...])
    for c in range(6):
        for t in range(2):
            rows = slice(c * 16 + t * 8, c * 16 + t * 8 + 8)
            halo = [lo_ref[0, rows, :], lo_ref[1, rows, :], hi_ref[0, rows, :], hi_ref[1, rows, :]]
            halo = [v + add[rows, j * NZL : (j + 1) * NZL] for j, v in enumerate(halo)]
            for k in range(NXL):
                val = val_ref[k, rows, :]
                for j in range(4):
                    if LX.halo[j][k] != 0.0:
                        val = val + float(LX.halo[j][k]) * halo[j]
                buf[k, rows, :] = val
        rows = slice(c * 16, c * 16 + 16)
        copies.append(pltpu.make_async_copy(buf.at[:, rows, :], out_hbm.at[:, rows, :], sems.at[c]))
        copies[-1].start()
    for copy in copies:
        copy.wait()


def shift(val, axis, step):
    count = lax.axis_size(axis)
    return lax.ppermute(val, axis, [(i, (i + step) % count) for i in range(count)])


def exchange(lo, hi, axis):
    return shift(hi, axis, 1), shift(lo, axis, -1)


def swap(val, axis, start):
    count = lax.axis_size(axis)
    pairs = [(k % count, (k + 1) % count) for k in range(start, count + start, 2)]
    return lax.ppermute(val, axis, pairs + [(b, a) for a, b in pairs])


def on_device(u, velocity):
    full = (NXL, NYL, NZL)
    face_x = (2, NYL, NZL)
    face_y = (6, NXL, NZL)
    colshape = (NYL, 128)

    sz, dz = exact_right(LZ.avg.T), on_right(LZ.grad.T)
    sy, dy, fy = exact_left(LY.avg), on_left(LY.grad), on_left(LY.filt)
    ry, rz, rx = on_left(LY.res), on_right(LZ.res.T), on_left(LX.res)
    pay = np.zeros((NZL, 128))
    pay[NZL - 1, 0:32:2] = pay[0, 1:32:2] = 1.0
    pay[:, 32:64:2], pay[:, 33:64:2] = LZ.face[-1][:, None], LZ.face[0][:, None]
    pay_mat = pay
    pay = on_right(pay)
    ay = jnp.asarray(SPREAD.astype(np.float32))
    ty, tz = on_left(LY.both), on_right(LZ.both.T)

    hi = call(
        face_hi_kernel, face_x, pltpu.with_memory_space_constraint(u, pltpu.HBM), hbm=(0,),
        scratch=[pltpu.VMEM((8, NYL, NZL), F32), pltpu.SemaphoreType.DMA((4,))], name="face_hi",
    )
    xlo = shift(hi, "gx", 1)
    lo = call(face_lo_kernel, face_x, u, name="face_lo")
    xhi = shift(lo, "gx", -1)
    z1, z2, z3, z4, cols = call(
        local_z_kernel, [full] * 4 + [colshape], u, sz, on_right(np.concatenate([LZ.grad.T, LZ.filt.T], axis=1)),
        flops=3 * 10**9, nbytes=8 * 10**6, name="local_z",
    )
    inner = (NXL - 2, NYL, NZL)
    flux = call(
        flux_kernel, [inner] + [(inner, BF)] * 4 + [(3, NXL, NZL)] * 2,
        z1, z2, z3, u, velocity, sy, dy, flops=10**9, nbytes=12 * 10**6, name="flux",
    )
    dlt, cols = call(
        face_z_kernel, [(2, 3, NYL, NZL), colshape], xlo, xhi, cols, sz, dz, name="face_z"
    )
    near, far = swap(cols, "gz", 0), swap(cols, "gz", 1)
    r, lo, hi = call(
        residue_kernel, [full, face_y, face_y],
        *flux, z1, z2, z3, z4, dlt, u, velocity, sy, dy, ry, rz,
        scratch=[pltpu.VMEM((2, NYL, NZL), F32)], flops=3 * 10**9, nbytes=12 * 10**6, name="residue",
    )
    lo, hi, cval, hcols = call(
        face_y_kernel, [face_y, face_y, colshape, colshape], near, far, cols, lo, hi, sy, dy, ry,
        on_right(z_columns_x()), on_right(z_face_vectors()), on_left(y_rows()), name="face_y",
    )
    ylo, yhi = exchange(lo, hi, "gy")
    both = np.concatenate([LZ.both.T, pay_mat], axis=1)
    r2, vu, cols, cval = call(
        filter_kernel, [full, full, colshape, colshape],
        r, cval, z4, hcols, ty, fy, on_right(both), on_right(z_columns_z()),
        flops=3 * 10**9, nbytes=9 * 10**6, name="filter",
    )
    cols, rows = call(
        face_z2_kernel, [colshape, (8, NXL, NZL)], cols, r2, lo, hi, ylo, yhi, rx, rz, pay, ay,
        name="face_z2",
    )
    near, far = swap(cols, "gz", 0), swap(cols, "gz", 1)
    r2, vu, lo, hi = call(
        spread_kernel, [full, full, face_x, face_x], r2, vu, rows, ylo, yhi, cval, ay, tz, on_right(z_to_x()),
        scratch=[pltpu.VMEM((8, NXL, NZL), F32)], flops=10**9, nbytes=9 * 10**6, name="spread",
    )
    xlo, xhi = exchange(lo, hi, "gx")
    flo, fhi, hs = call(
        forward_kernel, [(8, 128), (8, 128), colshape], near, far, cval, on_right(z_short()), name="forward"
    )
    glo, ghi = exchange(flo, fhi, "gx")
    val = call(
        local_x_kernel, full, r2, vu, hs, on_right(z_spread()),
        flops=10**11, nbytes=10**8, name="local_x",
    )
    return call(
        final_kernel, full, val, xlo, xhi, glo, ghi, z_long(), hbm_out=True,
        scratch=[pltpu.VMEM(full, F32), pltpu.SemaphoreType.DMA((6,))], name="final",
    )


def solution(mesh):
    return jax.shard_map(
        on_device,
        mesh=mesh,
        in_specs=(P("gx", "gy", "gz"), P(None, "gx", "gy", "gz")),
        out_specs=P("gx", "gy", "gz"),
        check_vma=False,
    )
```

```python
import functools

import jax
import jax.numpy as jnp
import numpy as np
from jax import lax
from jax.experimental import pallas as pl
from jax.experimental.pallas import tpu as pltpu
from jax.sharding import PartitionSpec as P

DT = 0.002
NU_BASE = 0.3
SGS_COEF = 0.01
FILTER_STRENGTH = 0.3
GLL_POINTS = [
    -1.0,
    -0.8717401485096066,
    -0.5917001814331423,
    -0.2092992179024789,
    0.2092992179024789,
    0.5917001814331423,
    0.8717401485096066,
    1.0,
]
BF = jnp.bfloat16
F32 = jnp.float32
VM = pl.BlockSpec(memory_space=pltpu.VMEM)


def legendre_all(point):
    values_list = [1.0, point]
    for order in range(1, 7):
        values_list.append(
            ((2 * order + 1) * point * values_list[order] - order * values_list[order - 1])
            / (order + 1)
        )
    return values_list


def gll_tables():
    degree = 7
    table = [legendre_all(p) for p in GLL_POINTS]
    top = [table[i][degree] for i in range(8)]
    weights = [2.0 / (degree * (degree + 1) * top[i] * top[i]) for i in range(8)]
    derivative = [[0.0] * 8 for i in range(8)]
    for i in range(8):
        for j in range(8):
            if i != j:
                derivative[i][j] = top[i] / (top[j] * (GLL_POINTS[i] - GLL_POINTS[j]))
    derivative[0][0] = -degree * (degree + 1) / 4.0
    derivative[7][7] = degree * (degree + 1) / 4.0
    damping = [1.0] * 8
    for k in (6, 7):
        damping[k] = 1.0 - FILTER_STRENGTH * ((k - 5) / 2.0) ** 2
    gammas = [2.0 / (2 * k + 1) for k in range(7)] + [2.0 / degree]
    filter_mat = [[0.0] * 8 for i in range(8)]
    for i in range(8):
        for j in range(8):
            total = 0.0
            for k in range(8):
                total += table[i][k] * damping[k] * weights[j] * table[j][k] / gammas[k]
            filter_mat[i][j] = total
    return np.array(derivative), np.array(weights), np.array(filter_mat)


D, WT, FM = gll_tables()
DR = -DT * (D.T * WT[None, :]) / WT[:, None]


def block(mat, length):
    return np.kron(np.eye(length // 8), mat)


def average(length):
    mat = np.eye(length)
    for k in range(8, length, 8):
        mat[k - 1 : k + 1, k - 1 : k + 1] = 0.5
    mat[0, 0] = mat[-1, -1] = 0.5
    return mat


class Line:
    def __init__(self, length):
        avg = average(length)
        filt = block(FM, length)
        self.avg = avg
        self.grad = avg @ block(D, length)
        self.res = block(DR, length)
        self.filt = avg @ filt
        self.both = avg @ filt @ avg
        self.both[0, 0] += 0.25 * FM[7, 7]
        self.both[-1, -1] += 0.25 * FM[0, 0]
        self.face = filt @ avg
        first, last = np.eye(length)[0], np.eye(length)[-1]
        self.halo = np.stack([self.filt[:, 0] * 0.5, 0.5 * first, self.filt[:, -1] * 0.5, 0.5 * last])


def halves(mat):
    mat = np.asarray(mat, np.float64)
    high = mat.astype(jnp.bfloat16)
    low = (mat - high.astype(np.float64)).astype(jnp.bfloat16)
    return high, low


def on_right(mat):
    high, low = halves(mat)
    return jnp.asarray(np.concatenate([high, high, low], axis=0))


def on_left(mat):
    high, low = halves(mat)
    return jnp.asarray(np.concatenate([high, high, low], axis=1))


def exact_right(mat):
    mat = np.asarray(mat).astype(jnp.bfloat16)
    return jnp.asarray(np.concatenate([mat, mat], axis=0))


def exact_left(mat):
    mat = np.asarray(mat).astype(jnp.bfloat16)
    return jnp.asarray(np.concatenate([mat, mat], axis=1))


def split(val):
    high = val.astype(BF)
    return high, (val - high.astype(F32)).astype(BF)


def mm(a, b):
    return jnp.dot(a, b, preferred_element_type=F32)


def right(pair, mat):
    return mm(jnp.concatenate([pair[0], pair[1], pair[0]], axis=1), mat)


def right_exact(pair, mat):
    return mm(jnp.concatenate(pair, axis=1), mat)


def left(mat, pair):
    return mm(mat, jnp.concatenate([pair[0], pair[1], pair[0]], axis=0))


def left_exact(mat, pair):
    return mm(mat, jnp.concatenate(pair, axis=0))


def call(kernel, outs, *args, scratch=(), flops=0, nbytes=0, name=None, hbm=(), hbm_out=False, smem=(), limit=6 << 20):
    single = not isinstance(outs, list)
    place_at = pltpu.HBM if hbm_out else pltpu.VMEM
    pairs = [o if isinstance(o[0], tuple) else (o, F32) for o in ([outs] if single else outs)]
    shapes = [place_at(shape, dtype) for shape, dtype in pairs]
    kinds = {i: pl.BlockSpec(memory_space=pltpu.HBM) for i in hbm}
    kinds.update({i: pl.BlockSpec(memory_space=pltpu.SMEM) for i in smem})
    res = pl.pallas_call(
        kernel,
        out_shape=shapes,
        in_specs=[kinds.get(i, VM) for i in range(len(args))],
        out_specs=[pl.BlockSpec(memory_space=pltpu.HBM) if hbm_out else VM] * len(shapes),
        scratch_shapes=list(scratch),
        compiler_params=pltpu.CompilerParams(vmem_limit_bytes=limit),
        cost_estimate=pl.CostEstimate(flops=flops, bytes_accessed=nbytes, transcendentals=0),
        name=name,
    )(*args)
    return res[0] if single else res


NXL, NYL, NZL = 16, 96, 256
ROWS = NXL * NYL
TILES = NYL // 8


LX, LY, LZ = Line(NXL), Line(NYL), Line(NZL)


def face_hi_kernel(u_hbm, hi_ref, u_ref, sems):
    copies = []
    for c in range(8):
        copies.append(pltpu.make_async_copy(u_hbm.at[8 + c], u_ref.at[c], sems.at[c]))
        copies[-1].start()
    for copy in copies:
        copy.wait()
    for t in range(TILES):
        rows = slice(t * 8, t * 8 + 8)
        hi_ref[0, rows, :] = 0.5 * u_ref[7, rows, :]
        hi_ref[1, rows, :] = sum(float(0.5 * D[7, j]) * u_ref[j, rows, :] for j in range(8))


def face_lo_kernel(u_ref, lo_ref):
    for t in range(TILES):
        rows = slice(t * 8, t * 8 + 8)
        lo_ref[0, rows, :] = 0.5 * u_ref[0, rows, :]
        lo_ref[1, rows, :] = sum(float(0.5 * D[0, j]) * u_ref[j, rows, :] for j in range(8))


def even_odd(mat, nodes, sign):
    even = [nodes[j] + nodes[7 - j] for j in range(4)]
    odd = [nodes[j] - nodes[7 - j] for j in range(4)]
    out = [None] * 8
    for i in range(4):
        a = sum(float(0.5 * (mat[i, j] + mat[i, 7 - j])) * even[j] for j in range(4))
        b = sum(float(0.5 * (mat[i, j] - mat[i, 7 - j])) * odd[j] for j in range(4))
        out[i] = a + b
        out[7 - i] = (a - b) if sign > 0 else (b - a)
    return out


def average_x(vals):
    vals = list(vals)
    mid = 0.5 * (vals[7] + vals[8])
    vals[7] = vals[8] = mid
    vals[0] = 0.5 * vals[0]
    vals[15] = 0.5 * vals[15]
    return vals


def lane_iota(rows):
    return lax.broadcasted_iota(jnp.int32, (rows, 128), 1)


def pack_columns(fields, x, lane):
    total = None
    for q, field in enumerate(fields):
        ends = jnp.where(lane == 127, field[:, 128:256], field[:, 0:128])
        pos = 2 * (16 * q + x)
        rolled = pltpu.roll(ends, (pos - 127) % 128, 1)
        piece = jnp.where((lane == pos) | (lane == pos + 1), rolled, 0.0)
        total = piece if total is None else total + piece
    return total


def received(near_ref, far_ref):
    first = lax.rem(lax.axis_index("gz"), 2) == 0
    near, far = near_ref[...], far_ref[...]
    return jnp.where(first, far, near), jnp.where(first, near, far)


def halo_columns(near_ref, far_ref):
    low, high = received(near_ref, far_ref)
    return jnp.where((lane_iota(NYL) % 2) == 0, pltpu.roll(high, 127, 1), pltpu.roll(low, 1, 1))


def local_z_kernel(u_ref, sz_ref, dfz_ref, z1, z2, z3, z4, cols):
    lane = lane_iota(16)
    for t in range(NYL // 16):
        rows = slice(t * 16, t * 16 + 16)
        p = split(jnp.concatenate([u_ref[k, rows, :] for k in range(NXL)], axis=0))
        slabs = lambda val: [val[16 * k : 16 * k + 16] for k in range(NXL)]
        avg = slabs(right_exact(p, sz_ref[...]))
        both = right(p, dfz_ref[...])
        grads = even_odd(D, avg[:8], -1) + even_odd(D, avg[8:], -1)
        outs = [
            average_x(avg),
            average_x(slabs(both[:, 0:NZL])),
            average_x(grads),
            slabs(both[:, NZL:]),
        ]
        acc = None
        for k in range(NXL):
            vals = [o[k] for o in outs]
            for ref, val in zip((z1, z2, z3, z4), vals):
                ref[k, rows, :] = val
            piece = pack_columns(vals, k, lane)
            acc = piece if acc is None else acc + piece
        cols[rows, :] = acc


def face_z_kernel(lo_ref, hi_ref, cols_ref, sz_ref, dz_ref, dlt, cols):
    p = split(jnp.concatenate([lo_ref[0], hi_ref[0]], axis=0))
    g = split(jnp.concatenate([lo_ref[1], hi_ref[1]], axis=0))
    outs = [right_exact(p, sz_ref[...]), right(p, dz_ref[...]), right_exact(g, sz_ref[...])]
    lane = lane_iota(NYL)
    acc = cols_ref[...]
    for s, x in ((0, 0), (1, NXL - 1)):
        vals = [o[s * NYL : (s + 1) * NYL] for o in outs]
        for q in range(3):
            dlt[s, q] = vals[q]
        acc = acc + pack_columns(vals, x, lane)
    cols[...] = acc


def row_sum(vals, coefs):
    row = lax.broadcasted_iota(jnp.int32, vals.shape, 0)
    weight = jnp.zeros(vals.shape, F32)
    for k, c in enumerate(coefs):
        weight = jnp.where(row == k, float(c), weight)
    return jnp.sum(vals * weight, axis=0, keepdims=True)


def eddy(sx, sy, sz):
    mag = 1.0 + sx * sx + sy * sy + sz * sz
    return NU_BASE + SGS_COEF * (mag * lax.rsqrt(mag))


def face_mask():
    row = lax.broadcasted_iota(jnp.int32, (NYL, NZL), 0)
    lane = lax.broadcasted_iota(jnp.int32, (NYL, NZL), 1)
    inner = (lane != 0) & (lane != NZL - 1) & (row != 0) & (row != NYL - 1)
    return inner.astype(F32)


def flux_slab(vals, u, vel, avg, grad, mask, row_lo, row_hi):
    sy = left(grad, split(vals[0]))
    sz, sx = left_exact(avg, split(vals[1])), left_exact(avg, split(vals[2]))
    lane = lax.broadcasted_iota(jnp.int32, (1, NZL), 1)
    inner = (lane != 0) & (lane != NZL - 1)
    for q, val in enumerate((sx, sy, sz)):
        row_lo(q, jnp.where(inner, val[0:1, :], 0.0))
        row_hi(q, jnp.where(inner, val[NYL - 1 : NYL, :], 0.0))
    nu = eddy(sx, sy, sz) * mask
    return [nu * s - vel[d].astype(F32) * u for d, s in enumerate((sx, sy, sz))]


def setter(ref, x):
    def put(q, val):
        ref[q, x : x + 1, :] = val

    return put


def flux_kernel(
    z1, z2, z3, u_ref, v_ref, avg_ref, dy_ref, fx, fyh, fyl, fzh, fzl, row_lo, row_hi
):
    mask = face_mask()
    row_lo[...] = jnp.zeros_like(row_lo)
    row_hi[...] = jnp.zeros_like(row_hi)
    for x in range(1, NXL - 1):
        u = u_ref[x]
        f = flux_slab(
            [z1[x], z2[x], z3[x]], u, [v_ref[d, x] for d in range(3)], avg_ref[...], dy_ref[...], mask,
            setter(row_lo, x), setter(row_hi, x),
        )
        fx[x - 1] = f[0]
        fyh[x - 1], fyl[x - 1] = split(f[1])
        fzh[x - 1], fzl[x - 1] = split(f[2])


def residue_kernel(
    fx, fyh, fyl, fzh, fzl, row_lo, row_hi, z1, z2, z3, z4, dlt, u_ref, v_ref,
    avg_ref, dy_ref, ry_ref, rz_ref, r_ref, out_lo, out_hi, edge,
):
    out_lo[0:3] = row_lo[...]
    out_hi[0:3] = row_hi[...]
    mask = face_mask()
    ends = []
    for s, x in ((0, 0), (1, NXL - 1)):
        vals = [ref[x] + dlt[s, q] for q, ref in enumerate((z1, z2, z3))]
        f = flux_slab(
            vals, u_ref[x], [v_ref[d, x] for d in range(3)],
            avg_ref[...], dy_ref[...], mask, setter(out_lo, x), setter(out_hi, x),
        )
        edge[s] = f[0]
        ends.append([split(f[1]), split(f[2])])
    for t in range(TILES):
        rows = slice(t * 8, t * 8 + 8)
        nodes = [edge[0, rows, :]] + [fx[k, rows, :] for k in range(NXL - 2)] + [edge[1, rows, :]]
        for e in range(2):
            for k, val in enumerate(even_odd(DR, nodes[8 * e : 8 * e + 8], -1)):
                r_ref[8 * e + k, rows, :] = val
    face = LY.face
    rz = rz_ref[...]
    groups = [(0, NXL - 1)] + [tuple(range(1 + 7 * c, 8 + 7 * c)) for c in range(2)]
    for group in groups:
        if 0 in group:
            pair = [jnp.concatenate([ends[0][1][i], ends[1][1][i]], axis=0) for i in range(2)]
        else:
            xs = slice(group[0] - 1, group[-1])
            pair = [ref[xs].reshape(len(group) * NYL, NZL) for ref in (fzh, fzl)]
        along_z = right(pair, rz)
        for i, x in enumerate(group):
            ypair = ends[i][0] if 0 in group else (fyh[x - 1], fyl[x - 1])
            r_ref[x] = r_ref[x] + (left(ry_ref[...], ypair) + along_z[i * NYL : (i + 1) * NYL])
    for x in range(NXL):
        one = slice(x, x + 1)
        out_lo[3, one, :] = r_ref[x, 0:1, :]
        out_hi[3, one, :] = r_ref[x, NYL - 1 : NYL, :]
        out_lo[4, one, :] = row_sum(r_ref[x, 0:16, :], face[0, 0:16])
        out_hi[4, one, :] = row_sum(r_ref[x, NYL - 16 : NYL, :], face[-1, NYL - 16 :])
        out_lo[5, one, :] = row_sum(z4[x, 0:8, :], 0.5 * FM[0])
        out_hi[5, one, :] = row_sum(z4[x, NYL - 8 : NYL, :], 0.5 * FM[7])


def z_columns_x():
    mat = np.zeros((128, 128))
    for side in range(2):
        mat[side:32:2, side:32:2] = LX.res.T
    return mat


def z_face_vectors():
    mat = np.zeros((128, NZL))
    for x in range(NXL):
        for side, node in ((0, NZL - 1), (1, 0)):
            mat[2 * x + side, node] = 1.0
            mat[32 + 2 * x + side] = LZ.res[:, node]
    return mat


def y_rows():
    rows = np.zeros((8, NYL))
    rows[0], rows[1] = LY.face[0], LY.face[-1]
    rows[2, 0:8], rows[3, NYL - 8 :] = 0.5 * FM[0], 0.5 * FM[7]
    return rows


def face_y_kernel(
    near, far, cols, lo_ref, hi_ref, avg_ref, dy_ref, ry_ref, rx_ref, zv_ref, yr_ref,
    out_lo, out_hi, cval, halo_ref,
):
    lane = lane_iota(NYL)
    halo = halo_columns(near, far)
    halo_ref[...] = halo
    pair = split(cols[...] + halo)
    sy = left(dy_ref[...], pair)
    avg = left_exact(avg_ref[...], pair)
    sz, sx = pltpu.roll(avg, 96, 1), pltpu.roll(avg, 64, 1)
    row = lax.broadcasted_iota(jnp.int32, (NYL, 128), 0)
    keep = (lane < 32) & (row != 0) & (row != NYL - 1)
    nu = jnp.where(keep, eddy(sx, sy, sz), 0.0)
    tau = right(split(nu * sx), rx_ref[...]) + left(ry_ref[...], split(nu * sy))
    val = tau + pltpu.roll(nu * sz, 32, 1)
    cval[...] = val
    rows = left(yr_ref[...], split(jnp.concatenate([val, pltpu.roll(halo, 32, 1)], axis=1)))
    lane16 = lane_iota(NXL)
    row16 = lax.broadcasted_iota(jnp.int32, (NXL, 128), 0)
    diag = ((lane16 % 32) // 2) == row16
    short, long = diag & (lane16 < 32), diag & (lane16 < 64)
    parts_ = []
    for s, r in ((0, 0), (1, NYL - 1)):
        one = slice(r, r + 1)
        for vec, keep in (
            (sx[one], short), (sy[one], short), (sz[one], short), (val[one], long),
            (rows[s : s + 1, 0:128], long), (rows[2 + s : 3 + s, 128:256], short),
        ):
            parts_.append(jnp.where(keep, jnp.broadcast_to(vec, (NXL, 128)), 0.0))
    add = right(split(jnp.concatenate(parts_, axis=0)), zv_ref[...])
    for q in range(6):
        out_lo[q] = lo_ref[q] + add[16 * q : 16 * q + 16]
        out_hi[q] = hi_ref[q] + add[96 + 16 * q : 112 + 16 * q]


def place(pay, x, lane):
    return jnp.where(((lane % 32) // 2) == x, pay, 0.0)


def filter_kernel(r_ref, cval, z4, hcols, ty_ref, fy_ref, tp_ref, zc_ref, r2, vu, cols, cout):
    lane = lane_iota(NYL)
    acc = None
    for c in range(4):
        xs = range(4 * c, 4 * c + 4)
        val = jnp.concatenate([left(ty_ref[...], split(r_ref[x])) for x in xs], axis=0)
        out = right(split(val), tp_ref[...])
        for k, x in enumerate(xs):
            part = out[k * NYL : (k + 1) * NYL]
            r2[x] = part[:, 0:NZL]
            piece = place(part[:, NZL:], x, lane)
            acc = piece if acc is None else acc + piece
            rolled = pltpu.roll(hcols[...], (-2 * (48 + x) - 1) % 128, 1)
            field = jnp.concatenate(
                [
                    z4[x, :, 0:128] + jnp.where(lane == 0, rolled, 0.0),
                    z4[x, :, 128:256] + jnp.where(lane == 127, rolled, 0.0),
                ],
                axis=1,
            )
            vu[x] = left(fy_ref[...], split(field))
    val = left(ty_ref[...], split(cval[...]))
    cout[...] = val
    cols[...] = acc + right(split(val), zc_ref[...])


def z_columns_z():
    mat = np.zeros((128, 128))
    for x in range(NXL):
        for side, node in ((0, NZL - 1), (1, 0)):
            at = 2 * x + side
            mat[at, at], mat[32 + at, at] = 1.0, LZ.res[node, node]
            mat[at, 32 + at] = LZ.face[node, node]
            mat[32 + at, 32 + at] = LZ.face[node] @ LZ.res[:, node]
    return mat


def y_spread():
    low_t = LY.both[:, 0] + LY.halo[0] + LY.face[-1, -1] * LY.halo[1]
    low_g = (
        LY.both @ LY.res[:, 0] + DR[7, 7] * LY.halo[0] + (LY.face[-1] @ LY.res[:, -1]) * LY.halo[1]
    )
    high_t = LY.both[:, -1] + LY.halo[2] + LY.face[0, 0] * LY.halo[3]
    high_g = (
        LY.both @ LY.res[:, -1] + DR[0, 0] * LY.halo[2] + (LY.face[0] @ LY.res[:, 0]) * LY.halo[3]
    )
    return np.stack(
        [low_t, low_g, LY.halo[0], LY.halo[1], high_t, high_g, LY.halo[2], LY.halo[3]], axis=1
    )


SPREAD = y_spread()


def face_z2_kernel(
    cols_ref, after_ref, own_lo, own_hi, lo_ref, hi_ref, rx_ref, rz_ref, pay_ref, ay_ref, cols, rows_ref
):
    both = ((own_lo, lo_ref), (own_hi, hi_ref))
    flux = []
    for own, ref in both:
        s = [own[q] + ref[q] for q in range(3)]
        nu = eddy(*s)
        flux.append([nu * v for v in s])
    along_x = left(rx_ref[...], split(jnp.concatenate([flux[0][0], flux[1][0]], axis=1)))
    along_z = right(split(jnp.concatenate([flux[0][2], flux[1][2]], axis=0)), rz_ref[...])
    vals = []
    for s, (own, ref) in enumerate(both):
        tau = along_x[:, s * NZL : (s + 1) * NZL] + along_z[s * NXL : (s + 1) * NXL]
        vals += [tau, flux[s][1], ref[3], ref[4]]
    for k, val in enumerate(vals):
        rows_ref[k] = val
    pay = right(split(jnp.concatenate(vals, axis=0)), pay_ref[...])
    lane16 = lane_iota(NXL)
    row16 = lax.broadcasted_iota(jnp.int32, (NXL, 128), 0)
    keep = ((lane16 % 32) // 2) == row16
    vecs = []
    for k in range(8):
        val = pay[16 * k : 16 * k + 16]
        vec = jnp.sum(jnp.where(keep, val, 0.0), axis=0, keepdims=True)
        vecs.append(vec)
    for rows, ks in ((slice(0, 24), range(4)), (slice(NYL - 24, NYL), range(4, 8))):
        acc = cols_ref[rows, :]
        for k in ks:
            acc = acc + ay_ref[rows, k : k + 1] * vecs[k]
        cols[rows, :] = acc
    cols[24 : NYL - 24, :] = cols_ref[24 : NYL - 24, :]


def spread_kernel(
    r2, vu, rows_ref, lo_ref, hi_ref, cval, ay_ref, tz_ref, mat_ref, out, vout, pay_lo, pay_hi, zr
):
    zr[...] = right(split(rows_ref[...].reshape(8 * NXL, NZL)), tz_ref[...]).reshape(8, NXL, NZL)
    add = right(split(cval[...]), mat_ref[...])
    row8 = lax.broadcasted_iota(jnp.int32, (8, NZL), 0)
    for t in range(TILES):
        rows = slice(t * 8, t * 8 + 8)
        r, w = [], []
        for x in range(NXL):
            one = slice(x, x + 1)
            val, wal = r2[x, rows, :], vu[x, rows, :]
            for k in range(8):
                if np.any(SPREAD[rows, k]):
                    val = val + ay_ref[rows, k : k + 1] * zr[k, one, :]
            if t == 0:
                wal = wal + jnp.where(row8 == 0, lo_ref[5, one, :], 0.0)
            if t == TILES - 1:
                wal = wal + jnp.where(row8 == 7, hi_ref[5, one, :], 0.0)
            out[x, rows, :] = val
            vout[x, rows, :] = wal
            r.append(val)
            w.append(wal)
        a = [s + v for s, v in zip(average_x(r), w)]
        low = sum(float(FM[0, j]) * a[j] for j in range(8))
        high = sum(float(FM[7, j]) * a[8 + j] for j in range(8))
        for q, (ref, val) in enumerate(((pay_lo, r[0]), (pay_lo, low), (pay_hi, r[15]), (pay_hi, high))):
            ref[q % 2, rows, :] = val + add[rows, q * NZL : (q + 1) * NZL]


def z_vectors():
    vecs = [[LZ.halo[0], LZ.halo[2]], [LZ.halo[1], LZ.halo[3]]]
    vecs.append([LZ.both[:, -1], LZ.both[:, 0]])
    vecs.append([LZ.both @ LZ.res[:, -1], LZ.both @ LZ.res[:, 0]])
    return vecs


def z_spread():
    add = np.zeros((128, NZL))
    for q, pair in enumerate(z_vectors()):
        for side in range(2):
            add[32 * q + side] = pair[side]
    return add


def z_to_x():
    out = np.zeros((128, 4 * NZL))
    low, high = LX.face[0], LX.face[-1]
    for x in range(NXL):
        for q, pair in enumerate(z_vectors()[2:]):
            for side in range(2):
                lane, vec = 2 * (16 * q + x) + side, pair[side]
                if x == 0:
                    out[lane, 0:NZL] = vec
                if x == NXL - 1:
                    out[lane, 2 * NZL : 3 * NZL] = vec
                out[lane, NZL : 2 * NZL] = low[x] * vec
                out[lane, 3 * NZL :] = high[x] * vec
    return out


def z_short():
    out = np.zeros((128, 128))
    low, high = LX.face[0], LX.face[-1]
    for x in range(NXL):
        for q in range(2):
            for side in range(2):
                lane, c = 2 * (16 * q + x) + side, 2 * q + side
                if x == 0:
                    out[lane, c] = 1.0
                if x == NXL - 1:
                    out[lane, 8 + c] = 1.0
                out[lane, 4 + c], out[lane, 12 + c] = low[x], high[x]
    return out


def z_long():
    out = np.zeros((16, 4 * NZL))
    for q, pair in enumerate(z_vectors()[:2]):
        for side in range(2):
            for k in range(4):
                out[4 * k + 2 * q + side, k * NZL : (k + 1) * NZL] = pair[side]
    high, low = halves(out)
    rest = np.zeros((80, 4 * NZL)).astype(jnp.bfloat16)
    return jnp.asarray(np.concatenate([high, high, low, rest], axis=0))


def forward_kernel(near, far, cval, mat_ref, flo, fhi, hs):
    low, high = received(near, far)
    lane = lane_iota(NYL)
    halo = jnp.where((lane % 2) == 0, low, high)
    hs[...] = jnp.where(lane < 64, halo, pltpu.roll(cval[...], 64, 1))
    short = right(split(halo), mat_ref[...])
    lane8 = lane_iota(8)
    for ref, base in ((flo, 0), (fhi, 8)):
        acc = None
        for t in range(TILES):
            piece = pltpu.roll(short[8 * t : 8 * t + 8], (8 * t - base) % 128, 1)
            piece = jnp.where((lane8 // 8) == t, piece, 0.0)
            acc = piece if acc is None else acc + piece
        ref[...] = acc


def forwarded(glo, ghi, mat):
    lane8 = lane_iota(8)
    tiles = []
    for t in range(TILES):
        low = pltpu.roll(glo, (-8 * t) % 128, 1)
        high = pltpu.roll(ghi, (8 - 8 * t) % 128, 1)
        tiles.append(jnp.where(lane8 < 8, low, jnp.where(lane8 < 16, high, 0.0)))
    val = jnp.concatenate(tiles, axis=0)
    top = val.astype(BF).astype(F32)
    val = top + pltpu.roll(val - top, 16, 1) + pltpu.roll(top, 32, 1)
    return mm(val.astype(BF), mat)


def local_x_kernel(r2, vu, hs, add_ref, out):
    for t in range(NYL // 16):
        rows = slice(t * 16, t * 16 + 16)
        col = hs[rows, :]
        rolled = [pltpu.roll(col, (-2 * x) % 128, 1) if x else col for x in range(NXL)]
        add = right(split(jnp.concatenate(rolled, axis=0)), add_ref[...])
        r = [r2[x, rows, :] + add[16 * x : 16 * x + 16] for x in range(NXL)]
        a = [s + vu[k, rows, :] for k, s in enumerate(average_x(r))]
        f = average_x(even_odd(FM, a[:8], 1) + even_odd(FM, a[8:], 1))
        f[0] = f[0] + float(0.25 * FM[7, 7]) * r[0]
        f[15] = f[15] + float(0.25 * FM[0, 0]) * r[15]
        for k in range(NXL):
            out[k, rows, :] = f[k]


def final_kernel(val_ref, lo_ref, hi_ref, glo_ref, ghi_ref, mat_ref, out_hbm, buf, sems):
    copies = []
    add = forwarded(glo_ref[...], ghi_ref[...], mat_ref[...])
    for c in range(6):
        for t in range(2):
            rows = slice(c * 16 + t * 8, c * 16 + t * 8 + 8)
            halo = [lo_ref[0, rows, :], lo_ref[1, rows, :], hi_ref[0, rows, :], hi_ref[1, rows, :]]
            halo = [v + add[rows, j * NZL : (j + 1) * NZL] for j, v in enumerate(halo)]
            for k in range(NXL):
                val = val_ref[k, rows, :]
                for j in range(4):
                    if LX.halo[j][k] != 0.0:
                        val = val + float(LX.halo[j][k]) * halo[j]
                buf[k, rows, :] = val
        rows = slice(c * 16, c * 16 + 16)
        copies.append(pltpu.make_async_copy(buf.at[:, rows, :], out_hbm.at[:, rows, :], sems.at[c]))
        copies[-1].start()
    for copy in copies:
        copy.wait()


def shift(val, axis, step):
    count = lax.axis_size(axis)
    return lax.ppermute(val, axis, [(i, (i + step) % count) for i in range(count)])


def exchange(lo, hi, axis):
    return shift(hi, axis, 1), shift(lo, axis, -1)


def swap(val, axis, start):
    count = lax.axis_size(axis)
    pairs = [(k % count, (k + 1) % count) for k in range(start, count + start, 2)]
    return lax.ppermute(val, axis, pairs + [(b, a) for a, b in pairs])


def on_device(u, velocity):
    full = (NXL, NYL, NZL)
    face_x = (2, NYL, NZL)
    face_y = (6, NXL, NZL)
    colshape = (NYL, 128)

    sz, dz = exact_right(LZ.avg.T), on_right(LZ.grad.T)
    sy, dy, fy = exact_left(LY.avg), on_left(LY.grad), on_left(LY.filt)
    ry, rz, rx = on_left(LY.res), on_right(LZ.res.T), on_left(LX.res)
    pay = np.zeros((NZL, 128))
    pay[NZL - 1, 0:32:2] = pay[0, 1:32:2] = 1.0
    pay[:, 32:64:2], pay[:, 33:64:2] = LZ.face[-1][:, None], LZ.face[0][:, None]
    pay_mat = pay
    pay = on_right(pay)
    ay = jnp.asarray(SPREAD.astype(np.float32))
    ty, tz = on_left(LY.both), on_right(LZ.both.T)

    hi = call(
        face_hi_kernel, face_x, pltpu.with_memory_space_constraint(u, pltpu.HBM), hbm=(0,),
        scratch=[pltpu.VMEM((8, NYL, NZL), F32), pltpu.SemaphoreType.DMA((8,))], name="face_hi",
    )
    xlo = shift(hi, "gx", 1)
    lo = call(face_lo_kernel, face_x, u, name="face_lo")
    xhi = shift(lo, "gx", -1)
    z1, z2, z3, z4, cols = call(
        local_z_kernel, [full] * 4 + [colshape], u, sz, on_right(np.concatenate([LZ.grad.T, LZ.filt.T], axis=1)),
        flops=3 * 10**9, nbytes=8 * 10**6, name="local_z",
    )
    inner = (NXL - 2, NYL, NZL)
    flux = call(
        flux_kernel, [inner] + [(inner, BF)] * 4 + [(3, NXL, NZL)] * 2,
        z1, z2, z3, u, velocity, sy, dy, flops=10**9, nbytes=12 * 10**6, name="flux",
    )
    dlt, cols = call(
        face_z_kernel, [(2, 3, NYL, NZL), colshape], xlo, xhi, cols, sz, dz, name="face_z"
    )
    near, far = swap(cols, "gz", 0), swap(cols, "gz", 1)
    r, lo, hi = call(
        residue_kernel, [full, face_y, face_y],
        *flux, z1, z2, z3, z4, dlt, u, velocity, sy, dy, ry, rz,
        scratch=[pltpu.VMEM((2, NYL, NZL), F32)], flops=3 * 10**9, nbytes=12 * 10**6, name="residue",
    )
    lo, hi, cval, hcols = call(
        face_y_kernel, [face_y, face_y, colshape, colshape], near, far, cols, lo, hi, sy, dy, ry,
        on_right(z_columns_x()), on_right(z_face_vectors()), on_left(y_rows()), name="face_y",
    )
    ylo, yhi = exchange(lo, hi, "gy")
    both = np.concatenate([LZ.both.T, pay_mat], axis=1)
    r2, vu, cols, cval = call(
        filter_kernel, [full, full, colshape, colshape],
        r, cval, z4, hcols, ty, fy, on_right(both), on_right(z_columns_z()),
        flops=3 * 10**9, nbytes=9 * 10**6, name="filter",
    )
    cols, rows = call(
        face_z2_kernel, [colshape, (8, NXL, NZL)], cols, r2, lo, hi, ylo, yhi, rx, rz, pay, ay,
        name="face_z2",
    )
    near, far = swap(cols, "gz", 0), swap(cols, "gz", 1)
    r2, vu, lo, hi = call(
        spread_kernel, [full, full, face_x, face_x], r2, vu, rows, ylo, yhi, cval, ay, tz, on_right(z_to_x()),
        scratch=[pltpu.VMEM((8, NXL, NZL), F32)], flops=10**9, nbytes=9 * 10**6, name="spread",
    )
    xlo, xhi = exchange(lo, hi, "gx")
    flo, fhi, hs = call(
        forward_kernel, [(8, 128), (8, 128), colshape], near, far, cval, on_right(z_short()), name="forward"
    )
    glo, ghi = exchange(flo, fhi, "gx")
    val = call(
        local_x_kernel, full, r2, vu, hs, on_right(z_spread()),
        flops=10**11, nbytes=10**8, name="local_x",
    )
    return call(
        final_kernel, full, val, xlo, xhi, glo, ghi, z_long(), hbm_out=True,
        scratch=[pltpu.VMEM(full, F32), pltpu.SemaphoreType.DMA((6,))], name="final",
    )


def solution(mesh):
    return jax.shard_map(
        on_device,
        mesh=mesh,
        in_specs=(P("gx", "gy", "gz"), P(None, "gx", "gy", "gz")),
        out_specs=P("gx", "gy", "gz"),
        check_vma=False,
    )
```
